32 devices in a mesh: dp: 8 (over y, x, core), tensor: 4 (over z).
Axes of the slice: x: 2, y: 2, z: 4, core: 2. Of those that a mesh axis runs over, the one named last changes fastest.
Arguments:
- latent_in: bfloat16 [16, 256, 768], P('dp', 'tensor'), may hold values from -6 to 6
- condition: bfloat16 [16, 768], P('dp'), may hold values from -6 to 6
- w_ada: bfloat16 [768, 4608], P('dp', 'tensor'), may hold values from -0.21875 to 0.21875
- w_qkv: bfloat16 [3, 768, 768], P(None, 'dp', 'tensor'), may hold values from -0.21875 to 0.21875
- w_proj: bfloat16 [768, 768], P('tensor', 'dp'), may hold values from -1.25 to 1.25
- w_up: bfloat16 [768, 3072], P('dp', 'tensor'), may hold values from -0.21875 to 0.21875
- w_down: bfloat16 [3072, 768], P('tensor', 'dp'), may hold values from -0.109375 to 0.109375
- out_grad: bfloat16 [16, 256, 768], P('dp', 'tensor'), may hold values from -6 to 6
Outputs:
- latent_out: bfloat16 [16, 256, 768], P('dp', 'tensor')
- grad_latent: float32 [16, 256, 768], P('dp', 'tensor')
- grad_condition: float32 [16, 768], P('dp')
- grad_ada: float32 [768, 4608], P('dp', 'tensor')
- grad_qkv: float32 [3, 768, 768], P(None, 'dp', 'tensor')
- grad_proj: float32 [768, 768], P('tensor', 'dp')
- grad_up: float32 [768, 3072], P('dp', 'tensor')
- grad_down: float32 [3072, 768], P('tensor', 'dp')
The draws below stay inside these ranges and needn't reach their ends.
All inputs are finite; a program needn't handle non-finite values.
Results may differ from the reference program's by a relative error of at most 0.015.
The reference program's roundings to bfloat16 on the way count: a program that leaves them out, or rounds other values in their place, can miss the bound.
Values may be sent and summed in bfloat16 or wider, within the bound.
A program may use at most 128 MiB of HBM per device.

```python
import math
import jax
import jax.numpy as jnp
from jax import lax

D = 768
HEADS = 12
HEAD_DIM = 64
FF = 3072
SEQ = 256
LATENTS = 16


def with_spikes(drawn, rng, source, target, parts, factor):
    def block_of(position):
        return (jnp.arange(drawn.shape[position]) // (drawn.shape[position] // parts)).reshape((-1,) + (1,) * (drawn.ndim - 1 - position))

    first = jax.random.permutation(rng, parts)[block_of(target)]
    far = (block_of(target) + parts // 2) % parts
    return jnp.where((block_of(source) == first) | (block_of(source) == far), factor * drawn, drawn)


def levels(rng, extent, pieces, low, top_value):
    level = 1.0
    for axis_at, parts in pieces:
        steps = jax.random.uniform(jax.random.fold_in(jax.random.fold_in(rng, 6), axis_at), (parts,), jnp.float32, low / len(pieces), top_value / len(pieces))
        level = level * jnp.repeat(jnp.exp(steps), extent[axis_at] // parts).reshape((-1,) + (1,) * (len(extent) - 1 - axis_at))
    return level


def noise(stream_key, extent, deviation, limit, split=(), dtype=jnp.bfloat16):
    array = jax.random.normal(stream_key, extent, jnp.float32) * deviation
    if len(split) > 0:
        array = levels(stream_key, extent, split, -0.22, 0.18) * array
    return jnp.clip(array, min=-limit, max=limit).astype(dtype)


def gaussian_with(key, extent, scale, reach, split, heavy, held_as=jnp.bfloat16):
    array = scale * jax.random.normal(key, extent, jnp.float32)
    if split:
        array = array * levels(key, extent, split, -0.22, 0.18)
    return jnp.clip(with_spikes(array, jax.random.fold_in(key, 3), *heavy), -reach, reach).astype(held_as)


def setup_inputs(seed: int = 0) -> dict:
    key_list = jax.random.split(jax.random.key(seed), 9)
    latent_in = noise(key_list[0], (LATENTS, SEQ, D), 1.0, 6.0, ((0, 8), (1, 4)))
    condition = noise(key_list[1], (LATENTS, D), 1.0, 6.0, ((0, 8),))
    w_ada = noise(key_list[2], (D, 6 * D), D ** -0.5, 0.21875, ((0, 8), (1, 4)))
    w_qkv = noise(key_list[3], (3, D, D), D ** -0.5, 0.21875, ((1, 8), (2, 4)))
    w_proj = noise(key_list[4], (D, D), (D // 32) ** -0.5, 1.25, ((0, 4), (1, 8)))
    w_up = noise(key_list[5], (D, FF), D ** -0.5, 0.21875, ((0, 8), (1, 4)))
    w_down = noise(key_list[6], (FF, D), FF ** -0.5, 0.109375, ((0, 4), (1, 8)))
    out_grad = gaussian_with(key_list[7], (LATENTS, SEQ, D), 1.0, 6.0, ((0, 8), (1, 4)), (0, 2, 8, 2.0))
    return {"latent_in": latent_in, "condition": condition, "w_ada": w_ada, "w_qkv": w_qkv, "w_proj": w_proj, "w_up": w_up, "w_down": w_down, "out_grad": out_grad}


@jax.custom_vjp
def low(v):
    return lax.optimization_barrier(v.astype(jnp.bfloat16)).astype(jnp.float32)

@jax.custom_vjp
def low_back(v):
    return v

def low_keep(v):
    return (low(v), None)

def low_pass(kept, grad):
    return (grad,)

def back_keep(v):
    return (v, None)

def back_low(kept, grad):
    return (low(grad),)
low.defvjp(low_keep, low_pass)
low_back.defvjp(back_keep, back_low)
epsilon = 1e-06

def silu_value(values):
    return values / (1.0 + jnp.exp(-values))

def gelu_tanh(values):
    return 0.5 * values * (1.0 + jnp.tanh(math.sqrt(2.0 / math.pi) * (values + 0.044715 * values * values * values)))

def normalize(values):
    centered = values - lax.optimization_barrier(jnp.mean(values, axis=-1, keepdims=True))
    variance = lax.optimization_barrier(jnp.mean(centered * centered, axis=-1, keepdims=True))
    return centered * lax.rsqrt(variance + epsilon)

def mix(form, left, right):
    return jnp.einsum(form, left, right, precision=lax.Precision.HIGHEST)

def block_forward(latent, condition, w_ada, w_qkv, w_proj, w_up, w_down):
    group = latent.shape[0]
    cond_act = low(silu_value(condition))
    modulation = low_back(mix('gd,de->ge', cond_act, w_ada)).reshape(group, 6, 1, D)
    shift_a = modulation[:, 0]
    scale_a = modulation[:, 1]
    gate_a = modulation[:, 2]
    shift_f = modulation[:, 3]
    scale_f = modulation[:, 4]
    gate_f = modulation[:, 5]
    normed_a = normalize(latent)
    attn_in = low(normed_a * (1.0 + scale_a) + shift_a)
    projected = low(low_back(mix('gsd,jde->jgse', attn_in, w_qkv)))
    projected = projected.reshape(3, group, SEQ, HEADS, HEAD_DIM)
    scores = low_back(mix('gqhe,gkhe->ghqk', projected[0], projected[1]) * HEAD_DIM ** (-0.5))
    shifted = jnp.exp(scores - lax.optimization_barrier(jnp.max(scores, axis=-1, keepdims=True)))
    soft_probs = shifted / lax.optimization_barrier(jnp.sum(shifted, axis=-1, keepdims=True))
    mixed = mix('ghqk,gkhe->gqhe', low(soft_probs), projected[2]).reshape(group, SEQ, D)
    mixed = low(low_back(mixed))
    attn_out = low_back(mix('gsd,de->gse', mixed, w_proj))
    resid = latent + gate_a * attn_out
    normed_f = normalize(resid)
    ffn_in = low(normed_f * (1.0 + scale_f) + shift_f)
    hidden_preactivation = low_back(mix('gsd,df->gsf', ffn_in, w_up))
    hidden_units = low(gelu_tanh(hidden_preactivation))
    ffn_out = low_back(mix('gsf,fd->gsd', hidden_units, w_down))
    return resid + gate_f * ffn_out

def reference(latent_in, condition, w_ada, w_qkv, w_proj, w_up, w_down, out_grad):
    weights = (w_ada.astype(jnp.float32), w_qkv.astype(jnp.float32), w_proj.astype(jnp.float32), w_up.astype(jnp.float32), w_down.astype(jnp.float32))
    group = math.gcd(LATENTS, 16)
    count = LATENTS // group
    latents = latent_in.astype(jnp.float32).reshape(count, group, SEQ, D)
    conditions = condition.astype(jnp.float32).reshape(count, group, D)
    cotangents = out_grad.astype(jnp.float32).reshape(count, group, SEQ, D)

    def step(carry, item):
        latent, cond_rows, cotangent = item
        result, pull = jax.vjp(block_forward, latent, cond_rows, *weights)
        grads = pull(cotangent)
        carry = tuple((total + part for total, part in zip(carry, grads[2:])))
        return (carry, (result.astype(jnp.bfloat16), grads[0], grads[1]))
    initial = tuple((jnp.zeros_like(weight) for weight in weights))
    totals, outputs = lax.scan(step, initial, (latents, conditions, cotangents))
    latent_out = outputs[0].reshape(LATENTS, SEQ, D)
    grad_latent = outputs[1].reshape(LATENTS, SEQ, D)
    grad_condition = outputs[2].reshape(LATENTS, D)
    return (latent_out, grad_latent, grad_condition, totals[0], totals[1], totals[2], totals[3], totals[4])
```

```python
import functools
import math
import types

import jax
import jax.numpy as jnp
from jax import lax
from jax.experimental import pallas as pl
from jax.experimental.pallas import tpu as pltpu
from jax.sharding import PartitionSpec as P

MESH = pl.DeviceIdType.MESH
VMEM = pl.BlockSpec(memory_space=pltpu.VMEM)

HEAD_DIM = 64
EPS = 1e-06
f32 = jnp.float32
bf16 = jnp.bfloat16


def silu_value(values):
    return values / (1.0 + jnp.exp(-values))


def gelu_tanh(values):
    return (
        0.5
        * values
        * (
            1.0
            + jnp.tanh(math.sqrt(2.0 / math.pi) * (values + 0.044715 * values * values * values))
        )
    )


def norm_parts(values):
    centered = values - jnp.mean(values, axis=-1, keepdims=True)
    variance = jnp.mean(centered * centered, axis=-1, keepdims=True)
    inverse = lax.rsqrt(variance + EPS)
    return centered * inverse, inverse


def norm_back(normed, inverse, grad):
    return inverse * (
        grad
        - jnp.mean(grad, axis=-1, keepdims=True)
        - normed * jnp.mean(grad * normed, axis=-1, keepdims=True)
    )


def dot(form, left, right):
    return jnp.einsum(form, left, right, preferred_element_type=f32)


def gather_tensor(block, axis):
    return lax.all_gather(block, "tensor", axis=axis, tiled=True)


def greet(axes):
    barrier = pltpu.get_barrier_semaphore()
    total = 0
    for axis in axes:
        size = lax.axis_size(axis)
        me = lax.axis_index(axis)
        for step in range(1, size):
            pl.semaphore_signal(
                barrier, inc=1, device_id={axis: lax.rem(me + step, size)}, device_id_type=MESH
            )
        total += size - 1
    pl.semaphore_wait(barrier, total)


def start_exchange(axis, source, target, sems):
    size = lax.axis_size(axis)
    me = lax.axis_index(axis)
    copies = []
    for step in range(1, size):
        peer = lax.rem(me + step, size)
        copy = pltpu.make_async_remote_copy(
            src_ref=source(peer),
            dst_ref=target,
            send_sem=sems.at[0, step - 1],
            recv_sem=sems.at[1, step - 1],
            device_id={axis: peer},
            device_id_type=MESH,
        )
        copy.start()
        copies.append(copy)
    return copies


def wait_all(copies):
    for copy in copies:
        copy.wait()


def exchange(axis, source, target, sems):
    wait_all(start_exchange(axis, source, target, sems))


def sem_pair(axis):
    return pltpu.SemaphoreType.DMA((2, lax.axis_size(axis) - 1))


def call(kernel, outs, scratch, number, *args):
    return pl.pallas_call(
        kernel,
        out_shape=outs,
        in_specs=[VMEM] * len(args),
        out_specs=jax.tree.map(lambda _: VMEM, outs),
        scratch_shapes=scratch,
        compiler_params=pltpu.CompilerParams(
            collective_id=number, has_side_effects=True, vmem_limit_bytes=48 * 2**20
        ),
    )(*args)


def modulation_kernel(
    cond_ref, w_ref, x_ref, shard_ref, mod_ref, act_ref, x_all, w_all,
    cond_buf, part, recv, own, s0, s1, s2, s3, s4, s5
):
    count = lax.axis_size("dp")
    me, mine = lax.axis_index("dp"), lax.axis_index("tensor")
    greet(("dp", "tensor"))
    copies = start_exchange("dp", lambda peer: cond_ref.at[peer], cond_buf.at[me], s0)
    x_own = token_block(x_all, mine, x_ref.shape[1])
    x_copies = start_exchange("tensor", lambda peer: x_ref, x_own, s3)
    cond_buf[me] = cond_ref[me]
    x_own[...] = x_ref[...]
    w_all[me] = shard_ref[...]
    wait_all(copies)

    @pl.loop(0, count)
    def _(at):
        act = silu_value(cond_buf[at]).astype(bf16)
        act_ref[at] = act.astype(f32)
        part[at] = jnp.dot(act, w_ref[...], preferred_element_type=f32)

    copies = start_exchange("dp", lambda peer: part.at[peer], recv.at[me], s1)
    recv[me] = part[me]
    pairs = count // 2
    chip, side = me // 2, lax.rem(me, 2)
    sibling = 2 * chip + 1 - side

    def send(source, at, to, sems, number):
        copy = pltpu.make_async_remote_copy(
            src_ref=source,
            dst_ref=w_all.at[at],
            send_sem=sems.at[0, number],
            recv_sem=sems.at[1, number],
            device_id={"dp": to},
            device_id_type=MESH,
        )
        copy.start()
        return copy

    far = [
        send(shard_ref, me, 2 * lax.rem(chip + step, pairs) + side, s4, step)
        for step in range(1, pairs)
    ]
    near = [send(shard_ref, me, sibling, s5, 0)]
    wait_all(copies)
    own[...] = jnp.sum(recv[...], axis=0)
    copies = start_exchange("tensor", lambda peer: own, mod_ref.at[mine], s2)
    mod_ref[mine] = own[...]
    for step in range(1, pairs):
        far[step - 1].wait()
        came = 2 * lax.rem(chip + pairs - step, pairs) + side
        near.append(send(w_all.at[came], came, sibling, s5, step))
    wait_all(near)
    wait_all(copies)
    wait_all(x_copies)


def modulation_of(condition, w_ada, block, shard):
    count, group = lax.axis_size("dp"), lax.axis_size("tensor")
    rows, width = condition.shape
    shard_rows, columns = w_ada.shape
    blocks = condition.astype(f32).reshape(rows, count, shard_rows).transpose(1, 0, 2)
    mod, act, x_all, w_all = call(
        modulation_kernel,
        (
            jax.ShapeDtypeStruct((group, rows, columns), f32),
            jax.ShapeDtypeStruct((count, rows, shard_rows), f32),
            jax.ShapeDtypeStruct((rows, group * block.shape[1], width), bf16),
            jax.ShapeDtypeStruct((count,) + shard.shape, bf16),
        ),
        [
            pltpu.VMEM((count, rows, shard_rows), f32),
            pltpu.VMEM((count, rows, columns), f32),
            pltpu.VMEM((count, rows, columns), f32),
            pltpu.VMEM((rows, columns), f32),
            sem_pair("dp"),
            sem_pair("dp"),
            sem_pair("tensor"),
            sem_pair("tensor"),
            pltpu.SemaphoreType.DMA((2, count // 2)),
            pltpu.SemaphoreType.DMA((2, count // 2)),
        ],
        1,
        blocks,
        w_ada,
        block,
        shard,
    )
    mod = mod.transpose(1, 0, 2).reshape(rows, group * columns)
    act = act.reshape(count * rows, shard_rows).astype(bf16)
    return mod, act, x_all, w_all.reshape(count * shard.shape[0], shard.shape[1])


def token_block(ref, at, size):
    return ref.at[:, pl.ds(pl.multiple_of(at * size, size), size)]


def finish_reduce(part_ref, out_ref, recv, first, sems):
    group = lax.axis_size("tensor")
    mine = lax.axis_index("tensor")
    size = part_ref.shape[1] // group
    wait_all(first)
    total = token_block(part_ref, mine, size)[...].astype(f32)
    for step in range(1, group):
        total += recv[lax.rem(mine + step, group)].astype(f32)
    own = token_block(out_ref, mine, size)
    own[...] = total.astype(bf16)
    return start_exchange("tensor", lambda peer: own, own, sems)


def start_reduce(part_ref, recv, sems):
    group = lax.axis_size("tensor")
    size = part_ref.shape[1] // group
    return start_exchange(
        "tensor",
        lambda peer: token_block(part_ref, peer, size),
        recv.at[lax.axis_index("tensor")],
        sems,
    )


def reduce_kernel(part_ref, out_ref, recv, s0, s1):
    greet(("tensor",))
    first = start_reduce(part_ref, recv, s0)
    wait_all(finish_reduce(part_ref, out_ref, recv, first, s1))


def reduce_gather_kernel(part_ref, shard_ref, out_ref, w_all, recv, s0, s1, s2, s3):
    count = lax.axis_size("dp")
    me = lax.axis_index("dp")
    pairs = count // 2
    chip, side = me // 2, lax.rem(me, 2)
    sibling = 2 * chip + 1 - side
    greet(("dp", "tensor"))

    def send(source, at, to, sems, number):
        copy = pltpu.make_async_remote_copy(
            src_ref=source,
            dst_ref=w_all.at[at],
            send_sem=sems.at[0, number],
            recv_sem=sems.at[1, number],
            device_id={"dp": to},
            device_id_type=MESH,
        )
        copy.start()
        return copy

    first = start_reduce(part_ref, recv, s0)
    far = [
        send(shard_ref, me, 2 * lax.rem(chip + step, pairs) + side, s2, step)
        for step in range(1, pairs)
    ]
    near = [send(shard_ref, me, sibling, s3, 0)]
    w_all[me] = shard_ref[...]
    last = finish_reduce(part_ref, out_ref, recv, first, s1)
    for step in range(1, pairs):
        far[step - 1].wait()
        came = 2 * lax.rem(chip + pairs - step, pairs) + side
        near.append(send(w_all.at[came], came, sibling, s3, step))
    wait_all(near)
    wait_all(last)


def reduce_and_gather(part, shard, number):
    group, count = lax.axis_size("tensor"), lax.axis_size("dp")
    rows, seq, width = part.shape
    total, weights = call(
        reduce_gather_kernel,
        (
            jax.ShapeDtypeStruct(part.shape, bf16),
            jax.ShapeDtypeStruct((count,) + shard.shape, bf16),
        ),
        [
            pltpu.VMEM((group, rows, seq // group, width), bf16),
            sem_pair("tensor"),
            sem_pair("tensor"),
            pltpu.SemaphoreType.DMA((2, count // 2)),
            pltpu.SemaphoreType.DMA((2, count // 2)),
        ],
        number,
        part.astype(bf16),
        shard,
    )
    return total.astype(f32), weights.reshape(count * shard.shape[0], shard.shape[1])


def reduce_tensor(part, number):
    group = lax.axis_size("tensor")
    rows, seq, width = part.shape
    return call(
        reduce_kernel,
        jax.ShapeDtypeStruct(part.shape, bf16),
        [
            pltpu.VMEM((group, rows, seq // group, width), bf16),
            sem_pair("tensor"),
            sem_pair("tensor"),
        ],
        number,
        part.astype(bf16),
    ).astype(f32)


def final_kernel(
    attn_ref, ffn_ref, grad_ref, part_ref, w_ref, attn_out, ffn_out, grad_out, all_ref, act_ref,
    attn_recv, ffn_recv, pair_recv, stage, grad_recv, recv_mod, own, part, terms, gathered,
    s0, s1, s2, s3, m0, m1, m2, m3
):
    group = lax.axis_size("tensor")
    count = lax.axis_size("dp")
    pairs = count // 2
    me, mine = lax.axis_index("dp"), lax.axis_index("tensor")
    chip, side = me // 2, lax.rem(me, 2)
    size = attn_ref.shape[1] // group
    greet(("dp", "tensor"))
    copies = start_exchange("tensor", lambda peer: part_ref.at[peer], recv_mod.at[mine], m0)
    recv_mod[mine] = part_ref[mine]
    pair_copy = pltpu.make_async_remote_copy(
        src_ref=grad_ref.at[:, 1 - side],
        dst_ref=pair_recv,
        send_sem=s0.at[0],
        recv_sem=s0.at[1],
        device_id={"dp": 2 * chip + 1 - side},
        device_id_type=MESH,
    )
    pair_copy.start()
    attn_copies = start_exchange(
        "tensor", lambda peer: token_block(attn_ref, peer, size), attn_recv.at[mine], s1
    )
    ffn_copies = start_exchange(
        "tensor", lambda peer: token_block(ffn_ref, peer, size), ffn_recv.at[mine], s2
    )
    wait_all(copies)
    own[...] = jnp.sum(recv_mod[...], axis=0).astype(bf16).astype(f32)
    copies = start_exchange("dp", lambda peer: own, all_ref.at[me], m1)
    all_ref[me] = own[...]
    wait_all(copies)

    @pl.loop(0, count)
    def _(at):
        part[at] = lax.dot_general(
            all_ref[at].astype(bf16),
            w_ref[...],
            (((1,), (1,)), ((), ())),
            preferred_element_type=f32,
        )

    copies = start_exchange("dp", lambda peer: part.at[peer], terms.at[me], m2)
    terms[me] = part[me]
    pair_copy.wait()
    grad_copies = []
    for step in range(pairs):
        to = lax.rem(chip + step, pairs) if step else chip
        total = grad_ref[to, side].astype(f32) + pair_recv[to].astype(f32)
        if step == 0:
            grad_out[...] = total
            continue
        stage[to] = total.astype(bf16)
        copy = pltpu.make_async_remote_copy(
            src_ref=stage.at[to],
            dst_ref=grad_recv.at[chip],
            send_sem=s3.at[0, step - 1],
            recv_sem=s3.at[1, step - 1],
            device_id={"dp": 2 * to + side},
            device_id_type=MESH,
        )
        copy.start()
        grad_copies.append(copy)
    wait_all(copies)
    last_copies = start_exchange("tensor", lambda peer: terms, gathered.at[mine], m3)
    gathered[mine] = terms[...]
    wait_all(grad_copies)
    for step in range(1, pairs):
        grad_out[...] += grad_recv[lax.rem(chip + step, pairs)].astype(f32)
    for copies, source, recv, out in (
        (attn_copies, attn_ref, attn_recv, attn_out),
        (ffn_copies, ffn_ref, ffn_recv, ffn_out),
    ):
        wait_all(copies)
        total = token_block(source, mine, size)[...].astype(f32)
        for step in range(1, group):
            total += recv[lax.rem(mine + step, group)].astype(f32)
        out[...] = total
    wait_all(last_copies)
    act_ref[...] = jnp.sum(gathered[...], axis=0)


def final_sums(attn_part, ffn_part, grads, parts, w_ada):
    group, count = lax.axis_size("tensor"), lax.axis_size("dp")
    rows, seq, width = attn_part.shape
    depth, columns = grads.shape
    shard_rows = depth // count
    tokens = (rows, seq // group, width)
    mod_columns = w_ada.shape[1]
    attn_own, ffn_own, grads, everyone, act = call(
        final_kernel,
        (
            jax.ShapeDtypeStruct(tokens, f32),
            jax.ShapeDtypeStruct(tokens, f32),
            jax.ShapeDtypeStruct((shard_rows, columns), f32),
            jax.ShapeDtypeStruct((count, rows, mod_columns), f32),
            jax.ShapeDtypeStruct((count, rows, shard_rows), f32),
        ),
        [
            pltpu.VMEM((group,) + tokens, bf16),
            pltpu.VMEM((group,) + tokens, bf16),
            pltpu.VMEM((count // 2, shard_rows, columns), bf16),
            pltpu.VMEM((count // 2, shard_rows, columns), bf16),
            pltpu.VMEM((count // 2, shard_rows, columns), bf16),
            pltpu.VMEM((group, rows, mod_columns), f32),
            pltpu.VMEM((rows, mod_columns), f32),
            pltpu.VMEM((count, rows, shard_rows), f32),
            pltpu.VMEM((count, rows, shard_rows), f32),
            pltpu.VMEM((group, count, rows, shard_rows), f32),
            pltpu.SemaphoreType.DMA((2,)),
            sem_pair("tensor"),
            sem_pair("tensor"),
            pltpu.SemaphoreType.DMA((2, count // 2 - 1)),
            sem_pair("tensor"),
            sem_pair("dp"),
            sem_pair("dp"),
            sem_pair("tensor"),
        ],
        5,
        attn_part.astype(bf16),
        ffn_part.astype(bf16),
        grads.astype(bf16).reshape(count // 2, 2, shard_rows, columns),
        parts.reshape(rows, group, mod_columns).transpose(1, 0, 2),
        w_ada,
    )
    everyone = everyone.reshape(count * rows, mod_columns).astype(bf16)
    d_act = act.transpose(1, 0, 2).reshape(rows, count * shard_rows)
    return attn_own, ffn_own, grads, everyone, d_act


def shards(latent_in, condition, w_ada, w_qkv, w_proj, w_up, w_down, out_grad):
    rows, own_tokens, width = latent_in.shape
    scale = HEAD_DIM ** (-0.5)
    tensor_at = lax.axis_index("tensor")
    local = w_proj.shape[0]
    heads = local // HEAD_DIM
    units = w_down.shape[0]

    attn_shard = jnp.concatenate(
        [w_qkv[0], w_qkv[1], w_qkv[2], w_proj.T], axis=1
    )
    ffn_shard = jnp.concatenate([w_up, w_down.T], axis=1)
    modulation, cond_mine, tokens, attn_weights = modulation_of(
        condition, w_ada, latent_in, attn_shard
    )
    modulation = modulation.reshape(rows, 6, 1, width)
    shift_a, scale_a, gate_a, shift_f, scale_f, gate_f = (modulation[:, i] for i in range(6))

    w_in = attn_weights[:, : 3 * local]
    proj_t = attn_weights[:, 3 * local :]
    cotangent = gather_tensor(out_grad, 1).astype(f32)
    tokens = tokens.astype(f32)
    seq = tokens.shape[1]

    normed_a, inverse_a = norm_parts(tokens)
    attn_in = (normed_a * (1.0 + scale_a) + shift_a).astype(bf16)
    projected = dot("lsd,de->lse", attn_in, w_in).astype(bf16)
    projected = projected.reshape(rows, seq, 3, heads, HEAD_DIM)
    queries, keys, values = projected[:, :, 0], projected[:, :, 1], projected[:, :, 2]
    scores = dot("lqhe,lkhe->lhqk", queries, keys) * scale
    shifted = jnp.exp(scores - jnp.max(scores, axis=-1, keepdims=True))
    probs = shifted / jnp.sum(shifted, axis=-1, keepdims=True)
    probs_low = probs.astype(bf16)
    mixed = dot("lhqk,lkhe->lqhe", probs_low, values).reshape(rows, seq, local).astype(bf16)
    attn_out, ffn_weights = reduce_and_gather(dot("lsd,ed->lse", mixed, proj_t), ffn_shard, 3)
    up = ffn_weights[:, :units]
    down_t = ffn_weights[:, units:]
    resid = tokens + gate_a * attn_out
    normed_f, inverse_f = norm_parts(resid)
    ffn_in = (normed_f * (1.0 + scale_f) + shift_f).astype(bf16)
    hidden_pre = dot("lsd,dn->lsn", ffn_in, up)
    hidden, gelu_pull = jax.vjp(gelu_tanh, hidden_pre)
    hidden = hidden.astype(bf16)
    d_ffn_out = (gate_f * cotangent).astype(bf16)
    d_hidden_pre = gelu_pull(dot("lse,en->lsn", d_ffn_out, down_t))[0].astype(bf16)
    d_ffn_in = reduce_tensor(dot("lsn,dn->lsd", d_hidden_pre, up), 4)

    ffn_part = dot("lsn,en->lse", hidden, down_t)
    d_gate_f = jnp.sum(cotangent * ffn_part, axis=1)
    d_shift_f = jnp.sum(d_ffn_in, axis=1)
    d_scale_f = jnp.sum(d_ffn_in * normed_f, axis=1)
    d_resid = cotangent + norm_back(normed_f, inverse_f, d_ffn_in * (1.0 + scale_f))
    d_gate_a = jnp.sum(d_resid * attn_out, axis=1)
    d_attn_out = (gate_a * d_resid).astype(bf16)
    d_mixed = dot("lse,ed->lsd", d_attn_out, proj_t).astype(bf16)
    d_mixed = d_mixed.reshape(rows, seq, heads, HEAD_DIM)
    d_probs = dot("lqhe,lkhe->lhqk", d_mixed, values)
    d_scores = probs * (d_probs - jnp.sum(d_probs * probs, axis=-1, keepdims=True))
    d_scores = d_scores.astype(bf16)
    d_values = dot("lhqk,lqhe->lkhe", probs_low, d_mixed)
    d_queries = dot("lhqk,lkhe->lqhe", d_scores, keys) * scale
    d_keys = dot("lhqk,lqhe->lkhe", d_scores, queries) * scale
    d_projected = jnp.stack([d_queries, d_keys, d_values], axis=2)
    d_projected = d_projected.reshape(rows, seq, 3 * local).astype(bf16)
    d_attn_part = dot("lse,de->lsd", d_projected, w_in)

    grads = jnp.concatenate(
        [
            dot("lsd,lse->de", attn_in, d_projected).astype(bf16),
            dot("lse,lsd->ed", d_attn_out, mixed).astype(bf16),
            dot("lsd,lsn->dn", ffn_in, d_hidden_pre).astype(bf16),
            dot("lse,lsn->en", d_ffn_out, hidden).astype(bf16),
        ],
        axis=1,
    )
    d_shift_a = jnp.sum(d_attn_part, axis=1)
    d_scale_a = jnp.sum(d_attn_part * normed_a, axis=1)
    ones = jnp.where(tensor_at == 0, 1.0, 0.0)
    d_modulation = jnp.concatenate(
        [d_shift_a, d_scale_a, d_gate_a * ones, d_shift_f * ones, d_scale_f * ones, d_gate_f],
        axis=1,
    )
    d_attn_own, ffn_own, grads, d_mod_all, d_act = final_sums(
        d_attn_part, ffn_part, grads, d_modulation, w_ada
    )
    grad_attn, grad_ffn = grads[:, : 4 * local], grads[:, 4 * local :]
    first = tensor_at * own_tokens
    own = lambda value: lax.dynamic_slice_in_dim(value, first, own_tokens, 1)
    latent_out = (own(resid) + gate_f * ffn_own).astype(bf16)
    grad_latent = own(d_resid) + norm_back(
        own(normed_a), own(inverse_a), d_attn_own * (1.0 + scale_a)
    )

    grad_ada = dot("ld,le->de", cond_mine, d_mod_all)
    grad_condition = jax.vjp(silu_value, condition.astype(f32))[1](d_act)[0]

    grad_qkv = jnp.stack([grad_attn[:, j * local : (j + 1) * local] for j in range(3)], axis=0)
    grad_proj = grad_attn[:, 3 * local :].T
    grad_up = grad_ffn[:, :units]
    grad_down = grad_ffn[:, units:].T
    return (
        latent_out,
        grad_latent,
        grad_condition,
        grad_ada,
        grad_qkv,
        grad_proj,
        grad_up,
        grad_down,
    )


def dot_plain(left, right):
    return lax.dot_general(left, right, (((1,), (0,)), ((), ())), preferred_element_type=f32)


def dot_right(left, right):
    return lax.dot_general(left, right, (((1,), (1,)), ((), ())), preferred_element_type=f32)


def dot_left(left, right):
    return lax.dot_general(left, right, (((0,), (0,)), ((), ())), preferred_element_type=f32)


def gelu_and_slope(values):
    root = math.sqrt(2.0 / math.pi)
    squares = values * values
    bent = jnp.tanh(root * values * (1.0 + 0.044715 * squares))
    half = 0.5 * (1.0 + bent)
    slope = half + 0.5 * values * (1.0 - bent * bent) * (root * (1.0 + 3.0 * 0.044715 * squares))
    return values * half, slope


def block_kernel(names, *refs):
    v = types.SimpleNamespace(**dict(zip(names, refs)))
    count = lax.axis_size("dp")
    pairs = count // 2
    d, z = lax.axis_index("dp"), lax.axis_index("tensor")
    p, c, h, l = d // 2, lax.rem(d, 2), z // 2, lax.rem(z, 2)
    t = 2 * c + l
    t_sib, t_near, t_cross = 2 * (1 - c) + l, 2 * c + 1 - l, 2 * (1 - c) + 1 - l
    diag = c == h
    off = c != h
    sib = (2 * p + 1 - c, z)
    near = (d, 2 * h + 1 - l)
    cross = (2 * p + 1 - c, 2 * h + 1 - l)
    swap = (2 * p + h, 2 * c + l)
    rows, own, width = v.x_ref.shape
    seq = v.x_all.shape[1]
    half = seq // 2
    shard = v.ada_ref.shape[0]
    columns = v.ada_ref.shape[1]
    local = v.mixed.shape[2]
    heads = local // HEAD_DIM
    units = v.hidden.shape[2]
    scale = HEAD_DIM ** (-0.5)
    later = []

    def copy(source, target, sems, slot, to, there=None):
        return pltpu.make_async_remote_copy(
            src_ref=source,
            dst_ref=target,
            send_sem=sems.at[0, slot],
            recv_sem=sems.at[1, slot if there is None else there],
            device_id=to,
            device_id_type=MESH,
        )

    def send(*args, **kwargs):
        moved = copy(*args, **kwargs)
        moved.start()
        later.append(moved.wait_send)

    def send_if(condition, *args, **kwargs):
        moved = copy(*args, **kwargs)
        pl.when(condition)(moved.start)

        def finish():
            pl.when(condition)(moved.wait_send)

        later.append(finish)

    def came(target, sems, slot):
        copy(target, target, sems, slot, sib).wait_recv()

    def came_if(condition, target, sems, slot):
        pl.when(condition)(copy(target, target, sems, slot, sib).wait_recv)

    def tokens_of(ref, at, size=own):
        return ref.at[:, pl.ds(pl.multiple_of(at * size, size), size)]

    def rows_of(ref, at, size):
        return ref.at[pl.ds(pl.multiple_of(at * size, size), size)]

    barrier = pltpu.get_barrier_semaphore()
    here = 2 * d + h
    for step in range(1, 2 * count):
        other = lax.rem(here + step, 2 * count)
        pl.semaphore_signal(
            barrier,
            inc=1,
            device_id=(other // 2, 2 * lax.rem(other, 2) + l),
            device_id_type=MESH,
        )
    for side in range(2):
        for part in range(2):
            pl.semaphore_signal(
                barrier,
                inc=1,
                device_id=(2 * p + side, 2 * part + 1 - l),
                device_id_type=MESH,
            )
    pl.semaphore_wait(barrier, 2 * count - 1 + 4)

    for step in range(1, count):
        peer = lax.rem(d + step, count)
        send(v.cond_ref.at[peer], v.cond_buf.at[d], v.s_cond, step - 1, (peer, z))
    v.cond_buf[d] = v.cond_ref[d]

    def swap_in(ref, whole, sems):
        send_if(off, ref, tokens_of(whole, z), sems, 0, swap)

        @pl.when(diag)
        def _():
            tokens_of(whole, t)[...] = ref[...]

    def swap_came(whole, sems):
        came_if(off, tokens_of(whole, t), sems, 0)

    def spread_tokens(whole, sems):
        block = tokens_of(whole, t)
        send(block, block, sems, 0, sib)
        send(block, block, sems, 1, near)

    def forward_tokens(whole, sems):
        block = tokens_of(whole, t_near)
        came(block, sems, 1)
        send(block, block, sems, 2, sib)

    def tokens_came(whole, sems):
        came(tokens_of(whole, t_sib), sems, 0)
        came(tokens_of(whole, t_cross), sems, 2)

    def column_start(ref, whole, sems):
        block = rows_of(whole, d, shard)
        send(ref, block, sems, 1, (2 * p + h, 2 * (1 - h) + l), there=c)
        send_if(off, ref, block, sems, 0, sib, there=c)

        @pl.when(diag)
        def _():
            block[...] = ref[...]

    def column_came(whole, sems, condition):
        for side in range(2):
            local_one = jnp.logical_and(diag, c == side)
            came_if(
                jnp.logical_and(condition, jnp.logical_not(local_one)),
                rows_of(whole, 2 * p + side, shard),
                sems,
                side,
            )

    def plane_start(whole, sems, condition):
        block = rows_of(whole, p, 2 * shard)
        for step in range(1, pairs):
            to = lax.rem(p + step, pairs)
            send_if(condition, block, block, sems, step - 1, (2 * to + c, z))

    def plane_came(whole, sems):
        for step in range(1, pairs):
            source = lax.rem(p + pairs - step, pairs)
            came(rows_of(whole, source, 2 * shard), sems, step - 1)

    swap_in(v.x_ref, v.x_all, v.s_xswap)
    column_start(v.wa_ref, v.w_attn, v.s_acol)

    for step in range(1, count):
        came(v.cond_buf.at[lax.rem(d + count - step, count)], v.s_cond, step - 1)
    for at in range(count):
        v.act_rows[rows * at : rows * (at + 1)] = v.cond_buf[at]
    act = silu_value(v.act_rows[...]).astype(bf16)
    v.act_rows[...] = act.astype(f32)
    v.mod_rows[...] = dot_plain(act, v.ada_ref[...])
    for at in range(count):
        v.mod_part[at] = v.mod_rows[rows * at : rows * (at + 1)]
    for at in range(count):
        to = (2 * (at // 2) + h, 2 * (at % 2) + l)
        mine = jnp.logical_and(d == to[0], z == to[1])
        send_if(jnp.logical_not(mine), v.mod_part.at[at], v.mod_recv.at[d], v.s_mod, at, to, there=d)

        @pl.when(mine)
        def _():
            v.mod_recv[d] = v.mod_part[at]

    column_came(v.w_attn, v.s_acol, diag)
    plane_start(v.w_attn, v.s_aplane, diag)
    swap_came(v.x_all, v.s_xswap)
    spread_tokens(v.x_all, v.s_x)

    for at in range(count):
        mine = jnp.logical_and(d == at, z == 2 * c + l)
        came_if(jnp.logical_not(mine), v.mod_recv.at[at], v.s_mod, at)
    v.mod_all[t] = jnp.sum(v.mod_recv[...], axis=0)
    group = ((sib, t_sib), (near, t_near), (cross, t_cross))
    for slot, (to, _) in enumerate(group):
        send(v.mod_all.at[t], v.mod_all.at[t], v.s_modall, slot, to)

    column_came(v.w_attn, v.s_acol, off)
    plane_start(v.w_attn, v.s_aplane, off)
    column_start(v.wf_ref, v.w_ffn, v.s_fcol)
    swap_in(v.cot_ref, v.cot_all, v.s_cswap)
    forward_tokens(v.x_all, v.s_x)
    for slot, (_, at) in enumerate(group):
        came(v.mod_all.at[at], v.s_modall, slot)
    column_came(v.w_ffn, v.s_fcol, diag)
    plane_start(v.w_ffn, v.s_fplane, diag)
    for row in range(rows):
        full = jnp.concatenate([v.mod_all[at][row : row + 1] for at in range(4)], axis=1)
        for at in range(6):
            v.modv[at, row] = full[:, at * width : (at + 1) * width]
    tokens_came(v.x_all, v.s_x)

    order = [lax.rem(1 - c + turn, 2) for turn in range(2)]

    for row in order:
        normed, inverse = norm_parts(v.x_all[row].astype(f32))
        v.normed_a[row] = normed
        v.inverse_a[row] = inverse
        v.attn_in[row] = (normed * (1.0 + v.modv[1, row]) + v.modv[0, row]).astype(bf16)

    plane_came(v.w_attn, v.s_aplane)
    for row in order:
        v.qkv[row] = dot_plain(v.attn_in[row], v.w_attn[:, : 3 * local]).astype(bf16)

    def head(row, kind, at):
        first = kind * local + at * HEAD_DIM
        return v.qkv[row, :, first : first + HEAD_DIM]

    def exchange_start(part, pair, sems):
        send(part.at[1 - c], pair, sems, 0, sib)

    def exchange_near(part, pair, both, other, sems):
        came(pair, sems, 0)
        both[...] = (part[c].astype(f32) + pair[...].astype(f32)).astype(bf16)
        send(both, other, sems, 1, near)

    def exchange_back(both, other, out, sems):
        came(other, sems, 1)
        out[c] = (both[...].astype(f32) + other[...].astype(f32)).astype(bf16)
        send(out.at[c], out.at[c], sems, 2, sib)

    for turn, row in enumerate(order):
        for at in range(heads):
            scores = dot_right(head(row, 0, at), head(row, 1, at)) * scale
            shifted = jnp.exp(scores - jnp.max(scores, axis=-1, keepdims=True))
            probs = shifted / jnp.sum(shifted, axis=-1, keepdims=True)
            v.probs[row, at] = probs
            v.mixed[row, :, at * HEAD_DIM : (at + 1) * HEAD_DIM] = dot_plain(
                probs.astype(bf16), head(row, 2, at)
            ).astype(bf16)
        v.a_part[row] = dot_right(v.mixed[row], v.w_attn[:, 3 * local :]).astype(bf16)
        if turn == 0:
            exchange_start(v.a_part, v.a_pair, v.s_a)
    exchange_near(v.a_part, v.a_pair, v.a_both, v.a_other, v.s_a)

    swap_came(v.cot_all, v.s_cswap)
    spread_tokens(v.cot_all, v.s_cot)
    column_came(v.w_ffn, v.s_fcol, off)
    plane_start(v.w_ffn, v.s_fplane, off)
    exchange_back(v.a_both, v.a_other, v.a_out, v.s_a)
    forward_tokens(v.cot_all, v.s_cot)
    came(v.a_out.at[1 - c], v.s_a, 2)

    for row in order:
        resid = v.x_all[row].astype(f32) + v.modv[2, row] * v.a_out[row].astype(f32)
        v.resid[row] = resid
        normed, inverse = norm_parts(resid)
        v.normed_f[row] = normed
        v.inverse_f[row] = inverse
        v.ffn_in[row] = (normed * (1.0 + v.modv[4, row]) + v.modv[3, row]).astype(bf16)
    tokens_came(v.cot_all, v.s_cot)
    for row in order:
        v.d_ffn_out[row] = (v.modv[5, row] * v.cot_all[row].astype(f32)).astype(bf16)

    plane_came(v.w_ffn, v.s_fplane)
    for turn, row in enumerate(order):
        hidden, slope = gelu_and_slope(dot_plain(v.ffn_in[row], v.w_ffn[:, :units]))
        v.hidden[row] = hidden.astype(bf16)
        v.d_hidden[row] = (dot_plain(v.d_ffn_out[row], v.w_ffn[:, units:]) * slope).astype(bf16)
        v.b_part[row] = dot_right(v.d_hidden[row], v.w_ffn[:, :units]).astype(bf16)
        if turn == 0:
            exchange_start(v.b_part, v.b_pair, v.s_b)
    exchange_near(v.b_part, v.b_pair, v.b_both, v.b_other, v.s_b)

    def whole(ref):
        return ref[...].reshape(rows * seq, ref.shape[2])

    def reduce_start(at):
        for step in range(1, pairs):
            to = lax.rem(p + step, pairs)
            send(
                rows_of(v.grads.at[at], to, 2 * shard),
                v.grad_recv.at[at, step - 1],
                v.s_red.at[at],
                step - 1,
                (2 * to + c, z),
            )

    def reduce_column(at):
        total = rows_of(v.grads.at[at], p, 2 * shard)[...].astype(f32)
        for step in range(1, pairs):
            came(v.grad_recv.at[at, step - 1], v.s_red.at[at], step - 1)
            total += v.grad_recv[at, step - 1].astype(f32)
        v.grad_sum[at] = total
        v.grad_low[at] = total.astype(bf16)
        sems = v.s_home.at[at]
        low = v.grad_low.at[at]
        for side in range(2):
            send_if(
                off,
                low.at[pl.ds(side * shard, shard)],
                v.home_recv.at[at, 1],
                sems,
                side,
                (2 * p + side, 2 * c + l),
                there=1,
            )
        send_if(diag, rows_of(low, 1 - c, shard), v.home_recv.at[at, 0], sems, 0, sib, there=0)

    def reduce_end(at):
        came(v.home_recv.at[at, 1], v.s_home.at[at], 1)

        @pl.when(diag)
        def _():
            v.grad_ref[at] = rows_of(v.grad_sum.at[at], c, shard)[...] + v.home_recv[at, 1].astype(f32)

        @pl.when(off)
        def _():
            came(v.home_recv.at[at, 0], v.s_home.at[at], 0)
            v.grad_ref[at] = v.home_recv[at, 0].astype(f32) + v.home_recv[at, 1].astype(f32)

    v.grads[1] = dot_left(whole(v.ffn_in), whole(v.d_hidden)).astype(bf16)
    reduce_start(1)
    v.grads[2] = dot_left(whole(v.d_ffn_out), whole(v.hidden)).astype(bf16)
    reduce_start(2)
    exchange_back(v.b_both, v.b_other, v.b_out, v.s_b)
    for row in order:
        ffn_part = dot_right(v.hidden[row], v.w_ffn[:, units:])
        v.dvec[5, row] = jnp.sum(v.cot_all[row].astype(f32) * ffn_part, axis=0, keepdims=True)
        v.f_part[row] = ffn_part.astype(bf16)
    came(v.b_out.at[1 - c], v.s_b, 2)

    def scatter_start(part, pair, sems):
        send(tokens_of(part, 1 - c, half), pair, sems, 0, sib)

    def scatter_near(part, pair, kept, low, other, sems):
        came(pair, sems, 0)
        kept[...] = tokens_of(part, c, half)[...].astype(f32) + pair[...].astype(f32)
        low[...] = tokens_of(kept, 1 - l)[...].astype(bf16)
        send(low, other, sems, 1, near)

    def scatter_end(kept, other, sems):
        came(other, sems, 1)
        return tokens_of(kept, l)[...] + other[...].astype(f32)

    scatter_start(v.f_part, v.f_pair, v.s_f)
    for row in order:
        d_ffn_in = v.b_out[row].astype(f32)
        normed = v.normed_f[row]
        v.dvec[3, row] = jnp.sum(d_ffn_in, axis=0, keepdims=True)
        v.dvec[4, row] = jnp.sum(d_ffn_in * normed, axis=0, keepdims=True)
        d_resid = v.cot_all[row].astype(f32) + norm_back(
            normed, v.inverse_f[row], d_ffn_in * (1.0 + v.modv[4, row])
        )
        v.d_resid[row] = d_resid
        v.dvec[2, row] = jnp.sum(d_resid * v.a_out[row].astype(f32), axis=0, keepdims=True)
        v.d_attn_out[row] = (v.modv[2, row] * d_resid).astype(bf16)
    v.grads[0, :, 3 * local :] = dot_left(whole(v.d_attn_out), whole(v.mixed)).astype(bf16)
    for row in order:
        v.d_mixed[row] = dot_plain(v.d_attn_out[row], v.w_attn[:, 3 * local :]).astype(bf16)
        for at in range(heads):
            d_mixed = v.d_mixed[row, :, at * HEAD_DIM : (at + 1) * HEAD_DIM]
            probs = v.probs[row, at]
            d_probs = dot_right(d_mixed, head(row, 2, at))
            d_scores = probs * (d_probs - jnp.sum(d_probs * probs, axis=-1, keepdims=True))
            d_scores = d_scores.astype(bf16)
            found = (
                dot_plain(d_scores, head(row, 1, at)) * scale,
                dot_left(d_scores, head(row, 0, at)) * scale,
                dot_left(probs.astype(bf16), d_mixed),
            )
            for kind in range(3):
                first = kind * local + at * HEAD_DIM
                v.d_qkv[row, :, first : first + HEAD_DIM] = found[kind].astype(bf16)
    v.grads[0, :, : 3 * local] = dot_left(whole(v.attn_in), whole(v.d_qkv)).astype(bf16)
    reduce_start(0)
    for row in order:
        d_attn_in = dot_right(v.d_qkv[row], v.w_attn[:, : 3 * local])
        v.dvec[0, row] = jnp.sum(d_attn_in, axis=0, keepdims=True)
        v.dvec[1, row] = jnp.sum(d_attn_in * v.normed_a[row], axis=0, keepdims=True)
        v.e_part[row] = d_attn_in.astype(bf16)
    scatter_start(v.e_part, v.e_pair, v.s_e)
    first_one = jnp.where(t == 0, 1.0, 0.0)
    for row in range(rows):
        full = jnp.concatenate(
            [
                v.dvec[at, row] * first_one if at in (2, 3, 4) else v.dvec[at, row]
                for at in range(6)
            ],
            axis=1,
        )
        for at in range(4):
            v.dm_part[at, row : row + 1] = full[:, at * columns : (at + 1) * columns]
    for slot, (to, at) in enumerate(group):
        send(v.dm_part.at[at], v.dm_recv.at[t], v.s_dm, slot, to)
    v.dm_recv[t] = v.dm_part[t]
    scatter_near(v.e_part, v.e_pair, v.e_kept, v.e_low, v.e_other, v.s_e)
    scatter_near(v.f_part, v.f_pair, v.f_kept, v.f_low, v.f_other, v.s_f)
    for slot, (_, at) in enumerate(group):
        came(v.dm_recv.at[at], v.s_dm, slot)
    v.dm_own[...] = jnp.sum(v.dm_recv[...], axis=0).astype(bf16).astype(f32)
    j = 2 * p + h
    for at in range(count):
        mine = jnp.logical_and(d == at, z == 2 * c + l)
        send_if(
            jnp.logical_not(mine), v.dm_own, v.dm_all.at[j], v.s_dmall, at, (at, 2 * c + l), there=j
        )

        @pl.when(mine)
        def _():
            v.dm_all[j] = v.dm_own[...]

    reduce_column(1)
    reduce_column(2)
    for at in range(count):
        mine = jnp.logical_and(d == 2 * (at // 2) + h, z == 2 * (at % 2) + l)
        came_if(jnp.logical_not(mine), v.dm_all.at[at], v.s_dmall, at)
    for at in range(count):
        v.dm_rows[rows * at : rows * (at + 1)] = v.dm_all[at]
    everyone = v.dm_rows[...].astype(bf16)
    d_act = dot_right(everyone, v.ada_ref[...])
    for at in range(count):
        v.act_part[at] = d_act[rows * at : rows * (at + 1)]
    for step in range(1, count):
        peer = lax.rem(d + step, count)
        send(v.act_part.at[peer], v.terms.at[d], v.s_act, step - 1, (peer, z))
    v.terms[d] = v.act_part[d]
    v.grad_ada_ref[...] = dot_left(v.act_rows[...].astype(bf16), everyone)

    f_own = scatter_end(v.f_kept, v.f_other, v.s_f)
    gate_f = jnp.concatenate([v.modv[5, row][None] for row in range(rows)], axis=0)
    latent = (tokens_of(v.resid, t)[...] + gate_f * f_own).astype(bf16)
    v.latent_low[...] = latent
    send_if(off, v.latent_low, v.latent_ref, v.s_lswap, 0, swap)
    e_own = scatter_end(v.e_kept, v.e_other, v.s_e)
    scale_a = jnp.concatenate([v.modv[1, row][None] for row in range(rows)], axis=0)
    grad_x = tokens_of(v.d_resid, t)[...] + norm_back(
        tokens_of(v.normed_a, t)[...], tokens_of(v.inverse_a, t)[...], e_own * (1.0 + scale_a)
    )
    v.grad_x_low[...] = grad_x.astype(bf16)
    send_if(off, v.grad_x_low, v.grad_x_recv, v.s_gswap, 0, swap)

    @pl.when(diag)
    def _():
        v.latent_ref[...] = latent
        v.grad_x_ref[...] = grad_x

    for step in range(1, count):
        came(v.terms.at[lax.rem(d + count - step, count)], v.s_act, step - 1)
    v.gathered[z] = v.terms[...]
    for step in range(1, 4):
        peer = lax.rem(z + step, 4)
        send(v.terms, v.gathered.at[z], v.s_gat, step - 1, (d, peer))
    reduce_column(0)
    for step in range(1, 4):
        came(v.gathered.at[lax.rem(z + 4 - step, 4)], v.s_gat, step - 1)
    v.act_ref[...] = jnp.sum(v.gathered[...], axis=0)
    reduce_end(1)
    reduce_end(2)

    @pl.when(off)
    def _():
        came(v.grad_x_recv, v.s_gswap, 0)
        v.grad_x_ref[...] = v.grad_x_recv[...].astype(f32)
        came(v.latent_ref, v.s_lswap, 0)

    reduce_end(0)
    for finish in later:
        finish()


def block_call(cond, ada, x, cot, wa, wf, local, units):
    count = lax.axis_size("dp")
    pairs = count // 2
    rows, own, width = x.shape
    seq = 4 * own
    shard, columns = ada.shape
    shape = jax.ShapeDtypeStruct
    inputs = dict(cond_ref=cond, ada_ref=ada, x_ref=x, cot_ref=cot, wa_ref=wa, wf_ref=wf)
    outs = dict(
        latent_ref=shape(x.shape, bf16),
        grad_x_ref=shape(x.shape, f32),
        grad_ref=shape((3, shard, width), f32),
        grad_ada_ref=shape(ada.shape, f32),
        act_ref=shape((count, rows, shard), f32),
    )
    tokens = (rows, seq, width)
    half = (rows, seq // 2, width)
    low = dict(
        x_all=tokens, cot_all=tokens, attn_in=tokens, ffn_in=tokens,
        d_ffn_out=tokens, d_attn_out=tokens,
        hidden=(rows, seq, units), d_hidden=(rows, seq, units),
        w_attn=(width, 4 * local), w_ffn=(width, 2 * units),
        qkv=(rows, seq, 3 * local), d_qkv=(rows, seq, 3 * local),
        mixed=(rows, seq, local), d_mixed=(rows, seq, local),
        a_part=tokens, a_pair=(seq, width), a_both=(seq, width),
        a_other=(seq, width), a_out=tokens,
        b_part=tokens, b_pair=(seq, width), b_both=(seq, width),
        b_other=(seq, width), b_out=tokens,
        e_part=tokens, e_pair=half, e_low=x.shape, e_other=x.shape,
        f_part=tokens, f_pair=half, f_low=x.shape, f_other=x.shape,
        latent_low=x.shape, grad_x_low=x.shape, grad_x_recv=x.shape,
        grads=(3, width, width), grad_recv=(3, pairs - 1, 2 * shard, width),
        grad_low=(3, 2 * shard, width), home_recv=(3, 2, shard, width),
    )
    wide = dict(
        cond_buf=(count, rows, shard), act_rows=(count * rows, shard),
        mod_rows=(count * rows, columns), mod_part=(count, rows, columns),
        mod_recv=(count, rows, columns), mod_all=(4, rows, columns),
        modv=(6, rows, 1, width), dvec=(6, rows, 1, width),
        normed_a=tokens, inverse_a=(rows, seq, 1),
        resid=tokens, normed_f=tokens, inverse_f=(rows, seq, 1), d_resid=tokens,
        probs=(rows, local // HEAD_DIM, seq, seq),
        e_kept=half, f_kept=half, grad_sum=(3, 2 * shard, width),
        dm_part=(4, rows, columns), dm_recv=(4, rows, columns), dm_own=(rows, columns),
        dm_all=(count, rows, columns), dm_rows=(count * rows, columns),
        act_part=(count, rows, shard), terms=(count, rows, shard),
        gathered=(4, count, rows, shard),
    )
    sems = dict(
        s_cond=(2, count - 1), s_mod=(2, count), s_modall=(2, 3), s_xswap=(2, 1),
        s_cswap=(2, 1), s_x=(2, 3), s_cot=(2, 3), s_acol=(2, 2), s_fcol=(2, 2),
        s_aplane=(2, pairs - 1), s_fplane=(2, pairs - 1), s_a=(2, 3), s_b=(2, 3),
        s_e=(2, 2), s_f=(2, 2), s_red=(3, 2, pairs - 1), s_home=(3, 2, 2),
        s_dm=(2, 3), s_dmall=(2, count), s_act=(2, count - 1), s_gat=(2, 3),
        s_lswap=(2, 1), s_gswap=(2, 1),
    )
    scratch = {name: pltpu.VMEM(size, bf16) for name, size in low.items()}
    scratch.update({name: pltpu.VMEM(size, f32) for name, size in wide.items()})
    scratch.update({name: pltpu.SemaphoreType.DMA(size) for name, size in sems.items()})
    names = tuple(inputs) + tuple(outs) + tuple(scratch)
    return pl.pallas_call(
        functools.partial(block_kernel, names),
        out_shape=tuple(outs.values()),
        in_specs=[VMEM] * len(inputs),
        out_specs=tuple(VMEM for _ in outs),
        scratch_shapes=list(scratch.values()),
        compiler_params=pltpu.CompilerParams(
            collective_id=7, has_side_effects=True, vmem_limit_bytes=60 * 2**20
        ),
    )(*inputs.values())


def fast_shards(latent_in, condition, w_ada, w_qkv, w_proj, w_up, w_down, out_grad):
    count = lax.axis_size("dp")
    rows, _, width = latent_in.shape
    shard = w_ada.shape[0]
    local = w_proj.shape[0]
    units = w_down.shape[0]
    attn_shard = jnp.concatenate([w_qkv[0], w_qkv[1], w_qkv[2], w_proj.T], axis=1)
    ffn_shard = jnp.concatenate([w_up, w_down.T], axis=1)
    cond = condition.astype(f32)
    blocks = cond.reshape(rows, count, shard).transpose(1, 0, 2)
    latent_out, grad_latent, grads, grad_ada, act = block_call(
        blocks, w_ada, latent_in, out_grad, attn_shard, ffn_shard, local, units
    )
    d_act = act.transpose(1, 0, 2).reshape(rows, count * shard)
    grad_condition = jax.vjp(silu_value, cond)[1](d_act)[0]
    grad_qkv = jnp.stack([grads[0, :, j * local : (j + 1) * local] for j in range(3)], axis=0)
    return (
        latent_out,
        grad_latent,
        grad_condition,
        grad_ada,
        grad_qkv,
        grads[0, :, 3 * local :].T,
        grads[1],
        grads[2].T,
    )


def can_pair(mesh):
    count, group = mesh.shape["dp"], mesh.shape["tensor"]
    return group == 4 and count % 2 == 0


def body(mesh):
    def run(*args):
        shard = args[2].shape[0]
        square = args[5].shape[1] == args[0].shape[2] and 4 * args[4].shape[0] == args[0].shape[2]
        fits = can_pair(mesh) and shard % 16 == 0 and square and args[0].shape[1] % 16 == 0
        return (fast_shards if fits else shards)(*args)

    return run


def solution(mesh):
    return jax.shard_map(
        body(mesh),
        mesh=mesh,
        in_specs=(
            P("dp", "tensor", None),
            P("dp", None),
            P("dp", "tensor"),
            P(None, "dp", "tensor"),
            P("tensor", "dp"),
            P("dp", "tensor"),
            P("tensor", "dp"),
            P("dp", "tensor", None),
        ),
        out_specs=(
            P("dp", "tensor", None),
            P("dp", "tensor", None),
            P("dp", None),
            P("dp", "tensor"),
            P(None, "dp", "tensor"),
            P("tensor", "dp"),
            P("dp", "tensor"),
            P("tensor", "dp"),
        ),
        check_vma=False,
    )
```

```python
import functools
import math
import types

import jax
import jax.numpy as jnp
from jax import lax
from jax.experimental import pallas as pl
from jax.experimental.pallas import tpu as pltpu
from jax.sharding import PartitionSpec as P

MESH = pl.DeviceIdType.MESH
VMEM = pl.BlockSpec(memory_space=pltpu.VMEM)

HEAD_DIM = 64
FF_BLOCK = 256
EPS = 1e-06
f32 = jnp.float32
bf16 = jnp.bfloat16


def silu_value(values):
    return values / (1.0 + jnp.exp(-values))


def gelu_tanh(values):
    return (
        0.5
        * values
        * (
            1.0
            + jnp.tanh(math.sqrt(2.0 / math.pi) * (values + 0.044715 * values * values * values))
        )
    )


def norm_parts(values):
    centered = values - jnp.mean(values, axis=-1, keepdims=True)
    variance = jnp.mean(centered * centered, axis=-1, keepdims=True)
    inverse = lax.rsqrt(variance + EPS)
    return centered * inverse, inverse


def norm_back(normed, inverse, grad):
    return inverse * (
        grad
        - jnp.mean(grad, axis=-1, keepdims=True)
        - normed * jnp.mean(grad * normed, axis=-1, keepdims=True)
    )


def dot(form, left, right):
    return jnp.einsum(form, left, right, preferred_element_type=f32)


def gather_tensor(block, axis):
    return lax.all_gather(block, "tensor", axis=axis, tiled=True)


def greet(axes):
    barrier = pltpu.get_barrier_semaphore()
    total = 0
    for axis in axes:
        size = lax.axis_size(axis)
        me = lax.axis_index(axis)
        for step in range(1, size):
            pl.semaphore_signal(
                barrier, inc=1, device_id={axis: lax.rem(me + step, size)}, device_id_type=MESH
            )
        total += size - 1
    pl.semaphore_wait(barrier, total)


def start_exchange(axis, source, target, sems):
    size = lax.axis_size(axis)
    me = lax.axis_index(axis)
    copies = []
    for step in range(1, size):
        peer = lax.rem(me + step, size)
        copy = pltpu.make_async_remote_copy(
            src_ref=source(peer),
            dst_ref=target,
            send_sem=sems.at[0, step - 1],
            recv_sem=sems.at[1, step - 1],
            device_id={axis: peer},
            device_id_type=MESH,
        )
        copy.start()
        copies.append(copy)
    return copies


def wait_all(copies):
    for copy in copies:
        copy.wait()


def exchange(axis, source, target, sems):
    wait_all(start_exchange(axis, source, target, sems))


def sem_pair(axis):
    return pltpu.SemaphoreType.DMA((2, lax.axis_size(axis) - 1))


def call(kernel, outs, scratch, number, *args):
    return pl.pallas_call(
        kernel,
        out_shape=outs,
        in_specs=[VMEM] * len(args),
        out_specs=jax.tree.map(lambda _: VMEM, outs),
        scratch_shapes=scratch,
        compiler_params=pltpu.CompilerParams(
            collective_id=number, has_side_effects=True, vmem_limit_bytes=48 * 2**20
        ),
    )(*args)


def modulation_kernel(
    cond_ref, w_ref, x_ref, shard_ref, mod_ref, act_ref, x_all, w_all,
    cond_buf, part, recv, own, s0, s1, s2, s3, s4, s5
):
    count = lax.axis_size("dp")
    me, mine = lax.axis_index("dp"), lax.axis_index("tensor")
    greet(("dp", "tensor"))
    copies = start_exchange("dp", lambda peer: cond_ref.at[peer], cond_buf.at[me], s0)
    x_own = token_block(x_all, mine, x_ref.shape[1])
    x_copies = start_exchange("tensor", lambda peer: x_ref, x_own, s3)
    cond_buf[me] = cond_ref[me]
    x_own[...] = x_ref[...]
    w_all[me] = shard_ref[...]
    wait_all(copies)

    @pl.loop(0, count)
    def _(at):
        act = silu_value(cond_buf[at]).astype(bf16)
        act_ref[at] = act.astype(f32)
        part[at] = jnp.dot(act, w_ref[...], preferred_element_type=f32)

    copies = start_exchange("dp", lambda peer: part.at[peer], recv.at[me], s1)
    recv[me] = part[me]
    pairs = count // 2
    chip, side = me // 2, lax.rem(me, 2)
    sibling = 2 * chip + 1 - side

    def send(source, at, to, sems, number):
        copy = pltpu.make_async_remote_copy(
            src_ref=source,
            dst_ref=w_all.at[at],
            send_sem=sems.at[0, number],
            recv_sem=sems.at[1, number],
            device_id={"dp": to},
            device_id_type=MESH,
        )
        copy.start()
        return copy

    far = [
        send(shard_ref, me, 2 * lax.rem(chip + step, pairs) + side, s4, step)
        for step in range(1, pairs)
    ]
    near = [send(shard_ref, me, sibling, s5, 0)]
    wait_all(copies)
    own[...] = jnp.sum(recv[...], axis=0)
    copies = start_exchange("tensor", lambda peer: own, mod_ref.at[mine], s2)
    mod_ref[mine] = own[...]
    for step in range(1, pairs):
        far[step - 1].wait()
        came = 2 * lax.rem(chip + pairs - step, pairs) + side
        near.append(send(w_all.at[came], came, sibling, s5, step))
    wait_all(near)
    wait_all(copies)
    wait_all(x_copies)


def modulation_of(condition, w_ada, block, shard):
    count, group = lax.axis_size("dp"), lax.axis_size("tensor")
    rows, width = condition.shape
    shard_rows, columns = w_ada.shape
    blocks = condition.astype(f32).reshape(rows, count, shard_rows).transpose(1, 0, 2)
    mod, act, x_all, w_all = call(
        modulation_kernel,
        (
            jax.ShapeDtypeStruct((group, rows, columns), f32),
            jax.ShapeDtypeStruct((count, rows, shard_rows), f32),
            jax.ShapeDtypeStruct((rows, group * block.shape[1], width), bf16),
            jax.ShapeDtypeStruct((count,) + shard.shape, bf16),
        ),
        [
            pltpu.VMEM((count, rows, shard_rows), f32),
            pltpu.VMEM((count, rows, columns), f32),
            pltpu.VMEM((count, rows, columns), f32),
            pltpu.VMEM((rows, columns), f32),
            sem_pair("dp"),
            sem_pair("dp"),
            sem_pair("tensor"),
            sem_pair("tensor"),
            pltpu.SemaphoreType.DMA((2, count // 2)),
            pltpu.SemaphoreType.DMA((2, count // 2)),
        ],
        1,
        blocks,
        w_ada,
        block,
        shard,
    )
    mod = mod.transpose(1, 0, 2).reshape(rows, group * columns)
    act = act.reshape(count * rows, shard_rows).astype(bf16)
    return mod, act, x_all, w_all.reshape(count * shard.shape[0], shard.shape[1])


def token_block(ref, at, size):
    return ref.at[:, pl.ds(pl.multiple_of(at * size, size), size)]


def finish_reduce(part_ref, out_ref, recv, first, sems):
    group = lax.axis_size("tensor")
    mine = lax.axis_index("tensor")
    size = part_ref.shape[1] // group
    wait_all(first)
    total = token_block(part_ref, mine, size)[...].astype(f32)
    for step in range(1, group):
        total += recv[lax.rem(mine + step, group)].astype(f32)
    own = token_block(out_ref, mine, size)
    own[...] = total.astype(bf16)
    return start_exchange("tensor", lambda peer: own, own, sems)


def start_reduce(part_ref, recv, sems):
    group = lax.axis_size("tensor")
    size = part_ref.shape[1] // group
    return start_exchange(
        "tensor",
        lambda peer: token_block(part_ref, peer, size),
        recv.at[lax.axis_index("tensor")],
        sems,
    )


def reduce_kernel(part_ref, out_ref, recv, s0, s1):
    greet(("tensor",))
    first = start_reduce(part_ref, recv, s0)
    wait_all(finish_reduce(part_ref, out_ref, recv, first, s1))


def reduce_gather_kernel(part_ref, shard_ref, out_ref, w_all, recv, s0, s1, s2, s3):
    count = lax.axis_size("dp")
    me = lax.axis_index("dp")
    pairs = count // 2
    chip, side = me // 2, lax.rem(me, 2)
    sibling = 2 * chip + 1 - side
    greet(("dp", "tensor"))

    def send(source, at, to, sems, number):
        copy = pltpu.make_async_remote_copy(
            src_ref=source,
            dst_ref=w_all.at[at],
            send_sem=sems.at[0, number],
            recv_sem=sems.at[1, number],
            device_id={"dp": to},
            device_id_type=MESH,
        )
        copy.start()
        return copy

    first = start_reduce(part_ref, recv, s0)
    far = [
        send(shard_ref, me, 2 * lax.rem(chip + step, pairs) + side, s2, step)
        for step in range(1, pairs)
    ]
    near = [send(shard_ref, me, sibling, s3, 0)]
    w_all[me] = shard_ref[...]
    last = finish_reduce(part_ref, out_ref, recv, first, s1)
    for step in range(1, pairs):
        far[step - 1].wait()
        came = 2 * lax.rem(chip + pairs - step, pairs) + side
        near.append(send(w_all.at[came], came, sibling, s3, step))
    wait_all(near)
    wait_all(last)


def reduce_and_gather(part, shard, number):
    group, count = lax.axis_size("tensor"), lax.axis_size("dp")
    rows, seq, width = part.shape
    total, weights = call(
        reduce_gather_kernel,
        (
            jax.ShapeDtypeStruct(part.shape, bf16),
            jax.ShapeDtypeStruct((count,) + shard.shape, bf16),
        ),
        [
            pltpu.VMEM((group, rows, seq // group, width), bf16),
            sem_pair("tensor"),
            sem_pair("tensor"),
            pltpu.SemaphoreType.DMA((2, count // 2)),
            pltpu.SemaphoreType.DMA((2, count // 2)),
        ],
        number,
        part.astype(bf16),
        shard,
    )
    return total.astype(f32), weights.reshape(count * shard.shape[0], shard.shape[1])


def reduce_tensor(part, number):
    group = lax.axis_size("tensor")
    rows, seq, width = part.shape
    return call(
        reduce_kernel,
        jax.ShapeDtypeStruct(part.shape, bf16),
        [
            pltpu.VMEM((group, rows, seq // group, width), bf16),
            sem_pair("tensor"),
            sem_pair("tensor"),
        ],
        number,
        part.astype(bf16),
    ).astype(f32)


def final_kernel(
    attn_ref, ffn_ref, grad_ref, part_ref, w_ref, attn_out, ffn_out, grad_out, all_ref, act_ref,
    attn_recv, ffn_recv, pair_recv, stage, grad_recv, recv_mod, own, part, terms, gathered,
    s0, s1, s2, s3, m0, m1, m2, m3
):
    group = lax.axis_size("tensor")
    count = lax.axis_size("dp")
    pairs = count // 2
    me, mine = lax.axis_index("dp"), lax.axis_index("tensor")
    chip, side = me // 2, lax.rem(me, 2)
    size = attn_ref.shape[1] // group
    greet(("dp", "tensor"))
    copies = start_exchange("tensor", lambda peer: part_ref.at[peer], recv_mod.at[mine], m0)
    recv_mod[mine] = part_ref[mine]
    pair_copy = pltpu.make_async_remote_copy(
        src_ref=grad_ref.at[:, 1 - side],
        dst_ref=pair_recv,
        send_sem=s0.at[0],
        recv_sem=s0.at[1],
        device_id={"dp": 2 * chip + 1 - side},
        device_id_type=MESH,
    )
    pair_copy.start()
    attn_copies = start_exchange(
        "tensor", lambda peer: token_block(attn_ref, peer, size), attn_recv.at[mine], s1
    )
    ffn_copies = start_exchange(
        "tensor", lambda peer: token_block(ffn_ref, peer, size), ffn_recv.at[mine], s2
    )
    wait_all(copies)
    own[...] = jnp.sum(recv_mod[...], axis=0).astype(bf16).astype(f32)
    copies = start_exchange("dp", lambda peer: own, all_ref.at[me], m1)
    all_ref[me] = own[...]
    wait_all(copies)

    @pl.loop(0, count)
    def _(at):
        part[at] = lax.dot_general(
            all_ref[at].astype(bf16),
            w_ref[...],
            (((1,), (1,)), ((), ())),
            preferred_element_type=f32,
        )

    copies = start_exchange("dp", lambda peer: part.at[peer], terms.at[me], m2)
    terms[me] = part[me]
    pair_copy.wait()
    grad_copies = []
    for step in range(pairs):
        to = lax.rem(chip + step, pairs) if step else chip
        total = grad_ref[to, side].astype(f32) + pair_recv[to].astype(f32)
        if step == 0:
            grad_out[...] = total
            continue
        stage[to] = total.astype(bf16)
        copy = pltpu.make_async_remote_copy(
            src_ref=stage.at[to],
            dst_ref=grad_recv.at[chip],
            send_sem=s3.at[0, step - 1],
            recv_sem=s3.at[1, step - 1],
            device_id={"dp": 2 * to + side},
            device_id_type=MESH,
        )
        copy.start()
        grad_copies.append(copy)
    wait_all(copies)
    last_copies = start_exchange("tensor", lambda peer: terms, gathered.at[mine], m3)
    gathered[mine] = terms[...]
    wait_all(grad_copies)
    for step in range(1, pairs):
        grad_out[...] += grad_recv[lax.rem(chip + step, pairs)].astype(f32)
    for copies, source, recv, out in (
        (attn_copies, attn_ref, attn_recv, attn_out),
        (ffn_copies, ffn_ref, ffn_recv, ffn_out),
    ):
        wait_all(copies)
        total = token_block(source, mine, size)[...].astype(f32)
        for step in range(1, group):
            total += recv[lax.rem(mine + step, group)].astype(f32)
        out[...] = total
    wait_all(last_copies)
    act_ref[...] = jnp.sum(gathered[...], axis=0)


def final_sums(attn_part, ffn_part, grads, parts, w_ada):
    group, count = lax.axis_size("tensor"), lax.axis_size("dp")
    rows, seq, width = attn_part.shape
    depth, columns = grads.shape
    shard_rows = depth // count
    tokens = (rows, seq // group, width)
    mod_columns = w_ada.shape[1]
    attn_own, ffn_own, grads, everyone, act = call(
        final_kernel,
        (
            jax.ShapeDtypeStruct(tokens, f32),
            jax.ShapeDtypeStruct(tokens, f32),
            jax.ShapeDtypeStruct((shard_rows, columns), f32),
            jax.ShapeDtypeStruct((count, rows, mod_columns), f32),
            jax.ShapeDtypeStruct((count, rows, shard_rows), f32),
        ),
        [
            pltpu.VMEM((group,) + tokens, bf16),
            pltpu.VMEM((group,) + tokens, bf16),
            pltpu.VMEM((count // 2, shard_rows, columns), bf16),
            pltpu.VMEM((count // 2, shard_rows, columns), bf16),
            pltpu.VMEM((count // 2, shard_rows, columns), bf16),
            pltpu.VMEM((group, rows, mod_columns), f32),
            pltpu.VMEM((rows, mod_columns), f32),
            pltpu.VMEM((count, rows, shard_rows), f32),
            pltpu.VMEM((count, rows, shard_rows), f32),
            pltpu.VMEM((group, count, rows, shard_rows), f32),
            pltpu.SemaphoreType.DMA((2,)),
            sem_pair("tensor"),
            sem_pair("tensor"),
            pltpu.SemaphoreType.DMA((2, count // 2 - 1)),
            sem_pair("tensor"),
            sem_pair("dp"),
            sem_pair("dp"),
            sem_pair("tensor"),
        ],
        5,
        attn_part.astype(bf16),
        ffn_part.astype(bf16),
        grads.astype(bf16).reshape(count // 2, 2, shard_rows, columns),
        parts.reshape(rows, group, mod_columns).transpose(1, 0, 2),
        w_ada,
    )
    everyone = everyone.reshape(count * rows, mod_columns).astype(bf16)
    d_act = act.transpose(1, 0, 2).reshape(rows, count * shard_rows)
    return attn_own, ffn_own, grads, everyone, d_act


def shards(latent_in, condition, w_ada, w_qkv, w_proj, w_up, w_down, out_grad):
    rows, own_tokens, width = latent_in.shape
    scale = HEAD_DIM ** (-0.5)
    tensor_at = lax.axis_index("tensor")
    local = w_proj.shape[0]
    heads = local // HEAD_DIM
    units = w_down.shape[0]

    attn_shard = jnp.concatenate(
        [w_qkv[0], w_qkv[1], w_qkv[2], w_proj.T], axis=1
    )
    ffn_shard = jnp.concatenate([w_up, w_down.T], axis=1)
    modulation, cond_mine, tokens, attn_weights = modulation_of(
        condition, w_ada, latent_in, attn_shard
    )
    modulation = modulation.reshape(rows, 6, 1, width)
    shift_a, scale_a, gate_a, shift_f, scale_f, gate_f = (modulation[:, i] for i in range(6))

    w_in = attn_weights[:, : 3 * local]
    proj_t = attn_weights[:, 3 * local :]
    cotangent = gather_tensor(out_grad, 1).astype(f32)
    tokens = tokens.astype(f32)
    seq = tokens.shape[1]

    normed_a, inverse_a = norm_parts(tokens)
    attn_in = (normed_a * (1.0 + scale_a) + shift_a).astype(bf16)
    projected = dot("lsd,de->lse", attn_in, w_in).astype(bf16)
    projected = projected.reshape(rows, seq, 3, heads, HEAD_DIM)
    queries, keys, values = projected[:, :, 0], projected[:, :, 1], projected[:, :, 2]
    scores = dot("lqhe,lkhe->lhqk", queries, keys) * scale
    shifted = jnp.exp(scores - jnp.max(scores, axis=-1, keepdims=True))
    probs = shifted / jnp.sum(shifted, axis=-1, keepdims=True)
    probs_low = probs.astype(bf16)
    mixed = dot("lhqk,lkhe->lqhe", probs_low, values).reshape(rows, seq, local).astype(bf16)
    attn_out, ffn_weights = reduce_and_gather(dot("lsd,ed->lse", mixed, proj_t), ffn_shard, 3)
    up = ffn_weights[:, :units]
    down_t = ffn_weights[:, units:]
    resid = tokens + gate_a * attn_out
    normed_f, inverse_f = norm_parts(resid)
    ffn_in = (normed_f * (1.0 + scale_f) + shift_f).astype(bf16)
    hidden_pre = dot("lsd,dn->lsn", ffn_in, up)
    hidden, gelu_pull = jax.vjp(gelu_tanh, hidden_pre)
    hidden = hidden.astype(bf16)
    d_ffn_out = (gate_f * cotangent).astype(bf16)
    d_hidden_pre = gelu_pull(dot("lse,en->lsn", d_ffn_out, down_t))[0].astype(bf16)
    d_ffn_in = reduce_tensor(dot("lsn,dn->lsd", d_hidden_pre, up), 4)

    ffn_part = dot("lsn,en->lse", hidden, down_t)
    d_gate_f = jnp.sum(cotangent * ffn_part, axis=1)
    d_shift_f = jnp.sum(d_ffn_in, axis=1)
    d_scale_f = jnp.sum(d_ffn_in * normed_f, axis=1)
    d_resid = cotangent + norm_back(normed_f, inverse_f, d_ffn_in * (1.0 + scale_f))
    d_gate_a = jnp.sum(d_resid * attn_out, axis=1)
    d_attn_out = (gate_a * d_resid).astype(bf16)
    d_mixed = dot("lse,ed->lsd", d_attn_out, proj_t).astype(bf16)
    d_mixed = d_mixed.reshape(rows, seq, heads, HEAD_DIM)
    d_probs = dot("lqhe,lkhe->lhqk", d_mixed, values)
    d_scores = probs * (d_probs - jnp.sum(d_probs * probs, axis=-1, keepdims=True))
    d_scores = d_scores.astype(bf16)
    d_values = dot("lhqk,lqhe->lkhe", probs_low, d_mixed)
    d_queries = dot("lhqk,lkhe->lqhe", d_scores, keys) * scale
    d_keys = dot("lhqk,lqhe->lkhe", d_scores, queries) * scale
    d_projected = jnp.stack([d_queries, d_keys, d_values], axis=2)
    d_projected = d_projected.reshape(rows, seq, 3 * local).astype(bf16)
    d_attn_part = dot("lse,de->lsd", d_projected, w_in)

    grads = jnp.concatenate(
        [
            dot("lsd,lse->de", attn_in, d_projected).astype(bf16),
            dot("lse,lsd->ed", d_attn_out, mixed).astype(bf16),
            dot("lsd,lsn->dn", ffn_in, d_hidden_pre).astype(bf16),
            dot("lse,lsn->en", d_ffn_out, hidden).astype(bf16),
        ],
        axis=1,
    )
    d_shift_a = jnp.sum(d_attn_part, axis=1)
    d_scale_a = jnp.sum(d_attn_part * normed_a, axis=1)
    ones = jnp.where(tensor_at == 0, 1.0, 0.0)
    d_modulation = jnp.concatenate(
        [d_shift_a, d_scale_a, d_gate_a * ones, d_shift_f * ones, d_scale_f * ones, d_gate_f],
        axis=1,
    )
    d_attn_own, ffn_own, grads, d_mod_all, d_act = final_sums(
        d_attn_part, ffn_part, grads, d_modulation, w_ada
    )
    grad_attn, grad_ffn = grads[:, : 4 * local], grads[:, 4 * local :]
    first = tensor_at * own_tokens
    own = lambda value: lax.dynamic_slice_in_dim(value, first, own_tokens, 1)
    latent_out = (own(resid) + gate_f * ffn_own).astype(bf16)
    grad_latent = own(d_resid) + norm_back(
        own(normed_a), own(inverse_a), d_attn_own * (1.0 + scale_a)
    )

    grad_ada = dot("ld,le->de", cond_mine, d_mod_all)
    grad_condition = jax.vjp(silu_value, condition.astype(f32))[1](d_act)[0]

    grad_qkv = jnp.stack([grad_attn[:, j * local : (j + 1) * local] for j in range(3)], axis=0)
    grad_proj = grad_attn[:, 3 * local :].T
    grad_up = grad_ffn[:, :units]
    grad_down = grad_ffn[:, units:].T
    return (
        latent_out,
        grad_latent,
        grad_condition,
        grad_ada,
        grad_qkv,
        grad_proj,
        grad_up,
        grad_down,
    )


def dot_plain(left, right):
    return lax.dot_general(left, right, (((1,), (0,)), ((), ())), preferred_element_type=f32)


def dot_right(left, right):
    return lax.dot_general(left, right, (((1,), (1,)), ((), ())), preferred_element_type=f32)


def dot_left(left, right):
    return lax.dot_general(left, right, (((0,), (0,)), ((), ())), preferred_element_type=f32)


def gelu_and_slope(values):
    root = math.sqrt(2.0 / math.pi)
    squares = values * values
    bent = jnp.tanh(root * values * (1.0 + 0.044715 * squares))
    half = 0.5 * (1.0 + bent)
    slope = half + 0.5 * values * (1.0 - bent * bent) * (root * (1.0 + 3.0 * 0.044715 * squares))
    return values * half, slope


def block_kernel(names, *refs):
    v = types.SimpleNamespace(**dict(zip(names, refs)))
    count = lax.axis_size("dp")
    pairs = count // 2
    d, z = lax.axis_index("dp"), lax.axis_index("tensor")
    p, c, h, l = d // 2, lax.rem(d, 2), z // 2, lax.rem(z, 2)
    t = 2 * c + l
    t_sib, t_near, t_cross = 2 * (1 - c) + l, 2 * c + 1 - l, 2 * (1 - c) + 1 - l
    diag = c == h
    off = c != h
    sib = (2 * p + 1 - c, z)
    near = (d, 2 * h + 1 - l)
    cross = (2 * p + 1 - c, 2 * h + 1 - l)
    swap = (2 * p + h, 2 * c + l)
    rows, own, width = v.x_ref.shape
    seq = v.x_all.shape[1]
    half = seq // 2
    shard = v.ada_ref.shape[0]
    columns = v.ada_ref.shape[1]
    local = v.mixed.shape[2]
    heads = local // HEAD_DIM
    chunks, _, wide = v.w_ffn.shape
    block = wide // 2
    scale = HEAD_DIM ** (-0.5)
    later = []

    def copy(source, target, sems, slot, to, there=None):
        return pltpu.make_async_remote_copy(
            src_ref=source,
            dst_ref=target,
            send_sem=sems.at[0, slot],
            recv_sem=sems.at[1, slot if there is None else there],
            device_id=to,
            device_id_type=MESH,
        )

    def send(*args, **kwargs):
        moved = copy(*args, **kwargs)
        moved.start()
        later.append(moved.wait_send)

    def send_if(condition, *args, **kwargs):
        moved = copy(*args, **kwargs)
        pl.when(condition)(moved.start)

        def finish():
            pl.when(condition)(moved.wait_send)

        later.append(finish)

    def came(target, sems, slot):
        copy(target, target, sems, slot, sib).wait_recv()

    def came_if(condition, target, sems, slot):
        pl.when(condition)(copy(target, target, sems, slot, sib).wait_recv)

    def tokens_of(ref, at, size=own):
        return ref.at[:, pl.ds(pl.multiple_of(at * size, size), size)]

    def rows_of(ref, at, size):
        return ref.at[pl.ds(pl.multiple_of(at * size, size), size)]

    barrier = pltpu.get_barrier_semaphore()
    here = 2 * d + h
    for step in range(1, 2 * count):
        other = lax.rem(here + step, 2 * count)
        pl.semaphore_signal(
            barrier,
            inc=1,
            device_id=(other // 2, 2 * lax.rem(other, 2) + l),
            device_id_type=MESH,
        )
    for side in range(2):
        for part in range(2):
            pl.semaphore_signal(
                barrier,
                inc=1,
                device_id=(2 * p + side, 2 * part + 1 - l),
                device_id_type=MESH,
            )

    cond = v.cond_ref[...].astype(f32)
    for at in range(count):
        v.cond_own[at] = cond[:, at * shard : (at + 1) * shard]
    for at in range(heads):
        v.a_shard[at] = jnp.concatenate(
            [v.qkv_ref[kind, :, at * HEAD_DIM : (at + 1) * HEAD_DIM] for kind in range(3)], axis=1
        )
    v.a_shard[heads] = v.proj_ref[...].T
    for at in range(chunks):
        v.f_shard[at, :, :block] = v.up_ref[:, at * block : (at + 1) * block]
        v.f_shard[at, :, block:] = v.down_ref[:, at * block : (at + 1) * block]
    pl.semaphore_wait(barrier, 2 * count - 1 + 4)

    def swap_in(ref, whole, sems):
        send_if(off, ref, tokens_of(whole, z), sems, 0, swap)

        @pl.when(diag)
        def _():
            tokens_of(whole, t)[...] = ref[...]

    def swap_came(whole, sems):
        came_if(off, tokens_of(whole, t), sems, 0)

    def spread_tokens(whole, sems, condition):
        mine = tokens_of(whole, t)
        send_if(condition, mine, mine, sems, 1, near)
        send_if(condition, mine, mine, sems, 0, sib)

    def forward_tokens(whole, sems):
        mine = tokens_of(whole, t_near)
        came(mine, sems, 1)
        send(mine, mine, sems, 2, sib)

    def tokens_came(whole, sems):
        came(tokens_of(whole, t_sib), sems, 0)
        came(tokens_of(whole, t_cross), sems, 2)

    def column_near(ref, whole, sems):
        mine = rows_of(whole, d, shard)
        send_if(off, ref, mine, sems, 0, sib, there=c)

        @pl.when(diag)
        def _():
            mine[...] = ref[...]

    def column_far(ref, whole, sems):
        send(ref, rows_of(whole, d, shard), sems, 1, (2 * p + h, 2 * (1 - h) + l), there=c)

    def column_on(whole, sems, plane, condition):
        for side in range(2):
            local_one = jnp.logical_and(diag, c == side)
            came_if(
                jnp.logical_and(condition, jnp.logical_not(local_one)),
                rows_of(whole, 2 * p + side, shard),
                sems,
                side,
            )
        mine = rows_of(whole, p, 2 * shard)
        for step in range(1, pairs):
            to = lax.rem(p + step, pairs)
            send_if(condition, mine, mine, plane, step - 1, (2 * to + c, z))

    def plane_came(whole, plane):
        for step in range(1, pairs):
            source = lax.rem(p + pairs - step, pairs)
            came(rows_of(whole, source, 2 * shard), plane, step - 1)

    def attn_on(at, condition):
        column_on(v.w_attn.at[at], v.s_acol.at[at], v.s_aplane.at[at], condition)

    def ffn_on(at, condition):
        column_on(v.w_ffn.at[at], v.s_fcol.at[at], v.s_fplane.at[at], condition)

    for step in range(1, count):
        peer = lax.rem(d + step, count)
        send(v.cond_own.at[peer], v.cond_buf.at[d], v.s_cond, step - 1, (peer, z))
    v.cond_buf[d] = v.cond_own[d]
    swap_in(v.x_ref, v.x_all, v.s_xswap)
    spread_tokens(v.x_all, v.s_x, diag)
    for at in range(heads + 1):
        column_near(v.a_shard.at[at], v.w_attn.at[at], v.s_acol.at[at])
    for at in range(heads + 1):
        column_far(v.a_shard.at[at], v.w_attn.at[at], v.s_acol.at[at])
    for at in range(heads + 1):
        attn_on(at, diag)
    for at in range(chunks):
        column_near(v.f_shard.at[at], v.w_ffn.at[at], v.s_fcol.at[at])

    for step in range(1, count):
        came(v.cond_buf.at[lax.rem(d + count - step, count)], v.s_cond, step - 1)
    for at in range(count):
        v.act_rows[rows * at : rows * (at + 1)] = v.cond_buf[at]
    act = silu_value(v.act_rows[...]).astype(bf16)
    v.act_rows[...] = act.astype(f32)
    v.mod_rows[...] = dot_plain(act, v.ada_ref[...])
    for at in range(count):
        v.mod_part[at] = v.mod_rows[rows * at : rows * (at + 1)]
    for at in range(count):
        to = (2 * (at // 2) + h, 2 * (at % 2) + l)
        mine = jnp.logical_and(d == to[0], z == to[1])
        send_if(jnp.logical_not(mine), v.mod_part.at[at], v.mod_recv.at[d], v.s_mod, at, to, there=d)

        @pl.when(mine)
        def _():
            v.mod_recv[d] = v.mod_part[at]

    swap_came(v.x_all, v.s_xswap)
    spread_tokens(v.x_all, v.s_x, off)
    for at in range(count):
        mine = jnp.logical_and(d == at, z == 2 * c + l)
        came_if(jnp.logical_not(mine), v.mod_recv.at[at], v.s_mod, at)
    v.mod_all[t] = jnp.sum(v.mod_recv[...], axis=0)
    group = ((sib, t_sib), (near, t_near), (cross, t_cross))
    for slot, (to, _) in enumerate(group):
        send(v.mod_all.at[t], v.mod_all.at[t], v.s_modall, slot, to)

    for at in range(heads + 1):
        attn_on(at, off)
    for at in range(chunks):
        column_far(v.f_shard.at[at], v.w_ffn.at[at], v.s_fcol.at[at])
    forward_tokens(v.x_all, v.s_x)
    ffn_on(0, diag)
    for slot, (_, at) in enumerate(group):
        came(v.mod_all.at[at], v.s_modall, slot)
    for row in range(rows):
        full = jnp.concatenate([v.mod_all[at][row : row + 1] for at in range(4)], axis=1)
        for at in range(6):
            v.modv[at, row] = full[:, at * width : (at + 1) * width]
    tokens_came(v.x_all, v.s_x)

    order = [lax.rem(1 - c + turn, 2) for turn in range(2)]

    for row in order:
        normed, inverse = norm_parts(v.x_all[row].astype(f32))
        v.normed_a[row] = normed
        v.inverse_a[row] = inverse
        v.attn_in[row] = (normed * (1.0 + v.modv[1, row]) + v.modv[0, row]).astype(bf16)

    def part_of(at, row, kind):
        return v.qkv[at, row, :, kind * HEAD_DIM : (kind + 1) * HEAD_DIM]

    def exchange_start(part, pair, sems):
        send(part.at[1 - c], pair, sems, 0, sib)

    def exchange_near(part, pair, both, other, sems):
        came(pair, sems, 0)
        both[...] = (part[c].astype(f32) + pair[...].astype(f32)).astype(bf16)
        send(both, other, sems, 1, near)

    def exchange_back(both, other, out, sems):
        came(other, sems, 1)
        out[c] = (both[...].astype(f32) + other[...].astype(f32)).astype(bf16)
        send(out.at[c], out.at[c], sems, 2, sib)

    swap_in(v.cot_ref, v.cot_all, v.s_cswap)
    for at in range(heads):
        plane_came(v.w_attn.at[at], v.s_aplane.at[at])
        for row in order:
            v.qkv[at, row] = dot_plain(v.attn_in[row], v.w_attn[at]).astype(bf16)
            scores = dot_right(part_of(at, row, 0), part_of(at, row, 1)) * scale
            shifted = jnp.exp(scores - jnp.max(scores, axis=-1, keepdims=True))
            probs = shifted / jnp.sum(shifted, axis=-1, keepdims=True)
            v.probs[row, at] = probs
            v.mixed[row, :, at * HEAD_DIM : (at + 1) * HEAD_DIM] = dot_plain(
                probs.astype(bf16), part_of(at, row, 2)
            ).astype(bf16)
        if at == 0:
            ffn_on(1, diag)
        if at == 1:
            ffn_on(0, off)
            ffn_on(2, diag)
    ffn_on(1, off)
    plane_came(v.w_attn.at[heads], v.s_aplane.at[heads])
    for turn, row in enumerate(order):
        v.a_part[row] = dot_right(v.mixed[row], v.w_attn[heads]).astype(bf16)
        if turn == 0:
            exchange_start(v.a_part, v.a_pair, v.s_a)
    exchange_near(v.a_part, v.a_pair, v.a_both, v.a_other, v.s_a)
    ffn_on(2, off)
    swap_came(v.cot_all, v.s_cswap)
    spread_tokens(v.cot_all, v.s_cot, count > 0)
    exchange_back(v.a_both, v.a_other, v.a_out, v.s_a)
    forward_tokens(v.cot_all, v.s_cot)

    for turn in (1, 0):
        row = order[turn]
        if turn == 0:
            came(v.a_out.at[1 - c], v.s_a, 2)
        resid = v.x_all[row].astype(f32) + v.modv[2, row] * v.a_out[row].astype(f32)
        v.resid[row] = resid
        normed, inverse = norm_parts(resid)
        v.normed_f[row] = normed
        v.inverse_f[row] = inverse
        v.ffn_in[row] = (normed * (1.0 + v.modv[4, row]) + v.modv[3, row]).astype(bf16)

    def whole(ref):
        return ref[...].reshape(rows * seq, ref.shape[-1])

    class Reduction:
        def __init__(self, grads, recv, total, low, home, plane, column):
            self.grads, self.recv, self.total, self.low = grads, recv, total, low
            self.home, self.plane, self.column = home, plane, column

        def start(self):
            for step in range(1, pairs):
                to = lax.rem(p + step, pairs)
                send(
                    rows_of(self.grads, to, 2 * shard),
                    self.recv.at[step - 1],
                    self.plane,
                    step - 1,
                    (2 * to + c, z),
                )

        def middle(self):
            total = rows_of(self.grads, p, 2 * shard)[...].astype(f32)
            for step in range(1, pairs):
                came(self.recv.at[step - 1], self.plane, step - 1)
                total += self.recv[step - 1].astype(f32)
            self.total[...] = total
            self.low[...] = total.astype(bf16)
            for side in range(2):
                send_if(
                    off,
                    self.low.at[pl.ds(side * shard, shard)],
                    self.home.at[1],
                    self.column,
                    side,
                    (2 * p + side, 2 * c + l),
                    there=1,
                )
            send_if(
                diag, rows_of(self.low, 1 - c, shard), self.home.at[0], self.column, 0, sib, there=0
            )

        def end(self):
            came(self.home.at[1], self.column, 1)
            came_if(off, self.home.at[0], self.column, 0)
            first = jnp.where(
                diag, rows_of(self.total, c, shard)[...], self.home[0].astype(f32)
            )
            return first + self.home[1].astype(f32)

    attn_sums = [
        Reduction(
            v.ga.at[at], v.ga_recv.at[at], v.ga_sum.at[at], v.ga_low.at[at], v.ga_home.at[at],
            v.s_ared.at[at], v.s_ahome.at[at],
        )
        for at in range(heads + 1)
    ]
    ffn_sums = [
        Reduction(
            v.gf.at[at], v.gf_recv.at[at], v.gf_sum.at[at], v.gf_low.at[at], v.gf_home.at[at],
            v.s_fred.at[at], v.s_fhome.at[at],
        )
        for at in range(chunks)
    ]

    def half_of(ref, at, size):
        return ref.at[pl.ds(pl.multiple_of(at * size, size), size)]

    def scatter_start(part, pair, sems, row):
        send(half_of(part.at[row], 1 - c, half), pair.at[row], sems, 2 * row, sib)

    def scatter_near(part, pair, kept, low, other, sems, row):
        came(pair.at[row], sems, 2 * row)
        kept[row] = half_of(part.at[row], c, half)[...].astype(f32) + pair[row].astype(f32)
        low[row] = half_of(kept.at[row], 1 - l, own)[...].astype(bf16)
        send(low.at[row], other.at[row], sems, 2 * row + 1, near)

    def scatter_end(kept, other, sems, row):
        came(other.at[row], sems, 2 * row + 1)
        return half_of(kept.at[row], l, own)[...] + other[row].astype(f32)

    def ffn_grads(at):
        v.gf[at, :, :block] = dot_left(whole(v.ffn_in), whole(v.d_hidden.at[at])).astype(bf16)
        v.gf[at, :, block:] = dot_left(whole(v.d_ffn_out), whole(v.hidden.at[at])).astype(bf16)
        ffn_sums[at].start()

    tokens_came(v.cot_all, v.s_cot)
    for row in order:
        v.d_ffn_out[row] = (v.modv[5, row] * v.cot_all[row].astype(f32)).astype(bf16)
    for at in range(chunks):
        plane_came(v.w_ffn.at[at], v.s_fplane.at[at])
        for row in order:
            hidden, slope = gelu_and_slope(dot_plain(v.ffn_in[row], v.w_ffn[at, :, :block]))
            v.hidden[at, row] = hidden.astype(bf16)
            v.d_hidden[at, row] = (
                dot_plain(v.d_ffn_out[row], v.w_ffn[at, :, block:]) * slope
            ).astype(bf16)
        if at < chunks - 1:
            ffn_grads(at)
    for turn, row in enumerate(order):
        total = dot_right(v.d_hidden[0, row], v.w_ffn[0, :, :block])
        for at in range(1, chunks):
            total += dot_right(v.d_hidden[at, row], v.w_ffn[at, :, :block])
        v.b_part[row] = total.astype(bf16)
        if turn == 0:
            exchange_start(v.b_part, v.b_pair, v.s_b)
    exchange_near(v.b_part, v.b_pair, v.b_both, v.b_other, v.s_b)

    ffn_grads(chunks - 1)
    for row in order:
        total = dot_right(v.hidden[0, row], v.w_ffn[0, :, block:])
        for at in range(1, chunks):
            total += dot_right(v.hidden[at, row], v.w_ffn[at, :, block:])
        v.dvec[5, row] = jnp.sum(v.cot_all[row].astype(f32) * total, axis=0, keepdims=True)
        v.f_part[row] = total.astype(bf16)
    for row in range(rows):
        scatter_start(v.f_part, v.f_pair, v.s_f, row)
    exchange_back(v.b_both, v.b_other, v.b_out, v.s_b)
    for row in range(rows):
        scatter_near(v.f_part, v.f_pair, v.f_kept, v.f_low, v.f_other, v.s_f, row)

    for turn in (1, 0):
        row = order[turn]
        if turn == 0:
            came(v.b_out.at[1 - c], v.s_b, 2)
        d_ffn_in = v.b_out[row].astype(f32)
        normed = v.normed_f[row]
        v.dvec[3, row] = jnp.sum(d_ffn_in, axis=0, keepdims=True)
        v.dvec[4, row] = jnp.sum(d_ffn_in * normed, axis=0, keepdims=True)
        d_resid = v.cot_all[row].astype(f32) + norm_back(
            normed, v.inverse_f[row], d_ffn_in * (1.0 + v.modv[4, row])
        )
        v.d_resid[row] = d_resid
        v.dvec[2, row] = jnp.sum(d_resid * v.a_out[row].astype(f32), axis=0, keepdims=True)
        v.d_attn_out[row] = (v.modv[2, row] * d_resid).astype(bf16)
        v.d_mixed[row] = dot_plain(v.d_attn_out[row], v.w_attn[heads]).astype(bf16)
    for at in range(heads):
        for row in order:
            d_mixed = v.d_mixed[row, :, at * HEAD_DIM : (at + 1) * HEAD_DIM]
            probs = v.probs[row, at]
            d_probs = dot_right(d_mixed, part_of(at, row, 2))
            d_scores = probs * (d_probs - jnp.sum(d_probs * probs, axis=-1, keepdims=True))
            d_scores = d_scores.astype(bf16)
            found = (
                dot_plain(d_scores, part_of(at, row, 1)) * scale,
                dot_left(d_scores, part_of(at, row, 0)) * scale,
                dot_left(probs.astype(bf16), d_mixed),
            )
            v.d_qkv[at, row] = jnp.concatenate(found, axis=1).astype(bf16)
        v.ga[at] = dot_left(whole(v.attn_in), whole(v.d_qkv.at[at])).astype(bf16)
        attn_sums[at].start()
        ffn_sums[at].middle()
        if at == 0:
            v.ga[heads] = dot_left(whole(v.d_attn_out), whole(v.mixed)).astype(bf16)
            attn_sums[heads].start()
            for row in range(rows):
                f_own = scatter_end(v.f_kept, v.f_other, v.s_f, row)
                v.latent_low[row] = (
                    half_of(v.resid.at[row], t, own)[...] + v.modv[5, row] * f_own
                ).astype(bf16)
            send_if(off, v.latent_low, v.latent_ref, v.s_lswap, 0, swap)

            @pl.when(diag)
            def _():
                v.latent_ref[...] = v.latent_low[...]

    for row in range(rows):
        d_attn_in = dot_right(v.d_qkv[0, row], v.w_attn[0])
        for at in range(1, heads):
            d_attn_in += dot_right(v.d_qkv[at, row], v.w_attn[at])
        v.e_part[row] = d_attn_in.astype(bf16)
        scatter_start(v.e_part, v.e_pair, v.s_e, row)
        v.dvec[0, row] = jnp.sum(d_attn_in, axis=0, keepdims=True)
        v.dvec[1, row] = jnp.sum(d_attn_in * v.normed_a[row], axis=0, keepdims=True)
        if row == 1:
            scatter_near(v.e_part, v.e_pair, v.e_kept, v.e_low, v.e_other, v.s_e, 0)
    first_one = jnp.where(t == 0, 1.0, 0.0)
    for row in range(rows):
        full = jnp.concatenate(
            [
                v.dvec[at, row] * first_one if at in (2, 3, 4) else v.dvec[at, row]
                for at in range(6)
            ],
            axis=1,
        )
        for at in range(4):
            v.dm_part[at, row : row + 1] = full[:, at * columns : (at + 1) * columns]
    for slot, (to, at) in enumerate(group):
        send(v.dm_part.at[at], v.dm_recv.at[t], v.s_dm, slot, to)
    v.dm_recv[t] = v.dm_part[t]
    scatter_near(v.e_part, v.e_pair, v.e_kept, v.e_low, v.e_other, v.s_e, 1)
    for slot, (_, at) in enumerate(group):
        came(v.dm_recv.at[at], v.s_dm, slot)
    v.dm_own[...] = jnp.sum(v.dm_recv[...], axis=0).astype(bf16).astype(f32)
    j = 2 * p + h
    for at in range(count):
        mine = jnp.logical_and(d == at, z == 2 * c + l)
        send_if(
            jnp.logical_not(mine), v.dm_own, v.dm_all.at[j], v.s_dmall, at, (at, 2 * c + l), there=j
        )

        @pl.when(mine)
        def _():
            v.dm_all[j] = v.dm_own[...]

    for row in range(rows):
        e_own = scatter_end(v.e_kept, v.e_other, v.s_e, row)
        v.grad_x_own[row] = half_of(v.d_resid.at[row], t, own)[...] + norm_back(
            half_of(v.normed_a.at[row], t, own)[...],
            half_of(v.inverse_a.at[row], t, own)[...],
            e_own * (1.0 + v.modv[1, row]),
        )
        v.grad_x_low[row] = v.grad_x_own[row].astype(bf16)
        send_if(off, v.grad_x_low.at[row], v.grad_x_recv.at[row], v.s_gswap, row, swap)

    @pl.when(diag)
    def _():
        v.grad_x_ref[...] = v.grad_x_own[...]

    for at in range(count):
        mine = jnp.logical_and(d == 2 * (at // 2) + h, z == 2 * (at % 2) + l)
        came_if(jnp.logical_not(mine), v.dm_all.at[at], v.s_dmall, at)
    for at in range(count):
        v.dm_rows[rows * at : rows * (at + 1)] = v.dm_all[at]
    everyone = v.dm_rows[...].astype(bf16)
    d_act = dot_right(everyone, v.ada_ref[...])
    for at in range(count):
        v.act_part[at] = d_act[rows * at : rows * (at + 1)]
    for step in range(1, count):
        peer = lax.rem(d + step, count)
        send(v.act_part.at[peer], v.terms.at[d], v.s_act, step - 1, (peer, z))
    v.terms[d] = v.act_part[d]
    v.grad_ada_ref[...] = dot_left(v.act_rows[...].astype(bf16), everyone)
    attn_sums[heads].middle()
    for step in range(1, count):
        came(v.terms.at[lax.rem(d + count - step, count)], v.s_act, step - 1)
    v.gathered[z] = v.terms[...]
    for step in range(1, 4):
        peer = lax.rem(z + step, 4)
        send(v.terms, v.gathered.at[z], v.s_gat, step - 1, (d, peer))
    for at in range(heads):
        attn_sums[at].middle()

    def ffn_end(at):
        total = ffn_sums[at].end()
        v.grad_up_ref[:, at * block : (at + 1) * block] = total[:, :block]
        v.grad_down_ref[:, at * block : (at + 1) * block] = total[:, block:]

    ffn_end(0)
    ffn_end(1)
    for step in range(1, 4):
        came(v.gathered.at[lax.rem(z + 4 - step, 4)], v.s_gat, step - 1)
    for at in range(count):
        here = slice(at * shard, (at + 1) * shard)
        values = v.cond_own[at]
        gate = 1.0 / (1.0 + jnp.exp(-values))
        v.grad_cond_ref[:, here] = jnp.sum(v.gathered[:, at], axis=0) * (
            gate * (1.0 + values * (1.0 - gate))
        )
    ffn_end(2)
    v.grad_proj_ref[...] = attn_sums[heads].end().T

    @pl.when(off)
    def _():
        came(v.latent_ref, v.s_lswap, 0)
        for row in range(rows):
            came(v.grad_x_recv.at[row], v.s_gswap, row)
            v.grad_x_ref[row] = v.grad_x_recv[row].astype(f32)

    for at in range(heads):
        total = attn_sums[at].end()
        for kind in range(3):
            v.grad_qkv_ref[kind, :, at * HEAD_DIM : (at + 1) * HEAD_DIM] = total[
                :, kind * HEAD_DIM : (kind + 1) * HEAD_DIM
            ]
    for finish in later:
        finish()


def fast_shards(latent_in, condition, w_ada, w_qkv, w_proj, w_up, w_down, out_grad):
    count = lax.axis_size("dp")
    pairs = count // 2
    rows, own, width = latent_in.shape
    seq = 4 * own
    shard, columns = w_ada.shape
    local = w_proj.shape[0]
    units = w_down.shape[0]
    heads = local // HEAD_DIM
    chunks = units // FF_BLOCK
    shape = jax.ShapeDtypeStruct
    inputs = dict(
        x_ref=latent_in, cond_ref=condition, ada_ref=w_ada, qkv_ref=w_qkv, proj_ref=w_proj,
        up_ref=w_up, down_ref=w_down.T, cot_ref=out_grad,
    )
    outs = dict(
        latent_ref=shape(latent_in.shape, bf16),
        grad_x_ref=shape(latent_in.shape, f32),
        grad_cond_ref=shape(condition.shape, f32),
        grad_ada_ref=shape(w_ada.shape, f32),
        grad_qkv_ref=shape(w_qkv.shape, f32),
        grad_proj_ref=shape(w_proj.shape, f32),
        grad_up_ref=shape(w_up.shape, f32),
        grad_down_ref=shape(w_down.shape[::-1], f32),
    )
    tokens = (rows, seq, width)
    half = (rows, seq // 2, width)
    mine = latent_in.shape
    low = dict(
        a_shard=(heads + 1, shard, local), f_shard=(chunks, shard, 2 * FF_BLOCK),
        x_all=tokens, cot_all=tokens, attn_in=tokens, ffn_in=tokens,
        d_ffn_out=tokens, d_attn_out=tokens,
        hidden=(chunks, rows, seq, FF_BLOCK), d_hidden=(chunks, rows, seq, FF_BLOCK),
        w_attn=(heads + 1, width, local), w_ffn=(chunks, width, 2 * FF_BLOCK),
        qkv=(heads, rows, seq, 3 * HEAD_DIM), d_qkv=(heads, rows, seq, 3 * HEAD_DIM),
        mixed=(rows, seq, local), d_mixed=(rows, seq, local),
        a_part=tokens, a_pair=(seq, width), a_both=(seq, width),
        a_other=(seq, width), a_out=tokens,
        b_part=tokens, b_pair=(seq, width), b_both=(seq, width),
        b_other=(seq, width), b_out=tokens,
        e_part=tokens, e_pair=half, e_low=mine, e_other=mine,
        f_part=tokens, f_pair=half, f_low=mine, f_other=mine,
        latent_low=mine, grad_x_low=mine, grad_x_recv=mine,
        ga=(heads + 1, width, local), ga_recv=(heads + 1, pairs - 1, 2 * shard, local),
        ga_low=(heads + 1, 2 * shard, local), ga_home=(heads + 1, 2, shard, local),
        gf=(chunks, width, 2 * FF_BLOCK), gf_recv=(chunks, pairs - 1, 2 * shard, 2 * FF_BLOCK),
        gf_low=(chunks, 2 * shard, 2 * FF_BLOCK), gf_home=(chunks, 2, shard, 2 * FF_BLOCK),
    )
    wide = dict(
        cond_own=(count, rows, shard), cond_buf=(count, rows, shard),
        act_rows=(count * rows, shard),
        mod_rows=(count * rows, columns), mod_part=(count, rows, columns),
        mod_recv=(count, rows, columns), mod_all=(4, rows, columns),
        modv=(6, rows, 1, width), dvec=(6, rows, 1, width),
        normed_a=tokens, inverse_a=(rows, seq, 1),
        resid=tokens, normed_f=tokens, inverse_f=(rows, seq, 1), d_resid=tokens,
        probs=(rows, heads, seq, seq), grad_x_own=mine,
        e_kept=half, f_kept=half,
        ga_sum=(heads + 1, 2 * shard, local), gf_sum=(chunks, 2 * shard, 2 * FF_BLOCK),
        dm_part=(4, rows, columns), dm_recv=(4, rows, columns), dm_own=(rows, columns),
        dm_all=(count, rows, columns), dm_rows=(count * rows, columns),
        act_part=(count, rows, shard), terms=(count, rows, shard),
        gathered=(4, count, rows, shard),
    )
    sems = dict(
        s_cond=(2, count - 1), s_mod=(2, count), s_modall=(2, 3), s_xswap=(2, 1),
        s_cswap=(2, 1), s_x=(2, 3), s_cot=(2, 3),
        s_acol=(heads + 1, 2, 2), s_fcol=(chunks, 2, 2),
        s_aplane=(heads + 1, 2, pairs - 1), s_fplane=(chunks, 2, pairs - 1),
        s_a=(2, 3), s_b=(2, 3), s_e=(2, 2 * rows), s_f=(2, 2 * rows),
        s_ared=(heads + 1, 2, pairs - 1), s_fred=(chunks, 2, pairs - 1),
        s_ahome=(heads + 1, 2, 2), s_fhome=(chunks, 2, 2),
        s_dm=(2, 3), s_dmall=(2, count), s_act=(2, count - 1), s_gat=(2, 3),
        s_lswap=(2, 1), s_gswap=(2, rows),
    )
    scratch = {name: pltpu.VMEM(size, bf16) for name, size in low.items()}
    scratch.update({name: pltpu.VMEM(size, f32) for name, size in wide.items()})
    scratch.update({name: pltpu.SemaphoreType.DMA(size) for name, size in sems.items()})
    names = tuple(inputs) + tuple(outs) + tuple(scratch)
    results = pl.pallas_call(
        functools.partial(block_kernel, names),
        out_shape=tuple(outs.values()),
        in_specs=[VMEM] * len(inputs),
        out_specs=tuple(VMEM for _ in outs),
        scratch_shapes=list(scratch.values()),
        compiler_params=pltpu.CompilerParams(
            collective_id=7, has_side_effects=True, vmem_limit_bytes=60 * 2**20
        ),
    )(*inputs.values())
    return results[:7] + (results[7].T,)


def can_pair(mesh):
    count, group = mesh.shape["dp"], mesh.shape["tensor"]
    return group == 4 and count % 2 == 0


def body(mesh):
    def run(*args):
        fits = (
            can_pair(mesh)
            and args[2].shape[0] % 16 == 0
            and args[0].shape[1] % 16 == 0
            and args[6].shape[0] % FF_BLOCK == 0
        )
        return (fast_shards if fits else shards)(*args)

    return run


def solution(mesh):
    return jax.shard_map(
        body(mesh),
        mesh=mesh,
        in_specs=(
            P("dp", "tensor", None),
            P("dp", None),
            P("dp", "tensor"),
            P(None, "dp", "tensor"),
            P("tensor", "dp"),
            P("dp", "tensor"),
            P("tensor", "dp"),
            P("dp", "tensor", None),
        ),
        out_specs=(
            P("dp", "tensor", None),
            P("dp", "tensor", None),
            P("dp", None),
            P("dp", "tensor"),
            P(None, "dp", "tensor"),
            P("tensor", "dp"),
            P("dp", "tensor"),
            P("tensor", "dp"),
        ),
        check_vma=False,
    )
```

```python
import functools
import math
import types

import jax
import jax.numpy as jnp
from jax import lax
from jax.experimental import pallas as pl
from jax.experimental.pallas import tpu as pltpu
from jax.sharding import PartitionSpec as P

MESH = pl.DeviceIdType.MESH
VMEM = pl.BlockSpec(memory_space=pltpu.VMEM)

HEAD_DIM = 64
FF_BLOCK = 256
EPS = 1e-06
f32 = jnp.float32
bf16 = jnp.bfloat16


def silu_value(values):
    return values / (1.0 + jnp.exp(-values))


def gelu_tanh(values):
    return (
        0.5
        * values
        * (
            1.0
            + jnp.tanh(math.sqrt(2.0 / math.pi) * (values + 0.044715 * values * values * values))
        )
    )


def norm_parts(values):
    centered = values - jnp.mean(values, axis=-1, keepdims=True)
    variance = jnp.mean(centered * centered, axis=-1, keepdims=True)
    inverse = lax.rsqrt(variance + EPS)
    return centered * inverse, inverse


def norm_back(normed, inverse, grad):
    return inverse * (
        grad
        - jnp.mean(grad, axis=-1, keepdims=True)
        - normed * jnp.mean(grad * normed, axis=-1, keepdims=True)
    )


def dot(form, left, right):
    return jnp.einsum(form, left, right, preferred_element_type=f32)


def gather_tensor(block, axis):
    return lax.all_gather(block, "tensor", axis=axis, tiled=True)


def greet(axes):
    barrier = pltpu.get_barrier_semaphore()
    total = 0
    for axis in axes:
        size = lax.axis_size(axis)
        me = lax.axis_index(axis)
        for step in range(1, size):
            pl.semaphore_signal(
                barrier, inc=1, device_id={axis: lax.rem(me + step, size)}, device_id_type=MESH
            )
        total += size - 1
    pl.semaphore_wait(barrier, total)


def start_exchange(axis, source, target, sems):
    size = lax.axis_size(axis)
    me = lax.axis_index(axis)
    copies = []
    for step in range(1, size):
        peer = lax.rem(me + step, size)
        copy = pltpu.make_async_remote_copy(
            src_ref=source(peer),
            dst_ref=target,
            send_sem=sems.at[0, step - 1],
            recv_sem=sems.at[1, step - 1],
            device_id={axis: peer},
            device_id_type=MESH,
        )
        copy.start()
        copies.append(copy)
    return copies


def wait_all(copies):
    for copy in copies:
        copy.wait()


def exchange(axis, source, target, sems):
    wait_all(start_exchange(axis, source, target, sems))


def sem_pair(axis):
    return pltpu.SemaphoreType.DMA((2, lax.axis_size(axis) - 1))


def call(kernel, outs, scratch, number, *args):
    return pl.pallas_call(
        kernel,
        out_shape=outs,
        in_specs=[VMEM] * len(args),
        out_specs=jax.tree.map(lambda _: VMEM, outs),
        scratch_shapes=scratch,
        compiler_params=pltpu.CompilerParams(
            collective_id=number, has_side_effects=True, vmem_limit_bytes=48 * 2**20
        ),
    )(*args)


def modulation_kernel(
    cond_ref, w_ref, x_ref, shard_ref, mod_ref, act_ref, x_all, w_all,
    cond_buf, part, recv, own, s0, s1, s2, s3, s4, s5
):
    count = lax.axis_size("dp")
    me, mine = lax.axis_index("dp"), lax.axis_index("tensor")
    greet(("dp", "tensor"))
    copies = start_exchange("dp", lambda peer: cond_ref.at[peer], cond_buf.at[me], s0)
    x_own = token_block(x_all, mine, x_ref.shape[1])
    x_copies = start_exchange("tensor", lambda peer: x_ref, x_own, s3)
    cond_buf[me] = cond_ref[me]
    x_own[...] = x_ref[...]
    w_all[me] = shard_ref[...]
    wait_all(copies)

    @pl.loop(0, count)
    def _(at):
        act = silu_value(cond_buf[at]).astype(bf16)
        act_ref[at] = act.astype(f32)
        part[at] = jnp.dot(act, w_ref[...], preferred_element_type=f32)

    copies = start_exchange("dp", lambda peer: part.at[peer], recv.at[me], s1)
    recv[me] = part[me]
    pairs = count // 2
    chip, side = me // 2, lax.rem(me, 2)
    sibling = 2 * chip + 1 - side

    def send(source, at, to, sems, number):
        copy = pltpu.make_async_remote_copy(
            src_ref=source,
            dst_ref=w_all.at[at],
            send_sem=sems.at[0, number],
            recv_sem=sems.at[1, number],
            device_id={"dp": to},
            device_id_type=MESH,
        )
        copy.start()
        return copy

    far = [
        send(shard_ref, me, 2 * lax.rem(chip + step, pairs) + side, s4, step)
        for step in range(1, pairs)
    ]
    near = [send(shard_ref, me, sibling, s5, 0)]
    wait_all(copies)
    own[...] = jnp.sum(recv[...], axis=0)
    copies = start_exchange("tensor", lambda peer: own, mod_ref.at[mine], s2)
    mod_ref[mine] = own[...]
    for step in range(1, pairs):
        far[step - 1].wait()
        came = 2 * lax.rem(chip + pairs - step, pairs) + side
        near.append(send(w_all.at[came], came, sibling, s5, step))
    wait_all(near)
    wait_all(copies)
    wait_all(x_copies)


def modulation_of(condition, w_ada, block, shard):
    count, group = lax.axis_size("dp"), lax.axis_size("tensor")
    rows, width = condition.shape
    shard_rows, columns = w_ada.shape
    blocks = condition.astype(f32).reshape(rows, count, shard_rows).transpose(1, 0, 2)
    mod, act, x_all, w_all = call(
        modulation_kernel,
        (
            jax.ShapeDtypeStruct((group, rows, columns), f32),
            jax.ShapeDtypeStruct((count, rows, shard_rows), f32),
            jax.ShapeDtypeStruct((rows, group * block.shape[1], width), bf16),
            jax.ShapeDtypeStruct((count,) + shard.shape, bf16),
        ),
        [
            pltpu.VMEM((count, rows, shard_rows), f32),
            pltpu.VMEM((count, rows, columns), f32),
            pltpu.VMEM((count, rows, columns), f32),
            pltpu.VMEM((rows, columns), f32),
            sem_pair("dp"),
            sem_pair("dp"),
            sem_pair("tensor"),
            sem_pair("tensor"),
            pltpu.SemaphoreType.DMA((2, count // 2)),
            pltpu.SemaphoreType.DMA((2, count // 2)),
        ],
        1,
        blocks,
        w_ada,
        block,
        shard,
    )
    mod = mod.transpose(1, 0, 2).reshape(rows, group * columns)
    act = act.reshape(count * rows, shard_rows).astype(bf16)
    return mod, act, x_all, w_all.reshape(count * shard.shape[0], shard.shape[1])


def token_block(ref, at, size):
    return ref.at[:, pl.ds(pl.multiple_of(at * size, size), size)]


def finish_reduce(part_ref, out_ref, recv, first, sems):
    group = lax.axis_size("tensor")
    mine = lax.axis_index("tensor")
    size = part_ref.shape[1] // group
    wait_all(first)
    total = token_block(part_ref, mine, size)[...].astype(f32)
    for step in range(1, group):
        total += recv[lax.rem(mine + step, group)].astype(f32)
    own = token_block(out_ref, mine, size)
    own[...] = total.astype(bf16)
    return start_exchange("tensor", lambda peer: own, own, sems)


def start_reduce(part_ref, recv, sems):
    group = lax.axis_size("tensor")
    size = part_ref.shape[1] // group
    return start_exchange(
        "tensor",
        lambda peer: token_block(part_ref, peer, size),
        recv.at[lax.axis_index("tensor")],
        sems,
    )


def reduce_kernel(part_ref, out_ref, recv, s0, s1):
    greet(("tensor",))
    first = start_reduce(part_ref, recv, s0)
    wait_all(finish_reduce(part_ref, out_ref, recv, first, s1))


def reduce_gather_kernel(part_ref, shard_ref, out_ref, w_all, recv, s0, s1, s2, s3):
    count = lax.axis_size("dp")
    me = lax.axis_index("dp")
    pairs = count // 2
    chip, side = me // 2, lax.rem(me, 2)
    sibling = 2 * chip + 1 - side
    greet(("dp", "tensor"))

    def send(source, at, to, sems, number):
        copy = pltpu.make_async_remote_copy(
            src_ref=source,
            dst_ref=w_all.at[at],
            send_sem=sems.at[0, number],
            recv_sem=sems.at[1, number],
            device_id={"dp": to},
            device_id_type=MESH,
        )
        copy.start()
        return copy

    first = start_reduce(part_ref, recv, s0)
    far = [
        send(shard_ref, me, 2 * lax.rem(chip + step, pairs) + side, s2, step)
        for step in range(1, pairs)
    ]
    near = [send(shard_ref, me, sibling, s3, 0)]
    w_all[me] = shard_ref[...]
    last = finish_reduce(part_ref, out_ref, recv, first, s1)
    for step in range(1, pairs):
        far[step - 1].wait()
        came = 2 * lax.rem(chip + pairs - step, pairs) + side
        near.append(send(w_all.at[came], came, sibling, s3, step))
    wait_all(near)
    wait_all(last)


def reduce_and_gather(part, shard, number):
    group, count = lax.axis_size("tensor"), lax.axis_size("dp")
    rows, seq, width = part.shape
    total, weights = call(
        reduce_gather_kernel,
        (
            jax.ShapeDtypeStruct(part.shape, bf16),
            jax.ShapeDtypeStruct((count,) + shard.shape, bf16),
        ),
        [
            pltpu.VMEM((group, rows, seq // group, width), bf16),
            sem_pair("tensor"),
            sem_pair("tensor"),
            pltpu.SemaphoreType.DMA((2, count // 2)),
            pltpu.SemaphoreType.DMA((2, count // 2)),
        ],
        number,
        part.astype(bf16),
        shard,
    )
    return total.astype(f32), weights.reshape(count * shard.shape[0], shard.shape[1])


def reduce_tensor(part, number):
    group = lax.axis_size("tensor")
    rows, seq, width = part.shape
    return call(
        reduce_kernel,
        jax.ShapeDtypeStruct(part.shape, bf16),
        [
            pltpu.VMEM((group, rows, seq // group, width), bf16),
            sem_pair("tensor"),
            sem_pair("tensor"),
        ],
        number,
        part.astype(bf16),
    ).astype(f32)


def final_kernel(
    attn_ref, ffn_ref, grad_ref, part_ref, w_ref, attn_out, ffn_out, grad_out, all_ref, act_ref,
    attn_recv, ffn_recv, pair_recv, stage, grad_recv, recv_mod, own, part, terms, gathered,
    s0, s1, s2, s3, m0, m1, m2, m3
):
    group = lax.axis_size("tensor")
    count = lax.axis_size("dp")
    pairs = count // 2
    me, mine = lax.axis_index("dp"), lax.axis_index("tensor")
    chip, side = me // 2, lax.rem(me, 2)
    size = attn_ref.shape[1] // group
    greet(("dp", "tensor"))
    copies = start_exchange("tensor", lambda peer: part_ref.at[peer], recv_mod.at[mine], m0)
    recv_mod[mine] = part_ref[mine]
    pair_copy = pltpu.make_async_remote_copy(
        src_ref=grad_ref.at[:, 1 - side],
        dst_ref=pair_recv,
        send_sem=s0.at[0],
        recv_sem=s0.at[1],
        device_id={"dp": 2 * chip + 1 - side},
        device_id_type=MESH,
    )
    pair_copy.start()
    attn_copies = start_exchange(
        "tensor", lambda peer: token_block(attn_ref, peer, size), attn_recv.at[mine], s1
    )
    ffn_copies = start_exchange(
        "tensor", lambda peer: token_block(ffn_ref, peer, size), ffn_recv.at[mine], s2
    )
    wait_all(copies)
    own[...] = jnp.sum(recv_mod[...], axis=0).astype(bf16).astype(f32)
    copies = start_exchange("dp", lambda peer: own, all_ref.at[me], m1)
    all_ref[me] = own[...]
    wait_all(copies)

    @pl.loop(0, count)
    def _(at):
        part[at] = lax.dot_general(
            all_ref[at].astype(bf16),
            w_ref[...],
            (((1,), (1,)), ((), ())),
            preferred_element_type=f32,
        )

    copies = start_exchange("dp", lambda peer: part.at[peer], terms.at[me], m2)
    terms[me] = part[me]
    pair_copy.wait()
    grad_copies = []
    for step in range(pairs):
        to = lax.rem(chip + step, pairs) if step else chip
        total = grad_ref[to, side].astype(f32) + pair_recv[to].astype(f32)
        if step == 0:
            grad_out[...] = total
            continue
        stage[to] = total.astype(bf16)
        copy = pltpu.make_async_remote_copy(
            src_ref=stage.at[to],
            dst_ref=grad_recv.at[chip],
            send_sem=s3.at[0, step - 1],
            recv_sem=s3.at[1, step - 1],
            device_id={"dp": 2 * to + side},
            device_id_type=MESH,
        )
        copy.start()
        grad_copies.append(copy)
    wait_all(copies)
    last_copies = start_exchange("tensor", lambda peer: terms, gathered.at[mine], m3)
    gathered[mine] = terms[...]
    wait_all(grad_copies)
    for step in range(1, pairs):
        grad_out[...] += grad_recv[lax.rem(chip + step, pairs)].astype(f32)
    for copies, source, recv, out in (
        (attn_copies, attn_ref, attn_recv, attn_out),
        (ffn_copies, ffn_ref, ffn_recv, ffn_out),
    ):
        wait_all(copies)
        total = token_block(source, mine, size)[...].astype(f32)
        for step in range(1, group):
            total += recv[lax.rem(mine + step, group)].astype(f32)
        out[...] = total
    wait_all(last_copies)
    act_ref[...] = jnp.sum(gathered[...], axis=0)


def final_sums(attn_part, ffn_part, grads, parts, w_ada):
    group, count = lax.axis_size("tensor"), lax.axis_size("dp")
    rows, seq, width = attn_part.shape
    depth, columns = grads.shape
    shard_rows = depth // count
    tokens = (rows, seq // group, width)
    mod_columns = w_ada.shape[1]
    attn_own, ffn_own, grads, everyone, act = call(
        final_kernel,
        (
            jax.ShapeDtypeStruct(tokens, f32),
            jax.ShapeDtypeStruct(tokens, f32),
            jax.ShapeDtypeStruct((shard_rows, columns), f32),
            jax.ShapeDtypeStruct((count, rows, mod_columns), f32),
            jax.ShapeDtypeStruct((count, rows, shard_rows), f32),
        ),
        [
            pltpu.VMEM((group,) + tokens, bf16),
            pltpu.VMEM((group,) + tokens, bf16),
            pltpu.VMEM((count // 2, shard_rows, columns), bf16),
            pltpu.VMEM((count // 2, shard_rows, columns), bf16),
            pltpu.VMEM((count // 2, shard_rows, columns), bf16),
            pltpu.VMEM((group, rows, mod_columns), f32),
            pltpu.VMEM((rows, mod_columns), f32),
            pltpu.VMEM((count, rows, shard_rows), f32),
            pltpu.VMEM((count, rows, shard_rows), f32),
            pltpu.VMEM((group, count, rows, shard_rows), f32),
            pltpu.SemaphoreType.DMA((2,)),
            sem_pair("tensor"),
            sem_pair("tensor"),
            pltpu.SemaphoreType.DMA((2, count // 2 - 1)),
            sem_pair("tensor"),
            sem_pair("dp"),
            sem_pair("dp"),
            sem_pair("tensor"),
        ],
        5,
        attn_part.astype(bf16),
        ffn_part.astype(bf16),
        grads.astype(bf16).reshape(count // 2, 2, shard_rows, columns),
        parts.reshape(rows, group, mod_columns).transpose(1, 0, 2),
        w_ada,
    )
    everyone = everyone.reshape(count * rows, mod_columns).astype(bf16)
    d_act = act.transpose(1, 0, 2).reshape(rows, count * shard_rows)
    return attn_own, ffn_own, grads, everyone, d_act


def shards(latent_in, condition, w_ada, w_qkv, w_proj, w_up, w_down, out_grad):
    rows, own_tokens, width = latent_in.shape
    scale = HEAD_DIM ** (-0.5)
    tensor_at = lax.axis_index("tensor")
    local = w_proj.shape[0]
    heads = local // HEAD_DIM
    units = w_down.shape[0]

    attn_shard = jnp.concatenate(
        [w_qkv[0], w_qkv[1], w_qkv[2], w_proj.T], axis=1
    )
    ffn_shard = jnp.concatenate([w_up, w_down.T], axis=1)
    modulation, cond_mine, tokens, attn_weights = modulation_of(
        condition, w_ada, latent_in, attn_shard
    )
    modulation = modulation.reshape(rows, 6, 1, width)
    shift_a, scale_a, gate_a, shift_f, scale_f, gate_f = (modulation[:, i] for i in range(6))

    w_in = attn_weights[:, : 3 * local]
    proj_t = attn_weights[:, 3 * local :]
    cotangent = gather_tensor(out_grad, 1).astype(f32)
    tokens = tokens.astype(f32)
    seq = tokens.shape[1]

    normed_a, inverse_a = norm_parts(tokens)
    attn_in = (normed_a * (1.0 + scale_a) + shift_a).astype(bf16)
    projected = dot("lsd,de->lse", attn_in, w_in).astype(bf16)
    projected = projected.reshape(rows, seq, 3, heads, HEAD_DIM)
    queries, keys, values = projected[:, :, 0], projected[:, :, 1], projected[:, :, 2]
    scores = dot("lqhe,lkhe->lhqk", queries, keys) * scale
    shifted = jnp.exp(scores - jnp.max(scores, axis=-1, keepdims=True))
    probs = shifted / jnp.sum(shifted, axis=-1, keepdims=True)
    probs_low = probs.astype(bf16)
    mixed = dot("lhqk,lkhe->lqhe", probs_low, values).reshape(rows, seq, local).astype(bf16)
    attn_out, ffn_weights = reduce_and_gather(dot("lsd,ed->lse", mixed, proj_t), ffn_shard, 3)
    up = ffn_weights[:, :units]
    down_t = ffn_weights[:, units:]
    resid = tokens + gate_a * attn_out
    normed_f, inverse_f = norm_parts(resid)
    ffn_in = (normed_f * (1.0 + scale_f) + shift_f).astype(bf16)
    hidden_pre = dot("lsd,dn->lsn", ffn_in, up)
    hidden, gelu_pull = jax.vjp(gelu_tanh, hidden_pre)
    hidden = hidden.astype(bf16)
    d_ffn_out = (gate_f * cotangent).astype(bf16)
    d_hidden_pre = gelu_pull(dot("lse,en->lsn", d_ffn_out, down_t))[0].astype(bf16)
    d_ffn_in = reduce_tensor(dot("lsn,dn->lsd", d_hidden_pre, up), 4)

    ffn_part = dot("lsn,en->lse", hidden, down_t)
    d_gate_f = jnp.sum(cotangent * ffn_part, axis=1)
    d_shift_f = jnp.sum(d_ffn_in, axis=1)
    d_scale_f = jnp.sum(d_ffn_in * normed_f, axis=1)
    d_resid = cotangent + norm_back(normed_f, inverse_f, d_ffn_in * (1.0 + scale_f))
    d_gate_a = jnp.sum(d_resid * attn_out, axis=1)
    d_attn_out = (gate_a * d_resid).astype(bf16)
    d_mixed = dot("lse,ed->lsd", d_attn_out, proj_t).astype(bf16)
    d_mixed = d_mixed.reshape(rows, seq, heads, HEAD_DIM)
    d_probs = dot("lqhe,lkhe->lhqk", d_mixed, values)
    d_scores = probs * (d_probs - jnp.sum(d_probs * probs, axis=-1, keepdims=True))
    d_scores = d_scores.astype(bf16)
    d_values = dot("lhqk,lqhe->lkhe", probs_low, d_mixed)
    d_queries = dot("lhqk,lkhe->lqhe", d_scores, keys) * scale
    d_keys = dot("lhqk,lqhe->lkhe", d_scores, queries) * scale
    d_projected = jnp.stack([d_queries, d_keys, d_values], axis=2)
    d_projected = d_projected.reshape(rows, seq, 3 * local).astype(bf16)
    d_attn_part = dot("lse,de->lsd", d_projected, w_in)

    grads = jnp.concatenate(
        [
            dot("lsd,lse->de", attn_in, d_projected).astype(bf16),
            dot("lse,lsd->ed", d_attn_out, mixed).astype(bf16),
            dot("lsd,lsn->dn", ffn_in, d_hidden_pre).astype(bf16),
            dot("lse,lsn->en", d_ffn_out, hidden).astype(bf16),
        ],
        axis=1,
    )
    d_shift_a = jnp.sum(d_attn_part, axis=1)
    d_scale_a = jnp.sum(d_attn_part * normed_a, axis=1)
    ones = jnp.where(tensor_at == 0, 1.0, 0.0)
    d_modulation = jnp.concatenate(
        [d_shift_a, d_scale_a, d_gate_a * ones, d_shift_f * ones, d_scale_f * ones, d_gate_f],
        axis=1,
    )
    d_attn_own, ffn_own, grads, d_mod_all, d_act = final_sums(
        d_attn_part, ffn_part, grads, d_modulation, w_ada
    )
    grad_attn, grad_ffn = grads[:, : 4 * local], grads[:, 4 * local :]
    first = tensor_at * own_tokens
    own = lambda value: lax.dynamic_slice_in_dim(value, first, own_tokens, 1)
    latent_out = (own(resid) + gate_f * ffn_own).astype(bf16)
    grad_latent = own(d_resid) + norm_back(
        own(normed_a), own(inverse_a), d_attn_own * (1.0 + scale_a)
    )

    grad_ada = dot("ld,le->de", cond_mine, d_mod_all)
    grad_condition = jax.vjp(silu_value, condition.astype(f32))[1](d_act)[0]

    grad_qkv = jnp.stack([grad_attn[:, j * local : (j + 1) * local] for j in range(3)], axis=0)
    grad_proj = grad_attn[:, 3 * local :].T
    grad_up = grad_ffn[:, :units]
    grad_down = grad_ffn[:, units:].T
    return (
        latent_out,
        grad_latent,
        grad_condition,
        grad_ada,
        grad_qkv,
        grad_proj,
        grad_up,
        grad_down,
    )


def dot_plain(left, right):
    return lax.dot_general(left, right, (((1,), (0,)), ((), ())), preferred_element_type=f32)


def dot_right(left, right):
    return lax.dot_general(left, right, (((1,), (1,)), ((), ())), preferred_element_type=f32)


def dot_left(left, right):
    return lax.dot_general(left, right, (((0,), (0,)), ((), ())), preferred_element_type=f32)


def gelu_and_slope(values):
    root = math.sqrt(2.0 / math.pi)
    squares = values * values
    bent = jnp.tanh(root * values * (1.0 + 0.044715 * squares))
    half = 0.5 * (1.0 + bent)
    slope = half + 0.5 * values * (1.0 - bent * bent) * (root * (1.0 + 3.0 * 0.044715 * squares))
    return values * half, slope


def block_kernel(names, *refs):
    v = types.SimpleNamespace(**dict(zip(names, refs)))
    count = lax.axis_size("dp")
    pairs = count // 2
    d, z = lax.axis_index("dp"), lax.axis_index("tensor")
    p, c, h, l = d // 2, lax.rem(d, 2), z // 2, lax.rem(z, 2)
    t = 2 * c + l
    t_sib, t_near, t_cross = 2 * (1 - c) + l, 2 * c + 1 - l, 2 * (1 - c) + 1 - l
    diag = c == h
    off = c != h
    sib = (2 * p + 1 - c, z)
    near = (d, 2 * h + 1 - l)
    cross = (2 * p + 1 - c, 2 * h + 1 - l)
    swap = (2 * p + h, 2 * c + l)
    rows, own, width = v.x_ref.shape
    seq = v.x_all.shape[1]
    half = seq // 2
    shard = v.ada_ref.shape[0]
    columns = v.ada_ref.shape[1]
    local = v.mixed.shape[2]
    heads = local // HEAD_DIM
    chunks, _, wide = v.w_ffn.shape
    block = wide // 2
    scale = HEAD_DIM ** (-0.5)
    later = []

    def copy(source, target, sems, slot, to, there=None):
        return pltpu.make_async_remote_copy(
            src_ref=source,
            dst_ref=target,
            send_sem=sems.at[0, slot],
            recv_sem=sems.at[1, slot if there is None else there],
            device_id=to,
            device_id_type=MESH,
        )

    def send(*args, **kwargs):
        moved = copy(*args, **kwargs)
        moved.start()
        later.append(moved.wait_send)

    def send_if(condition, *args, **kwargs):
        moved = copy(*args, **kwargs)
        pl.when(condition)(moved.start)

        def finish():
            pl.when(condition)(moved.wait_send)

        later.append(finish)

    def came(target, sems, slot):
        copy(target, target, sems, slot, sib).wait_recv()

    def came_if(condition, target, sems, slot):
        pl.when(condition)(copy(target, target, sems, slot, sib).wait_recv)

    def tokens_of(ref, at, size=own):
        return ref.at[:, pl.ds(pl.multiple_of(at * size, size), size)]

    def rows_of(ref, at, size):
        return ref.at[pl.ds(pl.multiple_of(at * size, size), size)]

    barrier = pltpu.get_barrier_semaphore()
    here = 2 * d + h
    for step in range(1, 2 * count):
        other = lax.rem(here + step, 2 * count)
        pl.semaphore_signal(
            barrier,
            inc=1,
            device_id=(other // 2, 2 * lax.rem(other, 2) + l),
            device_id_type=MESH,
        )
    for side in range(2):
        for part in range(2):
            pl.semaphore_signal(
                barrier,
                inc=1,
                device_id=(2 * p + side, 2 * part + 1 - l),
                device_id_type=MESH,
            )

    cond = v.cond_ref[...].astype(f32)
    for at in range(count):
        v.cond_own[at] = cond[:, at * shard : (at + 1) * shard]
    for at in range(heads):
        v.a_shard[at] = jnp.concatenate(
            [v.qkv_ref[kind, :, at * HEAD_DIM : (at + 1) * HEAD_DIM] for kind in range(3)], axis=1
        )
    v.a_shard[heads] = v.proj_ref[...].T
    for at in range(chunks):
        v.f_shard[at, :, :block] = v.up_ref[:, at * block : (at + 1) * block]
        v.f_shard[at, :, block:] = v.down_ref[:, at * block : (at + 1) * block]
    pl.semaphore_wait(barrier, 2 * count - 1 + 4)

    def swap_in(ref, whole, sems):
        send_if(off, ref, tokens_of(whole, z), sems, 0, swap)

        @pl.when(diag)
        def _():
            tokens_of(whole, t)[...] = ref[...]

    def swap_came(whole, sems):
        came_if(off, tokens_of(whole, t), sems, 0)

    def spread_tokens(whole, sems, condition):
        mine = tokens_of(whole, t)
        send_if(condition, mine, mine, sems, 1, near)
        send_if(condition, mine, mine, sems, 0, sib)

    def forward_tokens(whole, sems):
        mine = tokens_of(whole, t_near)
        came(mine, sems, 1)
        send(mine, mine, sems, 2, sib)

    def tokens_came(whole, sems):
        came(tokens_of(whole, t_sib), sems, 0)
        came(tokens_of(whole, t_cross), sems, 2)

    def column_near(ref, whole, sems):
        mine = rows_of(whole, d, shard)
        send_if(off, ref, mine, sems, 0, sib, there=c)

        @pl.when(diag)
        def _():
            mine[...] = ref[...]

    def column_far(ref, whole, sems):
        send(ref, rows_of(whole, d, shard), sems, 1, (2 * p + h, 2 * (1 - h) + l), there=c)

    def column_on(whole, sems, plane, condition):
        for side in range(2):
            local_one = jnp.logical_and(diag, c == side)
            came_if(
                jnp.logical_and(condition, jnp.logical_not(local_one)),
                rows_of(whole, 2 * p + side, shard),
                sems,
                side,
            )
        mine = rows_of(whole, p, 2 * shard)
        for step in range(1, pairs):
            to = lax.rem(p + step, pairs)
            send_if(condition, mine, mine, plane, step - 1, (2 * to + c, z))

    def plane_came(whole, plane):
        for step in range(1, pairs):
            source = lax.rem(p + pairs - step, pairs)
            came(rows_of(whole, source, 2 * shard), plane, step - 1)

    def attn_on(at, condition):
        column_on(v.w_attn.at[at], v.s_acol.at[at], v.s_aplane.at[at], condition)

    def ffn_on(at, condition):
        column_on(v.w_ffn.at[at], v.s_fcol.at[at], v.s_fplane.at[at], condition)

    for step in range(1, count):
        peer = lax.rem(d + step, count)
        send(v.cond_own.at[peer], v.cond_buf.at[d], v.s_cond, step - 1, (peer, z))
    v.cond_buf[d] = v.cond_own[d]
    swap_in(v.x_ref, v.x_all, v.s_xswap)
    spread_tokens(v.x_all, v.s_x, diag)
    for at in range(heads + 1):
        column_near(v.a_shard.at[at], v.w_attn.at[at], v.s_acol.at[at])
    for at in range(heads + 1):
        column_far(v.a_shard.at[at], v.w_attn.at[at], v.s_acol.at[at])
    for at in range(heads + 1):
        attn_on(at, diag)
    for at in range(chunks):
        column_near(v.f_shard.at[at], v.w_ffn.at[at], v.s_fcol.at[at])

    for step in range(1, count):
        came(v.cond_buf.at[lax.rem(d + count - step, count)], v.s_cond, step - 1)
    for at in range(count):
        v.act_rows[rows * at : rows * (at + 1)] = v.cond_buf[at]
    act = silu_value(v.act_rows[...]).astype(bf16)
    v.act_rows[...] = act.astype(f32)
    v.mod_rows[...] = dot_plain(act, v.ada_ref[...])
    for at in range(count):
        v.mod_part[at] = v.mod_rows[rows * at : rows * (at + 1)]
    for at in range(count):
        to = (2 * (at // 2) + h, 2 * (at % 2) + l)
        mine = jnp.logical_and(d == to[0], z == to[1])
        send_if(jnp.logical_not(mine), v.mod_part.at[at], v.mod_recv.at[d], v.s_mod, at, to, there=d)

        @pl.when(mine)
        def _():
            v.mod_recv[d] = v.mod_part[at]

    swap_came(v.x_all, v.s_xswap)
    spread_tokens(v.x_all, v.s_x, off)
    for at in range(count):
        mine = jnp.logical_and(d == at, z == 2 * c + l)
        came_if(jnp.logical_not(mine), v.mod_recv.at[at], v.s_mod, at)
    v.mod_all[t] = jnp.sum(v.mod_recv[...], axis=0)
    group = ((sib, t_sib), (near, t_near), (cross, t_cross))
    for slot, (to, _) in enumerate(group):
        send(v.mod_all.at[t], v.mod_all.at[t], v.s_modall, slot, to)

    for at in range(heads + 1):
        attn_on(at, off)
    for at in range(chunks - 1):
        column_far(v.f_shard.at[at], v.w_ffn.at[at], v.s_fcol.at[at])
    forward_tokens(v.x_all, v.s_x)
    ffn_on(0, diag)
    for slot, (_, at) in enumerate(group):
        came(v.mod_all.at[at], v.s_modall, slot)
    for row in range(rows):
        full = jnp.concatenate([v.mod_all[at][row : row + 1] for at in range(4)], axis=1)
        for at in range(6):
            v.modv[at, row] = full[:, at * width : (at + 1) * width]
    tokens_came(v.x_all, v.s_x)

    order = [lax.rem(1 - c + turn, 2) for turn in range(2)]

    for row in order:
        normed, inverse = norm_parts(v.x_all[row].astype(f32))
        v.normed_a[row] = normed
        v.inverse_a[row] = inverse
        v.attn_in[row] = (normed * (1.0 + v.modv[1, row]) + v.modv[0, row]).astype(bf16)

    def part_of(at, row, kind):
        return v.qkv[at, row, :, kind * HEAD_DIM : (kind + 1) * HEAD_DIM]

    def exchange_start(part, pair, sems):
        send(part.at[1 - c], pair, sems, 0, sib)

    def exchange_near(part, pair, both, other, sems):
        came(pair, sems, 0)
        both[...] = (part[c].astype(f32) + pair[...].astype(f32)).astype(bf16)
        send(both, other, sems, 1, near)

    def exchange_back(both, other, out, sems):
        came(other, sems, 1)
        out[c] = (both[...].astype(f32) + other[...].astype(f32)).astype(bf16)
        send(out.at[c], out.at[c], sems, 2, sib)

    swap_in(v.cot_ref, v.cot_all, v.s_cswap)
    for at in range(heads):
        plane_came(v.w_attn.at[at], v.s_aplane.at[at])
        for row in order:
            v.qkv[at, row] = dot_plain(v.attn_in[row], v.w_attn[at]).astype(bf16)
            scores = dot_right(part_of(at, row, 0), part_of(at, row, 1)) * scale
            shifted = jnp.exp(scores - jnp.max(scores, axis=-1, keepdims=True))
            probs = shifted / jnp.sum(shifted, axis=-1, keepdims=True)
            v.probs[row, at] = probs
            v.mixed[row, :, at * HEAD_DIM : (at + 1) * HEAD_DIM] = dot_plain(
                probs.astype(bf16), part_of(at, row, 2)
            ).astype(bf16)
        if at == 0:
            column_far(v.f_shard.at[2], v.w_ffn.at[2], v.s_fcol.at[2])
            ffn_on(1, diag)
        if at == 1:
            ffn_on(0, off)
            ffn_on(2, diag)
    swap_came(v.cot_all, v.s_cswap)
    spread_tokens(v.cot_all, v.s_cot, count > 0)
    ffn_on(1, off)
    plane_came(v.w_attn.at[heads], v.s_aplane.at[heads])
    for turn, row in enumerate(order):
        v.a_part[row] = dot_right(v.mixed[row], v.w_attn[heads]).astype(bf16)
        if turn == 0:
            exchange_start(v.a_part, v.a_pair, v.s_a)
    exchange_near(v.a_part, v.a_pair, v.a_both, v.a_other, v.s_a)
    ffn_on(2, off)
    exchange_back(v.a_both, v.a_other, v.a_out, v.s_a)
    forward_tokens(v.cot_all, v.s_cot)

    for turn in (1, 0):
        row = order[turn]
        if turn == 0:
            came(v.a_out.at[1 - c], v.s_a, 2)
        resid = v.x_all[row].astype(f32) + v.modv[2, row] * v.a_out[row].astype(f32)
        v.resid[row] = resid
        normed, inverse = norm_parts(resid)
        v.normed_f[row] = normed
        v.inverse_f[row] = inverse
        v.ffn_in[row] = (normed * (1.0 + v.modv[4, row]) + v.modv[3, row]).astype(bf16)

    def whole(ref):
        return ref[...].reshape(rows * seq, ref.shape[-1])

    class Reduction:
        def __init__(self, grads, recv, total, low, home, plane, column):
            self.grads, self.recv, self.total, self.low = grads, recv, total, low
            self.home, self.plane, self.column = home, plane, column

        def start(self):
            for step in range(1, pairs):
                to = lax.rem(p + step, pairs)
                send(
                    rows_of(self.grads, to, 2 * shard),
                    self.recv.at[step - 1],
                    self.plane,
                    step - 1,
                    (2 * to + c, z),
                )

        def middle(self):
            total = rows_of(self.grads, p, 2 * shard)[...].astype(f32)
            for step in range(1, pairs):
                came(self.recv.at[step - 1], self.plane, step - 1)
                total += self.recv[step - 1].astype(f32)
            self.total[...] = total
            self.low[...] = total.astype(bf16)
            for side in range(2):
                send_if(
                    off,
                    self.low.at[pl.ds(side * shard, shard)],
                    self.home.at[1],
                    self.column,
                    side,
                    (2 * p + side, 2 * c + l),
                    there=1,
                )
            send_if(
                diag, rows_of(self.low, 1 - c, shard), self.home.at[0], self.column, 0, sib, there=0
            )

        def end(self):
            came(self.home.at[1], self.column, 1)
            came_if(off, self.home.at[0], self.column, 0)
            first = jnp.where(
                diag, rows_of(self.total, c, shard)[...], self.home[0].astype(f32)
            )
            return first + self.home[1].astype(f32)

    attn_sums = [
        Reduction(
            v.ga.at[at], v.ga_recv.at[at], v.ga_sum.at[at], v.ga_low.at[at], v.ga_home.at[at],
            v.s_ared.at[at], v.s_ahome.at[at],
        )
        for at in range(heads + 1)
    ]
    ffn_sums = [
        Reduction(
            v.gf.at[at], v.gf_recv.at[at], v.gf_sum.at[at], v.gf_low.at[at], v.gf_home.at[at],
            v.s_fred.at[at], v.s_fhome.at[at],
        )
        for at in range(chunks)
    ]

    def half_of(ref, at, size):
        return ref.at[pl.ds(pl.multiple_of(at * size, size), size)]

    def scatter_start(part, pair, sems, row):
        send(half_of(part.at[row], 1 - c, half), pair.at[row], sems, 2 * row, sib)

    def scatter_near(part, pair, kept, low, other, sems, row):
        came(pair.at[row], sems, 2 * row)
        kept[row] = half_of(part.at[row], c, half)[...].astype(f32) + pair[row].astype(f32)
        low[row] = half_of(kept.at[row], 1 - l, own)[...].astype(bf16)
        send(low.at[row], other.at[row], sems, 2 * row + 1, near)

    def scatter_end(kept, other, sems, row):
        came(other.at[row], sems, 2 * row + 1)
        return half_of(kept.at[row], l, own)[...] + other[row].astype(f32)

    def ffn_grads(at):
        v.gf[at, :, :block] = dot_left(whole(v.ffn_in), whole(v.d_hidden.at[at])).astype(bf16)
        v.gf[at, :, block:] = dot_left(whole(v.d_ffn_out), whole(v.hidden.at[at])).astype(bf16)
        ffn_sums[at].start()

    tokens_came(v.cot_all, v.s_cot)
    for row in order:
        v.d_ffn_out[row] = (v.modv[5, row] * v.cot_all[row].astype(f32)).astype(bf16)
    for at in range(chunks):
        plane_came(v.w_ffn.at[at], v.s_fplane.at[at])
        for row in order:
            hidden, slope = gelu_and_slope(dot_plain(v.ffn_in[row], v.w_ffn[at, :, :block]))
            v.hidden[at, row] = hidden.astype(bf16)
            v.d_hidden[at, row] = (
                dot_plain(v.d_ffn_out[row], v.w_ffn[at, :, block:]) * slope
            ).astype(bf16)
        if at < chunks - 1:
            ffn_grads(at)
    for turn, row in enumerate(order):
        total = dot_right(v.d_hidden[0, row], v.w_ffn[0, :, :block])
        for at in range(1, chunks):
            total += dot_right(v.d_hidden[at, row], v.w_ffn[at, :, :block])
        v.b_part[row] = total.astype(bf16)
        if turn == 0:
            exchange_start(v.b_part, v.b_pair, v.s_b)
    exchange_near(v.b_part, v.b_pair, v.b_both, v.b_other, v.s_b)

    ffn_grads(chunks - 1)
    for row in order:
        total = dot_right(v.hidden[0, row], v.w_ffn[0, :, block:])
        for at in range(1, chunks):
            total += dot_right(v.hidden[at, row], v.w_ffn[at, :, block:])
        v.dvec[5, row] = jnp.sum(v.cot_all[row].astype(f32) * total, axis=0, keepdims=True)
        v.f_part[row] = total.astype(bf16)
    for row in range(rows):
        scatter_start(v.f_part, v.f_pair, v.s_f, row)
    exchange_back(v.b_both, v.b_other, v.b_out, v.s_b)
    for row in range(rows):
        scatter_near(v.f_part, v.f_pair, v.f_kept, v.f_low, v.f_other, v.s_f, row)
    ffn_sums[0].middle()

    for turn in (1, 0):
        row = order[turn]
        if turn == 0:
            came(v.b_out.at[1 - c], v.s_b, 2)
        d_ffn_in = v.b_out[row].astype(f32)
        normed = v.normed_f[row]
        v.dvec[3, row] = jnp.sum(d_ffn_in, axis=0, keepdims=True)
        v.dvec[4, row] = jnp.sum(d_ffn_in * normed, axis=0, keepdims=True)
        d_resid = v.cot_all[row].astype(f32) + norm_back(
            normed, v.inverse_f[row], d_ffn_in * (1.0 + v.modv[4, row])
        )
        v.d_resid[row] = d_resid
        v.dvec[2, row] = jnp.sum(d_resid * v.a_out[row].astype(f32), axis=0, keepdims=True)
        v.d_attn_out[row] = (v.modv[2, row] * d_resid).astype(bf16)
        v.d_mixed[row] = dot_plain(v.d_attn_out[row], v.w_attn[heads]).astype(bf16)
    ffn_sums[1].middle()
    for at in range(heads):
        for row in order:
            d_mixed = v.d_mixed[row, :, at * HEAD_DIM : (at + 1) * HEAD_DIM]
            probs = v.probs[row, at]
            d_probs = dot_right(d_mixed, part_of(at, row, 2))
            d_scores = probs * (d_probs - jnp.sum(d_probs * probs, axis=-1, keepdims=True))
            d_scores = d_scores.astype(bf16)
            found = (
                dot_plain(d_scores, part_of(at, row, 1)) * scale,
                dot_left(d_scores, part_of(at, row, 0)) * scale,
                dot_left(probs.astype(bf16), d_mixed),
            )
            v.d_qkv[at, row] = jnp.concatenate(found, axis=1).astype(bf16)
        v.ga[at] = dot_left(whole(v.attn_in), whole(v.d_qkv.at[at])).astype(bf16)
        attn_sums[at].start()
        if at == 1:
            ffn_sums[2].middle()
        if at == 0:
            v.ga[heads] = dot_left(whole(v.d_attn_out), whole(v.mixed)).astype(bf16)
            attn_sums[heads].start()
            for row in range(rows):
                f_own = scatter_end(v.f_kept, v.f_other, v.s_f, row)
                v.latent_low[row] = (
                    half_of(v.resid.at[row], t, own)[...] + v.modv[5, row] * f_own
                ).astype(bf16)
            send_if(off, v.latent_low, v.latent_ref, v.s_lswap, 0, swap)

            @pl.when(diag)
            def _():
                v.latent_ref[...] = v.latent_low[...]

    for row in range(rows):
        d_attn_in = dot_right(v.d_qkv[0, row], v.w_attn[0])
        for at in range(1, heads):
            d_attn_in += dot_right(v.d_qkv[at, row], v.w_attn[at])
        v.e_part[row] = d_attn_in.astype(bf16)
        scatter_start(v.e_part, v.e_pair, v.s_e, row)
        v.dvec[0, row] = jnp.sum(d_attn_in, axis=0, keepdims=True)
        v.dvec[1, row] = jnp.sum(d_attn_in * v.normed_a[row], axis=0, keepdims=True)
        if row == 1:
            scatter_near(v.e_part, v.e_pair, v.e_kept, v.e_low, v.e_other, v.s_e, 0)
    first_one = jnp.where(t == 0, 1.0, 0.0)
    for row in range(rows):
        full = jnp.concatenate(
            [
                v.dvec[at, row] * first_one if at in (2, 3, 4) else v.dvec[at, row]
                for at in range(6)
            ],
            axis=1,
        )
        for at in range(4):
            v.dm_part[at, row : row + 1] = full[:, at * columns : (at + 1) * columns]
    for slot, (to, at) in enumerate(group):
        send(v.dm_part.at[at], v.dm_recv.at[t], v.s_dm, slot, to)
    v.dm_recv[t] = v.dm_part[t]
    scatter_near(v.e_part, v.e_pair, v.e_kept, v.e_low, v.e_other, v.s_e, 1)
    for slot, (_, at) in enumerate(group):
        came(v.dm_recv.at[at], v.s_dm, slot)
    v.dm_own[...] = jnp.sum(v.dm_recv[...], axis=0).astype(bf16).astype(f32)
    j = 2 * p + h
    for at in range(count):
        mine = jnp.logical_and(d == at, z == 2 * c + l)
        send_if(
            jnp.logical_not(mine), v.dm_own, v.dm_all.at[j], v.s_dmall, at, (at, 2 * c + l), there=j
        )

        @pl.when(mine)
        def _():
            v.dm_all[j] = v.dm_own[...]

    for row in range(rows):
        e_own = scatter_end(v.e_kept, v.e_other, v.s_e, row)
        v.grad_x_own[row] = half_of(v.d_resid.at[row], t, own)[...] + norm_back(
            half_of(v.normed_a.at[row], t, own)[...],
            half_of(v.inverse_a.at[row], t, own)[...],
            e_own * (1.0 + v.modv[1, row]),
        )
        v.grad_x_low[row] = v.grad_x_own[row].astype(bf16)
        send_if(off, v.grad_x_low.at[row], v.grad_x_recv.at[row], v.s_gswap, row, swap)

    @pl.when(diag)
    def _():
        v.grad_x_ref[...] = v.grad_x_own[...]

    for at in range(count):
        mine = jnp.logical_and(d == 2 * (at // 2) + h, z == 2 * (at % 2) + l)
        came_if(jnp.logical_not(mine), v.dm_all.at[at], v.s_dmall, at)
    for at in range(count):
        v.dm_rows[rows * at : rows * (at + 1)] = v.dm_all[at]
    everyone = v.dm_rows[...].astype(bf16)
    d_act = dot_right(everyone, v.ada_ref[...])
    for at in range(count):
        v.act_part[at] = d_act[rows * at : rows * (at + 1)]
    for step in range(1, count):
        peer = lax.rem(d + step, count)
        send(v.act_part.at[peer], v.terms.at[d], v.s_act, step - 1, (peer, z))
    v.terms[d] = v.act_part[d]
    v.grad_ada_ref[...] = dot_left(v.act_rows[...].astype(bf16), everyone)
    attn_sums[heads].middle()
    for step in range(1, count):
        came(v.terms.at[lax.rem(d + count - step, count)], v.s_act, step - 1)
    v.gathered[z] = v.terms[...]
    for step in range(1, 4):
        peer = lax.rem(z + step, 4)
        send(v.terms, v.gathered.at[z], v.s_gat, step - 1, (d, peer))
    for at in range(heads):
        attn_sums[at].middle()

    def ffn_end(at):
        total = ffn_sums[at].end()
        v.grad_up_ref[:, at * block : (at + 1) * block] = total[:, :block]
        v.grad_down_ref[:, at * block : (at + 1) * block] = total[:, block:]

    ffn_end(0)
    ffn_end(1)
    for step in range(1, 4):
        came(v.gathered.at[lax.rem(z + 4 - step, 4)], v.s_gat, step - 1)
    for at in range(count):
        here = slice(at * shard, (at + 1) * shard)
        values = v.cond_own[at]
        gate = 1.0 / (1.0 + jnp.exp(-values))
        v.grad_cond_ref[:, here] = jnp.sum(v.gathered[:, at], axis=0) * (
            gate * (1.0 + values * (1.0 - gate))
        )
    ffn_end(2)
    v.grad_proj_ref[...] = attn_sums[heads].end().T

    @pl.when(off)
    def _():
        came(v.latent_ref, v.s_lswap, 0)
        for row in range(rows):
            came(v.grad_x_recv.at[row], v.s_gswap, row)
            v.grad_x_ref[row] = v.grad_x_recv[row].astype(f32)

    for at in range(heads):
        total = attn_sums[at].end()
        for kind in range(3):
            v.grad_qkv_ref[kind, :, at * HEAD_DIM : (at + 1) * HEAD_DIM] = total[
                :, kind * HEAD_DIM : (kind + 1) * HEAD_DIM
            ]
    for finish in later:
        finish()


def hand_kernel(*refs):
    count = (len(refs) - 1) // 2
    sems = refs[-1]
    copies = [
        pltpu.make_async_copy(refs[at], refs[count + at], sems.at[at]) for at in range(count)
    ]
    for copy in copies:
        copy.start()
    for copy in copies:
        copy.wait()


def hand_over(arrays):
    anywhere = pl.BlockSpec(memory_space=pl.ANY)
    return pl.pallas_call(
        hand_kernel,
        out_shape=tuple(jax.ShapeDtypeStruct(one.shape, one.dtype) for one in arrays),
        in_specs=[anywhere] * len(arrays),
        out_specs=tuple(VMEM for _ in arrays),
        scratch_shapes=[pltpu.SemaphoreType.DMA((len(arrays),))],
    )(*arrays)


def fast_shards(latent_in, condition, w_ada, w_qkv, w_proj, w_up, w_down, out_grad):
    count = lax.axis_size("dp")
    pairs = count // 2
    rows, own, width = latent_in.shape
    seq = 4 * own
    shard, columns = w_ada.shape
    local = w_proj.shape[0]
    units = w_down.shape[0]
    heads = local // HEAD_DIM
    chunks = units // FF_BLOCK
    shape = jax.ShapeDtypeStruct
    inputs = dict(
        x_ref=latent_in, cond_ref=condition, ada_ref=w_ada, qkv_ref=w_qkv, proj_ref=w_proj,
        up_ref=w_up, down_ref=w_down.T, cot_ref=out_grad,
    )
    outs = dict(
        latent_ref=shape(latent_in.shape, bf16),
        grad_x_ref=shape(latent_in.shape, f32),
        grad_cond_ref=shape(condition.shape, f32),
        grad_ada_ref=shape(w_ada.shape, f32),
        grad_qkv_ref=shape(w_qkv.shape, f32),
        grad_proj_ref=shape(w_proj.shape, f32),
        grad_up_ref=shape(w_up.shape, f32),
        grad_down_ref=shape(w_down.shape[::-1], f32),
    )
    tokens = (rows, seq, width)
    half = (rows, seq // 2, width)
    mine = latent_in.shape
    low = dict(
        a_shard=(heads + 1, shard, local), f_shard=(chunks, shard, 2 * FF_BLOCK),
        x_all=tokens, cot_all=tokens, attn_in=tokens, ffn_in=tokens,
        d_ffn_out=tokens, d_attn_out=tokens,
        hidden=(chunks, rows, seq, FF_BLOCK), d_hidden=(chunks, rows, seq, FF_BLOCK),
        w_attn=(heads + 1, width, local), w_ffn=(chunks, width, 2 * FF_BLOCK),
        qkv=(heads, rows, seq, 3 * HEAD_DIM), d_qkv=(heads, rows, seq, 3 * HEAD_DIM),
        mixed=(rows, seq, local), d_mixed=(rows, seq, local),
        a_part=tokens, a_pair=(seq, width), a_both=(seq, width),
        a_other=(seq, width), a_out=tokens,
        b_part=tokens, b_pair=(seq, width), b_both=(seq, width),
        b_other=(seq, width), b_out=tokens,
        e_part=tokens, e_pair=half, e_low=mine, e_other=mine,
        f_part=tokens, f_pair=half, f_low=mine, f_other=mine,
        latent_low=mine, grad_x_low=mine, grad_x_recv=mine,
        ga=(heads + 1, width, local), ga_recv=(heads + 1, pairs - 1, 2 * shard, local),
        ga_low=(heads + 1, 2 * shard, local), ga_home=(heads + 1, 2, shard, local),
        gf=(chunks, width, 2 * FF_BLOCK), gf_recv=(chunks, pairs - 1, 2 * shard, 2 * FF_BLOCK),
        gf_low=(chunks, 2 * shard, 2 * FF_BLOCK), gf_home=(chunks, 2, shard, 2 * FF_BLOCK),
    )
    wide = dict(
        cond_own=(count, rows, shard), cond_buf=(count, rows, shard),
        act_rows=(count * rows, shard),
        mod_rows=(count * rows, columns), mod_part=(count, rows, columns),
        mod_recv=(count, rows, columns), mod_all=(4, rows, columns),
        modv=(6, rows, 1, width), dvec=(6, rows, 1, width),
        normed_a=tokens, inverse_a=(rows, seq, 1),
        resid=tokens, normed_f=tokens, inverse_f=(rows, seq, 1), d_resid=tokens,
        probs=(rows, heads, seq, seq), grad_x_own=mine,
        e_kept=half, f_kept=half,
        ga_sum=(heads + 1, 2 * shard, local), gf_sum=(chunks, 2 * shard, 2 * FF_BLOCK),
        dm_part=(4, rows, columns), dm_recv=(4, rows, columns), dm_own=(rows, columns),
        dm_all=(count, rows, columns), dm_rows=(count * rows, columns),
        act_part=(count, rows, shard), terms=(count, rows, shard),
        gathered=(4, count, rows, shard),
    )
    sems = dict(
        s_cond=(2, count - 1), s_mod=(2, count), s_modall=(2, 3), s_xswap=(2, 1),
        s_cswap=(2, 1), s_x=(2, 3), s_cot=(2, 3),
        s_acol=(heads + 1, 2, 2), s_fcol=(chunks, 2, 2),
        s_aplane=(heads + 1, 2, pairs - 1), s_fplane=(chunks, 2, pairs - 1),
        s_a=(2, 3), s_b=(2, 3), s_e=(2, 2 * rows), s_f=(2, 2 * rows),
        s_ared=(heads + 1, 2, pairs - 1), s_fred=(chunks, 2, pairs - 1),
        s_ahome=(heads + 1, 2, 2), s_fhome=(chunks, 2, 2),
        s_dm=(2, 3), s_dmall=(2, count), s_act=(2, count - 1), s_gat=(2, 3),
        s_lswap=(2, 1), s_gswap=(2, rows),
    )
    scratch = {name: pltpu.VMEM(size, bf16) for name, size in low.items()}
    scratch.update({name: pltpu.VMEM(size, f32) for name, size in wide.items()})
    scratch.update({name: pltpu.SemaphoreType.DMA(size) for name, size in sems.items()})
    names = tuple(inputs) + tuple(outs) + tuple(scratch)
    results = pl.pallas_call(
        functools.partial(block_kernel, names),
        out_shape=tuple(outs.values()),
        in_specs=[VMEM] * len(inputs),
        out_specs=tuple(VMEM for _ in outs),
        scratch_shapes=list(scratch.values()),
        compiler_params=pltpu.CompilerParams(
            collective_id=7, has_side_effects=True, vmem_limit_bytes=60 * 2**20
        ),
    )(*inputs.values())
    results = hand_over(results)
    return results[:7] + (results[7].T,)


def can_pair(mesh):
    count, group = mesh.shape["dp"], mesh.shape["tensor"]
    return group == 4 and count % 2 == 0


def body(mesh):
    def run(*args):
        fits = (
            can_pair(mesh)
            and args[2].shape[0] % 16 == 0
            and args[0].shape[1] % 16 == 0
            and args[6].shape[0] % FF_BLOCK == 0
        )
        return (fast_shards if fits else shards)(*args)

    return run


def solution(mesh):
    return jax.shard_map(
        body(mesh),
        mesh=mesh,
        in_specs=(
            P("dp", "tensor", None),
            P("dp", None),
            P("dp", "tensor"),
            P(None, "dp", "tensor"),
            P("tensor", "dp"),
            P("dp", "tensor"),
            P("tensor", "dp"),
            P("dp", "tensor", None),
        ),
        out_specs=(
            P("dp", "tensor", None),
            P("dp", "tensor", None),
            P("dp", None),
            P("dp", "tensor"),
            P(None, "dp", "tensor"),
            P("tensor", "dp"),
            P("dp", "tensor"),
            P("tensor", "dp"),
        ),
        check_vma=False,
    )
```

```python
import functools
import math
import types

import jax
import jax.numpy as jnp
from jax import lax
from jax.experimental import pallas as pl
from jax.experimental.pallas import tpu as pltpu
from jax.sharding import PartitionSpec as P

MESH = pl.DeviceIdType.MESH
VMEM = pl.BlockSpec(memory_space=pltpu.VMEM)

HEAD_DIM = 64
FF_BLOCK = 256
EPS = 1e-06
f32 = jnp.float32
bf16 = jnp.bfloat16


def silu_value(values):
    return values / (1.0 + jnp.exp(-values))


def gelu_tanh(values):
    return (
        0.5
        * values
        * (
            1.0
            + jnp.tanh(math.sqrt(2.0 / math.pi) * (values + 0.044715 * values * values * values))
        )
    )


def norm_parts(values):
    centered = values - jnp.mean(values, axis=-1, keepdims=True)
    variance = jnp.mean(centered * centered, axis=-1, keepdims=True)
    inverse = lax.rsqrt(variance + EPS)
    return centered * inverse, inverse


def norm_back(normed, inverse, grad):
    return inverse * (
        grad
        - jnp.mean(grad, axis=-1, keepdims=True)
        - normed * jnp.mean(grad * normed, axis=-1, keepdims=True)
    )


def dot(form, left, right):
    return jnp.einsum(form, left, right, preferred_element_type=f32)


def gather_tensor(block, axis):
    return lax.all_gather(block, "tensor", axis=axis, tiled=True)


def greet(axes):
    barrier = pltpu.get_barrier_semaphore()
    total = 0
    for axis in axes:
        size = lax.axis_size(axis)
        me = lax.axis_index(axis)
        for step in range(1, size):
            pl.semaphore_signal(
                barrier, inc=1, device_id={axis: lax.rem(me + step, size)}, device_id_type=MESH
            )
        total += size - 1
    pl.semaphore_wait(barrier, total)


def start_exchange(axis, source, target, sems):
    size = lax.axis_size(axis)
    me = lax.axis_index(axis)
    copies = []
    for step in range(1, size):
        peer = lax.rem(me + step, size)
        copy = pltpu.make_async_remote_copy(
            src_ref=source(peer),
            dst_ref=target,
            send_sem=sems.at[0, step - 1],
            recv_sem=sems.at[1, step - 1],
            device_id={axis: peer},
            device_id_type=MESH,
        )
        copy.start()
        copies.append(copy)
    return copies


def wait_all(copies):
    for copy in copies:
        copy.wait()


def exchange(axis, source, target, sems):
    wait_all(start_exchange(axis, source, target, sems))


def sem_pair(axis):
    return pltpu.SemaphoreType.DMA((2, lax.axis_size(axis) - 1))


def call(kernel, outs, scratch, number, *args):
    return pl.pallas_call(
        kernel,
        out_shape=outs,
        in_specs=[VMEM] * len(args),
        out_specs=jax.tree.map(lambda _: VMEM, outs),
        scratch_shapes=scratch,
        compiler_params=pltpu.CompilerParams(
            collective_id=number, has_side_effects=True, vmem_limit_bytes=48 * 2**20
        ),
    )(*args)


def modulation_kernel(
    cond_ref, w_ref, x_ref, shard_ref, mod_ref, act_ref, x_all, w_all,
    cond_buf, part, recv, own, s0, s1, s2, s3, s4, s5
):
    count = lax.axis_size("dp")
    me, mine = lax.axis_index("dp"), lax.axis_index("tensor")
    greet(("dp", "tensor"))
    copies = start_exchange("dp", lambda peer: cond_ref.at[peer], cond_buf.at[me], s0)
    x_own = token_block(x_all, mine, x_ref.shape[1])
    x_copies = start_exchange("tensor", lambda peer: x_ref, x_own, s3)
    cond_buf[me] = cond_ref[me]
    x_own[...] = x_ref[...]
    w_all[me] = shard_ref[...]
    wait_all(copies)

    @pl.loop(0, count)
    def _(at):
        act = silu_value(cond_buf[at]).astype(bf16)
        act_ref[at] = act.astype(f32)
        part[at] = jnp.dot(act, w_ref[...], preferred_element_type=f32)

    copies = start_exchange("dp", lambda peer: part.at[peer], recv.at[me], s1)
    recv[me] = part[me]
    pairs = count // 2
    chip, side = me // 2, lax.rem(me, 2)
    sibling = 2 * chip + 1 - side

    def send(source, at, to, sems, number):
        copy = pltpu.make_async_remote_copy(
            src_ref=source,
            dst_ref=w_all.at[at],
            send_sem=sems.at[0, number],
            recv_sem=sems.at[1, number],
            device_id={"dp": to},
            device_id_type=MESH,
        )
        copy.start()
        return copy

    far = [
        send(shard_ref, me, 2 * lax.rem(chip + step, pairs) + side, s4, step)
        for step in range(1, pairs)
    ]
    near = [send(shard_ref, me, sibling, s5, 0)]
    wait_all(copies)
    own[...] = jnp.sum(recv[...], axis=0)
    copies = start_exchange("tensor", lambda peer: own, mod_ref.at[mine], s2)
    mod_ref[mine] = own[...]
    for step in range(1, pairs):
        far[step - 1].wait()
        came = 2 * lax.rem(chip + pairs - step, pairs) + side
        near.append(send(w_all.at[came], came, sibling, s5, step))
    wait_all(near)
    wait_all(copies)
    wait_all(x_copies)


def modulation_of(condition, w_ada, block, shard):
    count, group = lax.axis_size("dp"), lax.axis_size("tensor")
    rows, width = condition.shape
    shard_rows, columns = w_ada.shape
    blocks = condition.astype(f32).reshape(rows, count, shard_rows).transpose(1, 0, 2)
    mod, act, x_all, w_all = call(
        modulation_kernel,
        (
            jax.ShapeDtypeStruct((group, rows, columns), f32),
            jax.ShapeDtypeStruct((count, rows, shard_rows), f32),
            jax.ShapeDtypeStruct((rows, group * block.shape[1], width), bf16),
            jax.ShapeDtypeStruct((count,) + shard.shape, bf16),
        ),
        [
            pltpu.VMEM((count, rows, shard_rows), f32),
            pltpu.VMEM((count, rows, columns), f32),
            pltpu.VMEM((count, rows, columns), f32),
            pltpu.VMEM((rows, columns), f32),
            sem_pair("dp"),
            sem_pair("dp"),
            sem_pair("tensor"),
            sem_pair("tensor"),
            pltpu.SemaphoreType.DMA((2, count // 2)),
            pltpu.SemaphoreType.DMA((2, count // 2)),
        ],
        1,
        blocks,
        w_ada,
        block,
        shard,
    )
    mod = mod.transpose(1, 0, 2).reshape(rows, group * columns)
    act = act.reshape(count * rows, shard_rows).astype(bf16)
    return mod, act, x_all, w_all.reshape(count * shard.shape[0], shard.shape[1])


def token_block(ref, at, size):
    return ref.at[:, pl.ds(pl.multiple_of(at * size, size), size)]


def finish_reduce(part_ref, out_ref, recv, first, sems):
    group = lax.axis_size("tensor")
    mine = lax.axis_index("tensor")
    size = part_ref.shape[1] // group
    wait_all(first)
    total = token_block(part_ref, mine, size)[...].astype(f32)
    for step in range(1, group):
        total += recv[lax.rem(mine + step, group)].astype(f32)
    own = token_block(out_ref, mine, size)
    own[...] = total.astype(bf16)
    return start_exchange("tensor", lambda peer: own, own, sems)


def start_reduce(part_ref, recv, sems):
    group = lax.axis_size("tensor")
    size = part_ref.shape[1] // group
    return start_exchange(
        "tensor",
        lambda peer: token_block(part_ref, peer, size),
        recv.at[lax.axis_index("tensor")],
        sems,
    )


def reduce_kernel(part_ref, out_ref, recv, s0, s1):
    greet(("tensor",))
    first = start_reduce(part_ref, recv, s0)
    wait_all(finish_reduce(part_ref, out_ref, recv, first, s1))


def reduce_gather_kernel(part_ref, shard_ref, out_ref, w_all, recv, s0, s1, s2, s3):
    count = lax.axis_size("dp")
    me = lax.axis_index("dp")
    pairs = count // 2
    chip, side = me // 2, lax.rem(me, 2)
    sibling = 2 * chip + 1 - side
    greet(("dp", "tensor"))

    def send(source, at, to, sems, number):
        copy = pltpu.make_async_remote_copy(
            src_ref=source,
            dst_ref=w_all.at[at],
            send_sem=sems.at[0, number],
            recv_sem=sems.at[1, number],
            device_id={"dp": to},
            device_id_type=MESH,
        )
        copy.start()
        return copy

    first = start_reduce(part_ref, recv, s0)
    far = [
        send(shard_ref, me, 2 * lax.rem(chip + step, pairs) + side, s2, step)
        for step in range(1, pairs)
    ]
    near = [send(shard_ref, me, sibling, s3, 0)]
    w_all[me] = shard_ref[...]
    last = finish_reduce(part_ref, out_ref, recv, first, s1)
    for step in range(1, pairs):
        far[step - 1].wait()
        came = 2 * lax.rem(chip + pairs - step, pairs) + side
        near.append(send(w_all.at[came], came, sibling, s3, step))
    wait_all(near)
    wait_all(last)


def reduce_and_gather(part, shard, number):
    group, count = lax.axis_size("tensor"), lax.axis_size("dp")
    rows, seq, width = part.shape
    total, weights = call(
        reduce_gather_kernel,
        (
            jax.ShapeDtypeStruct(part.shape, bf16),
            jax.ShapeDtypeStruct((count,) + shard.shape, bf16),
        ),
        [
            pltpu.VMEM((group, rows, seq // group, width), bf16),
            sem_pair("tensor"),
            sem_pair("tensor"),
            pltpu.SemaphoreType.DMA((2, count // 2)),
            pltpu.SemaphoreType.DMA((2, count // 2)),
        ],
        number,
        part.astype(bf16),
        shard,
    )
    return total.astype(f32), weights.reshape(count * shard.shape[0], shard.shape[1])


def reduce_tensor(part, number):
    group = lax.axis_size("tensor")
    rows, seq, width = part.shape
    return call(
        reduce_kernel,
        jax.ShapeDtypeStruct(part.shape, bf16),
        [
            pltpu.VMEM((group, rows, seq // group, width), bf16),
            sem_pair("tensor"),
            sem_pair("tensor"),
        ],
        number,
        part.astype(bf16),
    ).astype(f32)


def final_kernel(
    attn_ref, ffn_ref, grad_ref, part_ref, w_ref, attn_out, ffn_out, grad_out, all_ref, act_ref,
    attn_recv, ffn_recv, pair_recv, stage, grad_recv, recv_mod, own, part, terms, gathered,
    s0, s1, s2, s3, m0, m1, m2, m3
):
    group = lax.axis_size("tensor")
    count = lax.axis_size("dp")
    pairs = count // 2
    me, mine = lax.axis_index("dp"), lax.axis_index("tensor")
    chip, side = me // 2, lax.rem(me, 2)
    size = attn_ref.shape[1] // group
    greet(("dp", "tensor"))
    copies = start_exchange("tensor", lambda peer: part_ref.at[peer], recv_mod.at[mine], m0)
    recv_mod[mine] = part_ref[mine]
    pair_copy = pltpu.make_async_remote_copy(
        src_ref=grad_ref.at[:, 1 - side],
        dst_ref=pair_recv,
        send_sem=s0.at[0],
        recv_sem=s0.at[1],
        device_id={"dp": 2 * chip + 1 - side},
        device_id_type=MESH,
    )
    pair_copy.start()
    attn_copies = start_exchange(
        "tensor", lambda peer: token_block(attn_ref, peer, size), attn_recv.at[mine], s1
    )
    ffn_copies = start_exchange(
        "tensor", lambda peer: token_block(ffn_ref, peer, size), ffn_recv.at[mine], s2
    )
    wait_all(copies)
    own[...] = jnp.sum(recv_mod[...], axis=0).astype(bf16).astype(f32)
    copies = start_exchange("dp", lambda peer: own, all_ref.at[me], m1)
    all_ref[me] = own[...]
    wait_all(copies)

    @pl.loop(0, count)
    def _(at):
        part[at] = lax.dot_general(
            all_ref[at].astype(bf16),
            w_ref[...],
            (((1,), (1,)), ((), ())),
            preferred_element_type=f32,
        )

    copies = start_exchange("dp", lambda peer: part.at[peer], terms.at[me], m2)
    terms[me] = part[me]
    pair_copy.wait()
    grad_copies = []
    for step in range(pairs):
        to = lax.rem(chip + step, pairs) if step else chip
        total = grad_ref[to, side].astype(f32) + pair_recv[to].astype(f32)
        if step == 0:
            grad_out[...] = total
            continue
        stage[to] = total.astype(bf16)
        copy = pltpu.make_async_remote_copy(
            src_ref=stage.at[to],
            dst_ref=grad_recv.at[chip],
            send_sem=s3.at[0, step - 1],
            recv_sem=s3.at[1, step - 1],
            device_id={"dp": 2 * to + side},
            device_id_type=MESH,
        )
        copy.start()
        grad_copies.append(copy)
    wait_all(copies)
    last_copies = start_exchange("tensor", lambda peer: terms, gathered.at[mine], m3)
    gathered[mine] = terms[...]
    wait_all(grad_copies)
    for step in range(1, pairs):
        grad_out[...] += grad_recv[lax.rem(chip + step, pairs)].astype(f32)
    for copies, source, recv, out in (
        (attn_copies, attn_ref, attn_recv, attn_out),
        (ffn_copies, ffn_ref, ffn_recv, ffn_out),
    ):
        wait_all(copies)
        total = token_block(source, mine, size)[...].astype(f32)
        for step in range(1, group):
            total += recv[lax.rem(mine + step, group)].astype(f32)
        out[...] = total
    wait_all(last_copies)
    act_ref[...] = jnp.sum(gathered[...], axis=0)


def final_sums(attn_part, ffn_part, grads, parts, w_ada):
    group, count = lax.axis_size("tensor"), lax.axis_size("dp")
    rows, seq, width = attn_part.shape
    depth, columns = grads.shape
    shard_rows = depth // count
    tokens = (rows, seq // group, width)
    mod_columns = w_ada.shape[1]
    attn_own, ffn_own, grads, everyone, act = call(
        final_kernel,
        (
            jax.ShapeDtypeStruct(tokens, f32),
            jax.ShapeDtypeStruct(tokens, f32),
            jax.ShapeDtypeStruct((shard_rows, columns), f32),
            jax.ShapeDtypeStruct((count, rows, mod_columns), f32),
            jax.ShapeDtypeStruct((count, rows, shard_rows), f32),
        ),
        [
            pltpu.VMEM((group,) + tokens, bf16),
            pltpu.VMEM((group,) + tokens, bf16),
            pltpu.VMEM((count // 2, shard_rows, columns), bf16),
            pltpu.VMEM((count // 2, shard_rows, columns), bf16),
            pltpu.VMEM((count // 2, shard_rows, columns), bf16),
            pltpu.VMEM((group, rows, mod_columns), f32),
            pltpu.VMEM((rows, mod_columns), f32),
            pltpu.VMEM((count, rows, shard_rows), f32),
            pltpu.VMEM((count, rows, shard_rows), f32),
            pltpu.VMEM((group, count, rows, shard_rows), f32),
            pltpu.SemaphoreType.DMA((2,)),
            sem_pair("tensor"),
            sem_pair("tensor"),
            pltpu.SemaphoreType.DMA((2, count // 2 - 1)),
            sem_pair("tensor"),
            sem_pair("dp"),
            sem_pair("dp"),
            sem_pair("tensor"),
        ],
        5,
        attn_part.astype(bf16),
        ffn_part.astype(bf16),
        grads.astype(bf16).reshape(count // 2, 2, shard_rows, columns),
        parts.reshape(rows, group, mod_columns).transpose(1, 0, 2),
        w_ada,
    )
    everyone = everyone.reshape(count * rows, mod_columns).astype(bf16)
    d_act = act.transpose(1, 0, 2).reshape(rows, count * shard_rows)
    return attn_own, ffn_own, grads, everyone, d_act


def shards(latent_in, condition, w_ada, w_qkv, w_proj, w_up, w_down, out_grad):
    rows, own_tokens, width = latent_in.shape
    scale = HEAD_DIM ** (-0.5)
    tensor_at = lax.axis_index("tensor")
    local = w_proj.shape[0]
    heads = local // HEAD_DIM
    units = w_down.shape[0]

    attn_shard = jnp.concatenate(
        [w_qkv[0], w_qkv[1], w_qkv[2], w_proj.T], axis=1
    )
    ffn_shard = jnp.concatenate([w_up, w_down.T], axis=1)
    modulation, cond_mine, tokens, attn_weights = modulation_of(
        condition, w_ada, latent_in, attn_shard
    )
    modulation = modulation.reshape(rows, 6, 1, width)
    shift_a, scale_a, gate_a, shift_f, scale_f, gate_f = (modulation[:, i] for i in range(6))

    w_in = attn_weights[:, : 3 * local]
    proj_t = attn_weights[:, 3 * local :]
    cotangent = gather_tensor(out_grad, 1).astype(f32)
    tokens = tokens.astype(f32)
    seq = tokens.shape[1]

    normed_a, inverse_a = norm_parts(tokens)
    attn_in = (normed_a * (1.0 + scale_a) + shift_a).astype(bf16)
    projected = dot("lsd,de->lse", attn_in, w_in).astype(bf16)
    projected = projected.reshape(rows, seq, 3, heads, HEAD_DIM)
    queries, keys, values = projected[:, :, 0], projected[:, :, 1], projected[:, :, 2]
    scores = dot("lqhe,lkhe->lhqk", queries, keys) * scale
    shifted = jnp.exp(scores - jnp.max(scores, axis=-1, keepdims=True))
    probs = shifted / jnp.sum(shifted, axis=-1, keepdims=True)
    probs_low = probs.astype(bf16)
    mixed = dot("lhqk,lkhe->lqhe", probs_low, values).reshape(rows, seq, local).astype(bf16)
    attn_out, ffn_weights = reduce_and_gather(dot("lsd,ed->lse", mixed, proj_t), ffn_shard, 3)
    up = ffn_weights[:, :units]
    down_t = ffn_weights[:, units:]
    resid = tokens + gate_a * attn_out
    normed_f, inverse_f = norm_parts(resid)
    ffn_in = (normed_f * (1.0 + scale_f) + shift_f).astype(bf16)
    hidden_pre = dot("lsd,dn->lsn", ffn_in, up)
    hidden, gelu_pull = jax.vjp(gelu_tanh, hidden_pre)
    hidden = hidden.astype(bf16)
    d_ffn_out = (gate_f * cotangent).astype(bf16)
    d_hidden_pre = gelu_pull(dot("lse,en->lsn", d_ffn_out, down_t))[0].astype(bf16)
    d_ffn_in = reduce_tensor(dot("lsn,dn->lsd", d_hidden_pre, up), 4)

    ffn_part = dot("lsn,en->lse", hidden, down_t)
    d_gate_f = jnp.sum(cotangent * ffn_part, axis=1)
    d_shift_f = jnp.sum(d_ffn_in, axis=1)
    d_scale_f = jnp.sum(d_ffn_in * normed_f, axis=1)
    d_resid = cotangent + norm_back(normed_f, inverse_f, d_ffn_in * (1.0 + scale_f))
    d_gate_a = jnp.sum(d_resid * attn_out, axis=1)
    d_attn_out = (gate_a * d_resid).astype(bf16)
    d_mixed = dot("lse,ed->lsd", d_attn_out, proj_t).astype(bf16)
    d_mixed = d_mixed.reshape(rows, seq, heads, HEAD_DIM)
    d_probs = dot("lqhe,lkhe->lhqk", d_mixed, values)
    d_scores = probs * (d_probs - jnp.sum(d_probs * probs, axis=-1, keepdims=True))
    d_scores = d_scores.astype(bf16)
    d_values = dot("lhqk,lqhe->lkhe", probs_low, d_mixed)
    d_queries = dot("lhqk,lkhe->lqhe", d_scores, keys) * scale
    d_keys = dot("lhqk,lqhe->lkhe", d_scores, queries) * scale
    d_projected = jnp.stack([d_queries, d_keys, d_values], axis=2)
    d_projected = d_projected.reshape(rows, seq, 3 * local).astype(bf16)
    d_attn_part = dot("lse,de->lsd", d_projected, w_in)

    grads = jnp.concatenate(
        [
            dot("lsd,lse->de", attn_in, d_projected).astype(bf16),
            dot("lse,lsd->ed", d_attn_out, mixed).astype(bf16),
            dot("lsd,lsn->dn", ffn_in, d_hidden_pre).astype(bf16),
            dot("lse,lsn->en", d_ffn_out, hidden).astype(bf16),
        ],
        axis=1,
    )
    d_shift_a = jnp.sum(d_attn_part, axis=1)
    d_scale_a = jnp.sum(d_attn_part * normed_a, axis=1)
    ones = jnp.where(tensor_at == 0, 1.0, 0.0)
    d_modulation = jnp.concatenate(
        [d_shift_a, d_scale_a, d_gate_a * ones, d_shift_f * ones, d_scale_f * ones, d_gate_f],
        axis=1,
    )
    d_attn_own, ffn_own, grads, d_mod_all, d_act = final_sums(
        d_attn_part, ffn_part, grads, d_modulation, w_ada
    )
    grad_attn, grad_ffn = grads[:, : 4 * local], grads[:, 4 * local :]
    first = tensor_at * own_tokens
    own = lambda value: lax.dynamic_slice_in_dim(value, first, own_tokens, 1)
    latent_out = (own(resid) + gate_f * ffn_own).astype(bf16)
    grad_latent = own(d_resid) + norm_back(
        own(normed_a), own(inverse_a), d_attn_own * (1.0 + scale_a)
    )

    grad_ada = dot("ld,le->de", cond_mine, d_mod_all)
    grad_condition = jax.vjp(silu_value, condition.astype(f32))[1](d_act)[0]

    grad_qkv = jnp.stack([grad_attn[:, j * local : (j + 1) * local] for j in range(3)], axis=0)
    grad_proj = grad_attn[:, 3 * local :].T
    grad_up = grad_ffn[:, :units]
    grad_down = grad_ffn[:, units:].T
    return (
        latent_out,
        grad_latent,
        grad_condition,
        grad_ada,
        grad_qkv,
        grad_proj,
        grad_up,
        grad_down,
    )


def dot_plain(left, right):
    return lax.dot_general(left, right, (((1,), (0,)), ((), ())), preferred_element_type=f32)


def dot_right(left, right):
    return lax.dot_general(left, right, (((1,), (1,)), ((), ())), preferred_element_type=f32)


def dot_left(left, right):
    return lax.dot_general(left, right, (((0,), (0,)), ((), ())), preferred_element_type=f32)


def gelu_and_slope(values):
    root = math.sqrt(2.0 / math.pi)
    squares = values * values
    bent = jnp.tanh(root * values * (1.0 + 0.044715 * squares))
    half = 0.5 * (1.0 + bent)
    slope = half + 0.5 * values * (1.0 - bent * bent) * (root * (1.0 + 3.0 * 0.044715 * squares))
    return values * half, slope


def block_kernel(names, *refs):
    v = types.SimpleNamespace(**dict(zip(names, refs)))
    count = lax.axis_size("dp")
    pairs = count // 2
    d, z = lax.axis_index("dp"), lax.axis_index("tensor")
    p, c, h, l = d // 2, lax.rem(d, 2), z // 2, lax.rem(z, 2)
    t = 2 * c + l
    t_sib, t_near, t_cross = 2 * (1 - c) + l, 2 * c + 1 - l, 2 * (1 - c) + 1 - l
    diag = c == h
    off = c != h
    sib = (2 * p + 1 - c, z)
    near = (d, 2 * h + 1 - l)
    cross = (2 * p + 1 - c, 2 * h + 1 - l)
    swap = (2 * p + h, 2 * c + l)
    rows, own, width = v.x_ref.shape
    seq = v.x_all.shape[1]
    half = seq // 2
    shard = v.ada_ref.shape[0]
    columns = v.ada_ref.shape[1]
    local = v.mixed.shape[2]
    heads = local // HEAD_DIM
    chunks, _, wide = v.w_ffn.shape
    block = wide // 2
    scale = HEAD_DIM ** (-0.5)
    later = []

    def copy(source, target, sems, slot, to, there=None):
        return pltpu.make_async_remote_copy(
            src_ref=source,
            dst_ref=target,
            send_sem=sems.at[0, slot],
            recv_sem=sems.at[1, slot if there is None else there],
            device_id=to,
            device_id_type=MESH,
        )

    def send(*args, **kwargs):
        moved = copy(*args, **kwargs)
        moved.start()
        later.append(moved.wait_send)

    def send_if(condition, *args, **kwargs):
        moved = copy(*args, **kwargs)
        pl.when(condition)(moved.start)

        def finish():
            pl.when(condition)(moved.wait_send)

        later.append(finish)

    def came(target, sems, slot):
        copy(target, target, sems, slot, sib).wait_recv()

    def came_if(condition, target, sems, slot):
        pl.when(condition)(copy(target, target, sems, slot, sib).wait_recv)

    def tokens_of(ref, at, size=own):
        return ref.at[:, pl.ds(pl.multiple_of(at * size, size), size)]

    def rows_of(ref, at, size):
        return ref.at[pl.ds(pl.multiple_of(at * size, size), size)]

    barrier = pltpu.get_barrier_semaphore()
    here = 2 * d + h
    for step in range(1, 2 * count):
        other = lax.rem(here + step, 2 * count)
        pl.semaphore_signal(
            barrier,
            inc=1,
            device_id=(other // 2, 2 * lax.rem(other, 2) + l),
            device_id_type=MESH,
        )
    for side in range(2):
        for part in range(2):
            pl.semaphore_signal(
                barrier,
                inc=1,
                device_id=(2 * p + side, 2 * part + 1 - l),
                device_id_type=MESH,
            )

    cond = v.cond_ref[...].astype(f32)
    for at in range(count):
        v.cond_own[at] = cond[:, at * shard : (at + 1) * shard]
    for at in range(heads):
        v.a_shard[at] = jnp.concatenate(
            [v.qkv_ref[kind, :, at * HEAD_DIM : (at + 1) * HEAD_DIM] for kind in range(3)], axis=1
        )
    v.a_shard[heads] = v.proj_ref[...].T
    for at in range(chunks):
        v.f_shard[at, :, :block] = v.up_ref[:, at * block : (at + 1) * block]
        v.f_shard[at, :, block:] = v.down_ref[:, at * block : (at + 1) * block]
    pl.semaphore_wait(barrier, 2 * count - 1 + 4)

    def swap_in(ref, whole, sems):
        send_if(off, ref, tokens_of(whole, z), sems, 0, swap)

        @pl.when(diag)
        def _():
            tokens_of(whole, t)[...] = ref[...]

    def swap_came(whole, sems):
        came_if(off, tokens_of(whole, t), sems, 0)

    def spread_tokens(whole, sems, condition):
        mine = tokens_of(whole, t)
        send_if(condition, mine, mine, sems, 1, near)
        send_if(condition, mine, mine, sems, 0, sib)

    def forward_tokens(whole, sems):
        mine = tokens_of(whole, t_near)
        came(mine, sems, 1)
        send(mine, mine, sems, 2, sib)

    def tokens_came(whole, sems):
        came(tokens_of(whole, t_sib), sems, 0)
        came(tokens_of(whole, t_cross), sems, 2)

    def column_near(ref, whole, sems):
        mine = rows_of(whole, d, shard)
        send_if(off, ref, mine, sems, 0, sib, there=c)

        @pl.when(diag)
        def _():
            mine[...] = ref[...]

    def column_far(ref, whole, sems):
        send(ref, rows_of(whole, d, shard), sems, 1, (2 * p + h, 2 * (1 - h) + l), there=c)

    def column_on(whole, sems, plane, condition):
        for side in range(2):
            local_one = jnp.logical_and(diag, c == side)
            came_if(
                jnp.logical_and(condition, jnp.logical_not(local_one)),
                rows_of(whole, 2 * p + side, shard),
                sems,
                side,
            )
        mine = rows_of(whole, p, 2 * shard)
        for step in range(1, pairs):
            to = lax.rem(p + step, pairs)
            send_if(condition, mine, mine, plane, step - 1, (2 * to + c, z))

    def plane_came(whole, plane):
        for step in range(1, pairs):
            source = lax.rem(p + pairs - step, pairs)
            came(rows_of(whole, source, 2 * shard), plane, step - 1)

    def attn_on(at, condition):
        column_on(v.w_attn.at[at], v.s_acol.at[at], v.s_aplane.at[at], condition)

    def ffn_on(at, condition):
        column_on(v.w_ffn.at[at], v.s_fcol.at[at], v.s_fplane.at[at], condition)

    for step in range(1, count):
        peer = lax.rem(d + step, count)
        send(v.cond_own.at[peer], v.cond_buf.at[d], v.s_cond, step - 1, (peer, z))
    v.cond_buf[d] = v.cond_own[d]
    swap_in(v.x_ref, v.x_all, v.s_xswap)
    for at in range(heads + 1):
        column_far(v.a_shard.at[at], v.w_attn.at[at], v.s_acol.at[at])
    spread_tokens(v.x_all, v.s_x, diag)
    for at in range(heads + 1):
        column_near(v.a_shard.at[at], v.w_attn.at[at], v.s_acol.at[at])
    for at in range(heads + 1):
        attn_on(at, diag)
    for at in range(chunks):
        column_near(v.f_shard.at[at], v.w_ffn.at[at], v.s_fcol.at[at])

    for step in range(1, count):
        came(v.cond_buf.at[lax.rem(d + count - step, count)], v.s_cond, step - 1)
    for at in range(count):
        v.act_rows[rows * at : rows * (at + 1)] = v.cond_buf[at]
    act = silu_value(v.act_rows[...]).astype(bf16)
    v.act_rows[...] = act.astype(f32)
    v.mod_rows[...] = dot_plain(act, v.ada_ref[...])
    for at in range(count):
        v.mod_part[at] = v.mod_rows[rows * at : rows * (at + 1)]
    for at in range(count):
        to = (2 * (at // 2) + h, 2 * (at % 2) + l)
        mine = jnp.logical_and(d == to[0], z == to[1])
        send_if(jnp.logical_not(mine), v.mod_part.at[at], v.mod_recv.at[d], v.s_mod, at, to, there=d)

        @pl.when(mine)
        def _():
            v.mod_recv[d] = v.mod_part[at]

    swap_came(v.x_all, v.s_xswap)
    spread_tokens(v.x_all, v.s_x, off)
    for at in range(count):
        mine = jnp.logical_and(d == at, z == 2 * c + l)
        came_if(jnp.logical_not(mine), v.mod_recv.at[at], v.s_mod, at)
    v.mod_all[t] = jnp.sum(v.mod_recv[...], axis=0)
    group = ((sib, t_sib), (near, t_near), (cross, t_cross))
    for slot, (to, _) in enumerate(group):
        send(v.mod_all.at[t], v.mod_all.at[t], v.s_modall, slot, to)

    for at in range(heads + 1):
        attn_on(at, off)
    for at in range(chunks - 1):
        column_far(v.f_shard.at[at], v.w_ffn.at[at], v.s_fcol.at[at])
    forward_tokens(v.x_all, v.s_x)
    ffn_on(0, diag)
    for slot, (_, at) in enumerate(group):
        came(v.mod_all.at[at], v.s_modall, slot)
    for row in range(rows):
        full = jnp.concatenate([v.mod_all[at][row : row + 1] for at in range(4)], axis=1)
        for at in range(6):
            v.modv[at, row] = full[:, at * width : (at + 1) * width]
    tokens_came(v.x_all, v.s_x)

    order = [lax.rem(1 - c + turn, 2) for turn in range(2)]

    for row in order:
        normed, inverse = norm_parts(v.x_all[row].astype(f32))
        v.normed_a[row] = normed
        v.inverse_a[row] = inverse
        v.attn_in[row] = (normed * (1.0 + v.modv[1, row]) + v.modv[0, row]).astype(bf16)

    def part_of(at, row, kind):
        return v.qkv[at, row, :, kind * HEAD_DIM : (kind + 1) * HEAD_DIM]

    def exchange_start(part, pair, sems):
        send(part.at[1 - c], pair, sems, 0, sib)

    def exchange_near(part, pair, both, other, sems):
        came(pair, sems, 0)
        both[...] = (part[c].astype(f32) + pair[...].astype(f32)).astype(bf16)
        send(both, other, sems, 1, near)

    def exchange_back(both, other, out, sems):
        came(other, sems, 1)
        out[c] = (both[...].astype(f32) + other[...].astype(f32)).astype(bf16)
        send(out.at[c], out.at[c], sems, 2, sib)

    swap_in(v.cot_ref, v.cot_all, v.s_cswap)
    for at in range(heads):
        plane_came(v.w_attn.at[at], v.s_aplane.at[at])
        for row in order:
            v.qkv[at, row] = dot_plain(v.attn_in[row], v.w_attn[at]).astype(bf16)
            scores = dot_right(part_of(at, row, 0), part_of(at, row, 1)) * scale
            shifted = jnp.exp(scores - jnp.max(scores, axis=-1, keepdims=True))
            probs = shifted / jnp.sum(shifted, axis=-1, keepdims=True)
            v.probs[row, at] = probs
            v.mixed[row, :, at * HEAD_DIM : (at + 1) * HEAD_DIM] = dot_plain(
                probs.astype(bf16), part_of(at, row, 2)
            ).astype(bf16)
        if at == 0:
            column_far(v.f_shard.at[2], v.w_ffn.at[2], v.s_fcol.at[2])
            ffn_on(1, diag)
        if at == 1:
            ffn_on(0, off)
            ffn_on(2, diag)
    swap_came(v.cot_all, v.s_cswap)
    spread_tokens(v.cot_all, v.s_cot, count > 0)
    ffn_on(1, off)
    plane_came(v.w_attn.at[heads], v.s_aplane.at[heads])
    for turn, row in enumerate(order):
        v.a_part[row] = dot_right(v.mixed[row], v.w_attn[heads]).astype(bf16)
        if turn == 0:
            exchange_start(v.a_part, v.a_pair, v.s_a)
    exchange_near(v.a_part, v.a_pair, v.a_both, v.a_other, v.s_a)
    ffn_on(2, off)
    exchange_back(v.a_both, v.a_other, v.a_out, v.s_a)
    forward_tokens(v.cot_all, v.s_cot)

    for turn in (1, 0):
        row = order[turn]
        if turn == 0:
            came(v.a_out.at[1 - c], v.s_a, 2)
        resid = v.x_all[row].astype(f32) + v.modv[2, row] * v.a_out[row].astype(f32)
        v.resid[row] = resid
        normed, inverse = norm_parts(resid)
        v.normed_f[row] = normed
        v.inverse_f[row] = inverse
        v.ffn_in[row] = (normed * (1.0 + v.modv[4, row]) + v.modv[3, row]).astype(bf16)

    def whole(ref):
        return ref[...].reshape(rows * seq, ref.shape[-1])

    class Reduction:
        def __init__(self, grads, recv, total, low, home, plane, column):
            self.grads, self.recv, self.total, self.low = grads, recv, total, low
            self.home, self.plane, self.column = home, plane, column

        def start(self):
            for step in range(1, pairs):
                to = lax.rem(p + step, pairs)
                send(
                    rows_of(self.grads, to, 2 * shard),
                    self.recv.at[step - 1],
                    self.plane,
                    step - 1,
                    (2 * to + c, z),
                )

        def middle(self):
            total = rows_of(self.grads, p, 2 * shard)[...].astype(f32)
            for step in range(1, pairs):
                came(self.recv.at[step - 1], self.plane, step - 1)
                total += self.recv[step - 1].astype(f32)
            self.total[...] = total
            self.low[...] = total.astype(bf16)
            for side in range(2):
                send_if(
                    off,
                    self.low.at[pl.ds(side * shard, shard)],
                    self.home.at[1],
                    self.column,
                    side,
                    (2 * p + side, 2 * c + l),
                    there=1,
                )
            send_if(
                diag, rows_of(self.low, 1 - c, shard), self.home.at[0], self.column, 0, sib, there=0
            )

        def end(self):
            came(self.home.at[1], self.column, 1)
            came_if(off, self.home.at[0], self.column, 0)
            first = jnp.where(
                diag, rows_of(self.total, c, shard)[...], self.home[0].astype(f32)
            )
            return first + self.home[1].astype(f32)

    attn_sums = [
        Reduction(
            v.ga.at[at], v.ga_recv.at[at], v.ga_sum.at[at], v.ga_low.at[at], v.ga_home.at[at],
            v.s_ared.at[at], v.s_ahome.at[at],
        )
        for at in range(heads + 1)
    ]
    ffn_sums = [
        Reduction(
            v.gf.at[at], v.gf_recv.at[at], v.gf_sum.at[at], v.gf_low.at[at], v.gf_home.at[at],
            v.s_fred.at[at], v.s_fhome.at[at],
        )
        for at in range(chunks)
    ]

    def half_of(ref, at, size):
        return ref.at[pl.ds(pl.multiple_of(at * size, size), size)]

    def scatter_start(part, pair, sems, row):
        send(half_of(part.at[row], 1 - c, half), pair.at[row], sems, 2 * row, sib)

    def scatter_near(part, pair, kept, low, other, sems, row):
        came(pair.at[row], sems, 2 * row)
        kept[row] = half_of(part.at[row], c, half)[...].astype(f32) + pair[row].astype(f32)
        low[row] = half_of(kept.at[row], 1 - l, own)[...].astype(bf16)
        send(low.at[row], other.at[row], sems, 2 * row + 1, near)

    def scatter_end(kept, other, sems, row):
        came(other.at[row], sems, 2 * row + 1)
        return half_of(kept.at[row], l, own)[...] + other[row].astype(f32)

    def ffn_grads(at):
        v.gf[at, :, :block] = dot_left(whole(v.ffn_in), whole(v.d_hidden.at[at])).astype(bf16)
        v.gf[at, :, block:] = dot_left(whole(v.d_ffn_out), whole(v.hidden.at[at])).astype(bf16)
        ffn_sums[at].start()

    tokens_came(v.cot_all, v.s_cot)
    for row in order:
        v.d_ffn_out[row] = (v.modv[5, row] * v.cot_all[row].astype(f32)).astype(bf16)
    for at in range(chunks):
        plane_came(v.w_ffn.at[at], v.s_fplane.at[at])
        for row in order:
            hidden, slope = gelu_and_slope(dot_plain(v.ffn_in[row], v.w_ffn[at, :, :block]))
            v.hidden[at, row] = hidden.astype(bf16)
            v.d_hidden[at, row] = (
                dot_plain(v.d_ffn_out[row], v.w_ffn[at, :, block:]) * slope
            ).astype(bf16)
        if at == 0:
            ffn_grads(at)
    for turn, row in enumerate(order):
        total = dot_right(v.d_hidden[0, row], v.w_ffn[0, :, :block])
        for at in range(1, chunks):
            total += dot_right(v.d_hidden[at, row], v.w_ffn[at, :, :block])
        v.b_part[row] = total.astype(bf16)
        if turn == 0:
            exchange_start(v.b_part, v.b_pair, v.s_b)
    exchange_near(v.b_part, v.b_pair, v.b_both, v.b_other, v.s_b)

    for at in range(1, chunks):
        ffn_grads(at)
    for row in order:
        total = dot_right(v.hidden[0, row], v.w_ffn[0, :, block:])
        for at in range(1, chunks):
            total += dot_right(v.hidden[at, row], v.w_ffn[at, :, block:])
        v.dvec[5, row] = jnp.sum(v.cot_all[row].astype(f32) * total, axis=0, keepdims=True)
        v.f_part[row] = total.astype(bf16)
    for row in range(rows):
        scatter_start(v.f_part, v.f_pair, v.s_f, row)
    exchange_back(v.b_both, v.b_other, v.b_out, v.s_b)
    for row in range(rows):
        scatter_near(v.f_part, v.f_pair, v.f_kept, v.f_low, v.f_other, v.s_f, row)
    ffn_sums[0].middle()

    for turn in (1, 0):
        row = order[turn]
        if turn == 0:
            came(v.b_out.at[1 - c], v.s_b, 2)
        d_ffn_in = v.b_out[row].astype(f32)
        normed = v.normed_f[row]
        v.dvec[3, row] = jnp.sum(d_ffn_in, axis=0, keepdims=True)
        v.dvec[4, row] = jnp.sum(d_ffn_in * normed, axis=0, keepdims=True)
        d_resid = v.cot_all[row].astype(f32) + norm_back(
            normed, v.inverse_f[row], d_ffn_in * (1.0 + v.modv[4, row])
        )
        v.d_resid[row] = d_resid
        v.dvec[2, row] = jnp.sum(d_resid * v.a_out[row].astype(f32), axis=0, keepdims=True)
        v.d_attn_out[row] = (v.modv[2, row] * d_resid).astype(bf16)
        v.d_mixed[row] = dot_plain(v.d_attn_out[row], v.w_attn[heads]).astype(bf16)
    ffn_sums[1].middle()
    for at in range(heads):
        for row in order:
            d_mixed = v.d_mixed[row, :, at * HEAD_DIM : (at + 1) * HEAD_DIM]
            probs = v.probs[row, at]
            d_probs = dot_right(d_mixed, part_of(at, row, 2))
            d_scores = probs * (d_probs - jnp.sum(d_probs * probs, axis=-1, keepdims=True))
            d_scores = d_scores.astype(bf16)
            found = (
                dot_plain(d_scores, part_of(at, row, 1)) * scale,
                dot_left(d_scores, part_of(at, row, 0)) * scale,
                dot_left(probs.astype(bf16), d_mixed),
            )
            v.d_qkv[at, row] = jnp.concatenate(found, axis=1).astype(bf16)
        v.ga[at] = dot_left(whole(v.attn_in), whole(v.d_qkv.at[at])).astype(bf16)
        attn_sums[at].start()
        if at == 1:
            ffn_sums[2].middle()
        if at == 0:
            v.ga[heads] = dot_left(whole(v.d_attn_out), whole(v.mixed)).astype(bf16)
            attn_sums[heads].start()
            for row in range(rows):
                f_own = scatter_end(v.f_kept, v.f_other, v.s_f, row)
                v.latent_low[row] = (
                    half_of(v.resid.at[row], t, own)[...] + v.modv[5, row] * f_own
                ).astype(bf16)
            send_if(off, v.latent_low, v.latent_ref, v.s_lswap, 0, swap)

            @pl.when(diag)
            def _():
                v.latent_ref[...] = v.latent_low[...]

    for row in range(rows):
        d_attn_in = dot_right(v.d_qkv[0, row], v.w_attn[0])
        for at in range(1, heads):
            d_attn_in += dot_right(v.d_qkv[at, row], v.w_attn[at])
        v.e_part[row] = d_attn_in.astype(bf16)
        scatter_start(v.e_part, v.e_pair, v.s_e, row)
        v.dvec[0, row] = jnp.sum(d_attn_in, axis=0, keepdims=True)
        v.dvec[1, row] = jnp.sum(d_attn_in * v.normed_a[row], axis=0, keepdims=True)
        if row == 1:
            scatter_near(v.e_part, v.e_pair, v.e_kept, v.e_low, v.e_other, v.s_e, 0)
    first_one = jnp.where(t == 0, 1.0, 0.0)
    for row in range(rows):
        full = jnp.concatenate(
            [
                v.dvec[at, row] * first_one if at in (2, 3, 4) else v.dvec[at, row]
                for at in range(6)
            ],
            axis=1,
        )
        for at in range(4):
            v.dm_part[at, row : row + 1] = full[:, at * columns : (at + 1) * columns]
    for slot, (to, at) in enumerate(group):
        send(v.dm_part.at[at], v.dm_recv.at[t], v.s_dm, slot, to)
    v.dm_recv[t] = v.dm_part[t]
    scatter_near(v.e_part, v.e_pair, v.e_kept, v.e_low, v.e_other, v.s_e, 1)
    attn_sums[0].middle()
    attn_sums[heads].middle()
    for slot, (_, at) in enumerate(group):
        came(v.dm_recv.at[at], v.s_dm, slot)
    v.dm_own[...] = jnp.sum(v.dm_recv[...], axis=0).astype(bf16).astype(f32)
    j = 2 * p + h
    for at in range(count):
        mine = jnp.logical_and(d == at, z == 2 * c + l)
        send_if(
            jnp.logical_not(mine), v.dm_own, v.dm_all.at[j], v.s_dmall, at, (at, 2 * c + l), there=j
        )

        @pl.when(mine)
        def _():
            v.dm_all[j] = v.dm_own[...]

    for row in range(rows):
        e_own = scatter_end(v.e_kept, v.e_other, v.s_e, row)
        v.grad_x_own[row] = half_of(v.d_resid.at[row], t, own)[...] + norm_back(
            half_of(v.normed_a.at[row], t, own)[...],
            half_of(v.inverse_a.at[row], t, own)[...],
            e_own * (1.0 + v.modv[1, row]),
        )
        v.grad_x_low[row] = v.grad_x_own[row].astype(bf16)
        send_if(off, v.grad_x_low.at[row], v.grad_x_recv.at[row], v.s_gswap, row, swap)

    @pl.when(diag)
    def _():
        v.grad_x_ref[...] = v.grad_x_own[...]

    for at in range(1, heads - 1):
        attn_sums[at].middle()
    for at in range(count):
        mine = jnp.logical_and(d == 2 * (at // 2) + h, z == 2 * (at % 2) + l)
        came_if(jnp.logical_not(mine), v.dm_all.at[at], v.s_dmall, at)
    for at in range(count):
        v.dm_rows[rows * at : rows * (at + 1)] = v.dm_all[at]
    everyone = v.dm_rows[...].astype(bf16)
    d_act = dot_right(everyone, v.ada_ref[...])
    for at in range(count):
        v.act_part[at] = d_act[rows * at : rows * (at + 1)]
    for step in range(1, count):
        peer = lax.rem(d + step, count)
        send(v.act_part.at[peer], v.terms.at[d], v.s_act, step - 1, (peer, z))
    v.terms[d] = v.act_part[d]
    v.grad_ada_ref[...] = dot_left(v.act_rows[...].astype(bf16), everyone)
    attn_sums[heads - 1].middle()
    for step in range(1, count):
        came(v.terms.at[lax.rem(d + count - step, count)], v.s_act, step - 1)
    v.gathered[z] = v.terms[...]
    for step in range(1, 4):
        peer = lax.rem(z + step, 4)
        send(v.terms, v.gathered.at[z], v.s_gat, step - 1, (d, peer))

    def ffn_end(at):
        total = ffn_sums[at].end()
        v.grad_up_ref[:, at * block : (at + 1) * block] = total[:, :block]
        v.grad_down_ref[:, at * block : (at + 1) * block] = total[:, block:]

    ffn_end(0)
    ffn_end(1)
    for step in range(1, 4):
        came(v.gathered.at[lax.rem(z + 4 - step, 4)], v.s_gat, step - 1)
    for at in range(count):
        here = slice(at * shard, (at + 1) * shard)
        values = v.cond_own[at]
        gate = 1.0 / (1.0 + jnp.exp(-values))
        v.grad_cond_ref[:, here] = jnp.sum(v.gathered[:, at], axis=0) * (
            gate * (1.0 + values * (1.0 - gate))
        )
    ffn_end(2)
    v.grad_proj_ref[...] = attn_sums[heads].end().T

    @pl.when(off)
    def _():
        came(v.latent_ref, v.s_lswap, 0)
        for row in range(rows):
            came(v.grad_x_recv.at[row], v.s_gswap, row)
            v.grad_x_ref[row] = v.grad_x_recv[row].astype(f32)

    for at in range(heads):
        total = attn_sums[at].end()
        for kind in range(3):
            v.grad_qkv_ref[kind, :, at * HEAD_DIM : (at + 1) * HEAD_DIM] = total[
                :, kind * HEAD_DIM : (kind + 1) * HEAD_DIM
            ]
    for finish in later:
        finish()


def hand_kernel(*refs):
    count = (len(refs) - 1) // 2
    sems = refs[-1]
    copies = [
        pltpu.make_async_copy(refs[at], refs[count + at], sems.at[at]) for at in range(count)
    ]
    for copy in copies:
        copy.start()
    for copy in copies:
        copy.wait()


def hand_over(arrays):
    anywhere = pl.BlockSpec(memory_space=pl.ANY)
    return pl.pallas_call(
        hand_kernel,
        out_shape=tuple(jax.ShapeDtypeStruct(one.shape, one.dtype) for one in arrays),
        in_specs=[anywhere] * len(arrays),
        out_specs=tuple(VMEM for _ in arrays),
        scratch_shapes=[pltpu.SemaphoreType.DMA((len(arrays),))],
    )(*arrays)


def fast_shards(latent_in, condition, w_ada, w_qkv, w_proj, w_up, w_down, out_grad):
    count = lax.axis_size("dp")
    pairs = count // 2
    rows, own, width = latent_in.shape
    seq = 4 * own
    shard, columns = w_ada.shape
    local = w_proj.shape[0]
    units = w_down.shape[0]
    heads = local // HEAD_DIM
    chunks = units // FF_BLOCK
    shape = jax.ShapeDtypeStruct
    inputs = dict(
        x_ref=latent_in, cond_ref=condition, ada_ref=w_ada, qkv_ref=w_qkv, proj_ref=w_proj,
        up_ref=w_up, down_ref=w_down.T, cot_ref=out_grad,
    )
    outs = dict(
        latent_ref=shape(latent_in.shape, bf16),
        grad_x_ref=shape(latent_in.shape, f32),
        grad_cond_ref=shape(condition.shape, f32),
        grad_ada_ref=shape(w_ada.shape, f32),
        grad_qkv_ref=shape(w_qkv.shape, f32),
        grad_proj_ref=shape(w_proj.shape, f32),
        grad_up_ref=shape(w_up.shape, f32),
        grad_down_ref=shape(w_down.shape[::-1], f32),
    )
    tokens = (rows, seq, width)
    half = (rows, seq // 2, width)
    mine = latent_in.shape
    low = dict(
        a_shard=(heads + 1, shard, local), f_shard=(chunks, shard, 2 * FF_BLOCK),
        x_all=tokens, cot_all=tokens, attn_in=tokens, ffn_in=tokens,
        d_ffn_out=tokens, d_attn_out=tokens,
        hidden=(chunks, rows, seq, FF_BLOCK), d_hidden=(chunks, rows, seq, FF_BLOCK),
        w_attn=(heads + 1, width, local), w_ffn=(chunks, width, 2 * FF_BLOCK),
        qkv=(heads, rows, seq, 3 * HEAD_DIM), d_qkv=(heads, rows, seq, 3 * HEAD_DIM),
        mixed=(rows, seq, local), d_mixed=(rows, seq, local),
        a_part=tokens, a_pair=(seq, width), a_both=(seq, width),
        a_other=(seq, width), a_out=tokens,
        b_part=tokens, b_pair=(seq, width), b_both=(seq, width),
        b_other=(seq, width), b_out=tokens,
        e_part=tokens, e_pair=half, e_low=mine, e_other=mine,
        f_part=tokens, f_pair=half, f_low=mine, f_other=mine,
        latent_low=mine, grad_x_low=mine, grad_x_recv=mine,
        ga=(heads + 1, width, local), ga_recv=(heads + 1, pairs - 1, 2 * shard, local),
        ga_low=(heads + 1, 2 * shard, local), ga_home=(heads + 1, 2, shard, local),
        gf=(chunks, width, 2 * FF_BLOCK), gf_recv=(chunks, pairs - 1, 2 * shard, 2 * FF_BLOCK),
        gf_low=(chunks, 2 * shard, 2 * FF_BLOCK), gf_home=(chunks, 2, shard, 2 * FF_BLOCK),
    )
    wide = dict(
        cond_own=(count, rows, shard), cond_buf=(count, rows, shard),
        act_rows=(count * rows, shard),
        mod_rows=(count * rows, columns), mod_part=(count, rows, columns),
        mod_recv=(count, rows, columns), mod_all=(4, rows, columns),
        modv=(6, rows, 1, width), dvec=(6, rows, 1, width),
        normed_a=tokens, inverse_a=(rows, seq, 1),
        resid=tokens, normed_f=tokens, inverse_f=(rows, seq, 1), d_resid=tokens,
        probs=(rows, heads, seq, seq), grad_x_own=mine,
        e_kept=half, f_kept=half,
        ga_sum=(heads + 1, 2 * shard, local), gf_sum=(chunks, 2 * shard, 2 * FF_BLOCK),
        dm_part=(4, rows, columns), dm_recv=(4, rows, columns), dm_own=(rows, columns),
        dm_all=(count, rows, columns), dm_rows=(count * rows, columns),
        act_part=(count, rows, shard), terms=(count, rows, shard),
        gathered=(4, count, rows, shard),
    )
    sems = dict(
        s_cond=(2, count - 1), s_mod=(2, count), s_modall=(2, 3), s_xswap=(2, 1),
        s_cswap=(2, 1), s_x=(2, 3), s_cot=(2, 3),
        s_acol=(heads + 1, 2, 2), s_fcol=(chunks, 2, 2),
        s_aplane=(heads + 1, 2, pairs - 1), s_fplane=(chunks, 2, pairs - 1),
        s_a=(2, 3), s_b=(2, 3), s_e=(2, 2 * rows), s_f=(2, 2 * rows),
        s_ared=(heads + 1, 2, pairs - 1), s_fred=(chunks, 2, pairs - 1),
        s_ahome=(heads + 1, 2, 2), s_fhome=(chunks, 2, 2),
        s_dm=(2, 3), s_dmall=(2, count), s_act=(2, count - 1), s_gat=(2, 3),
        s_lswap=(2, 1), s_gswap=(2, rows),
    )
    scratch = {name: pltpu.VMEM(size, bf16) for name, size in low.items()}
    scratch.update({name: pltpu.VMEM(size, f32) for name, size in wide.items()})
    scratch.update({name: pltpu.SemaphoreType.DMA(size) for name, size in sems.items()})
    names = tuple(inputs) + tuple(outs) + tuple(scratch)
    results = pl.pallas_call(
        functools.partial(block_kernel, names),
        out_shape=tuple(outs.values()),
        in_specs=[VMEM] * len(inputs),
        out_specs=tuple(VMEM for _ in outs),
        scratch_shapes=list(scratch.values()),
        compiler_params=pltpu.CompilerParams(
            collective_id=7, has_side_effects=True, vmem_limit_bytes=60 * 2**20
        ),
    )(*inputs.values())
    results = hand_over(results)
    return results[:7] + (results[7].T,)


def can_pair(mesh):
    count, group = mesh.shape["dp"], mesh.shape["tensor"]
    return group == 4 and count % 2 == 0


def body(mesh):
    def run(*args):
        fits = (
            can_pair(mesh)
            and args[2].shape[0] % 16 == 0
            and args[0].shape[1] % 16 == 0
            and args[6].shape[0] % FF_BLOCK == 0
        )
        return (fast_shards if fits else shards)(*args)

    return run


def solution(mesh):
    return jax.shard_map(
        body(mesh),
        mesh=mesh,
        in_specs=(
            P("dp", "tensor", None),
            P("dp", None),
            P("dp", "tensor"),
            P(None, "dp", "tensor"),
            P("tensor", "dp"),
            P("dp", "tensor"),
            P("tensor", "dp"),
            P("dp", "tensor", None),
        ),
        out_specs=(
            P("dp", "tensor", None),
            P("dp", "tensor", None),
            P("dp", None),
            P("dp", "tensor"),
            P(None, "dp", "tensor"),
            P("tensor", "dp"),
            P("dp", "tensor"),
            P("tensor", "dp"),
        ),
        check_vma=False,
    )
```
